128 devices in a mesh: blk: 16 (over x_lo, y, core), grp: 8 (over z, x_hi).
Axes of the slice: x: 4 (x_hi: 2, x_lo: 2; x = x_hi * 2 + x_lo), y: 4, z: 4, core: 2. Of those that a mesh axis runs over, the one named last changes fastest.
Arguments:
- inverse: bfloat16 [2, 16, 1024, 1024], P(None, 'blk', 'grp'), may hold values from -0.0034375 to 0.1734375
- excite: bfloat16 [2, 16, 1024, 128], P(None, 'blk'), may hold values from -0.125 to 0.125
- coordinates: int32 [3, 16, 1024], replicated, may hold values from 0 to 31, as said below
- block_of_slot: int32 [16], replicated, may hold values from 0 to 15, each once
- panel_order: int32 [16], replicated, may hold values from 0 to 15, each once
Outputs:
- reduced: float32 [2, 2048, 2048], P(None, 'blk', 'grp')
- schur: float32 [2, 2048, 2048], P(None, 'blk', 'grp')
The draws below stay inside these ranges and needn't reach their ends.
Inputs may be any that keep to these rules, and one draw needn't show every extreme that they name: `coordinates`: components 0 and 1 lie in 0 to 31, component 2 in 0 to 31. No two unknowns of any blocks share a lattice point. `block_of_slot`: slot s is the (s mod 1)-th block of index s // 1 of blk; every block number appears once. `panel_order`: every block number appears once; the first 2 are eliminated in that order, without pivoting.
All inputs are finite; a program needn't handle non-finite values.
Results may differ from the reference program's by a relative error of at most 0.0055.
Values may be sent and summed in bfloat16 or wider, within the bound.
No kernel may reach another device: no remote copies, remote signals or barrier semaphores. Data moves between devices by JAX's collectives and lax.ppermute only.
A program may use at most 64 MiB of HBM per device.

```python
import math
import jax
import jax.numpy as jnp
from jax import lax

UNK = 1024
NCBF = 128
PANELS = 2
BLOCKS = 16
ORDER = 2048


def patch_shape():
    log_size = UNK.bit_length() - 1
    patch_width = 2 ** ((log_size + 1) // 2)
    return (patch_width, UNK // patch_width)


def draw_coordinates(key, part):
    base = jax.random.fold_in(key, 17)
    pick_key, order_key, flip_key = jax.random.split(base, 3)
    patch_width, patch_height = patch_shape()
    per_layer = 1024 // UNK
    across = 32 // patch_width
    positions = jnp.arange(BLOCKS, dtype=jnp.int32)
    choose = jax.random.randint(pick_key, (BLOCKS,), 0, 2).astype(jnp.int32)
    choose = jnp.where(positions == 0, 0, jnp.where(positions == BLOCKS - 1, 1, choose))
    slot_ids = 2 * positions + choose
    shuffle = jax.random.permutation(order_key, BLOCKS).astype(jnp.int32)
    placed = jnp.take(slot_ids, shuffle)
    layer_of = placed // per_layer
    patch_of = placed % per_layer
    start_x = patch_of % across * patch_width
    start_y = patch_of // across * patch_height
    mirror = jax.random.randint(flip_key, (2, BLOCKS, 1), 0, 2).astype(jnp.int32)
    unknown = jnp.arange(UNK, dtype=jnp.int32)
    inner_x = (unknown % patch_width)[None, :]
    inner_y = (unknown // patch_width)[None, :]
    first = start_x[:, None] + jnp.where(mirror[0] == 1, patch_width - 1 - inner_x, inner_x)
    second = start_y[:, None] + jnp.where(mirror[1] == 1, patch_height - 1 - inner_y, inner_y)
    third = jnp.broadcast_to(layer_of[:, None], (BLOCKS, UNK))
    return jnp.stack([first, second, third]).astype(jnp.int32)


def draw_excite(key, part):
    base = jax.random.fold_in(key, 29)
    keys = jax.random.split(base, 5)
    patch_width, patch_height = patch_shape()
    columns = (BLOCKS, 1, NCBF)
    radius = 0.7 * jnp.sqrt(jax.random.uniform(keys[0], columns, jnp.float32))
    heading = jax.random.uniform(keys[1], columns, jnp.float32, -math.pi, math.pi)
    offset = jax.random.uniform(keys[2], columns, jnp.float32, -math.pi, math.pi)
    level = jnp.exp(jax.random.uniform(keys[3], columns, jnp.float32, math.log(0.04), math.log(0.08)))
    rough = 1.0 + 0.5 * jax.random.uniform(keys[4], (BLOCKS, UNK, NCBF), jnp.float32, -1.0, 1.0)
    unknown = jnp.arange(UNK, dtype=jnp.int32)
    inner_x = (unknown % patch_width).astype(jnp.float32)[None, :, None]
    inner_y = (unknown // patch_width).astype(jnp.float32)[None, :, None]
    angle = radius * (jnp.cos(heading) * inner_x + jnp.sin(heading) * inner_y) + offset
    amplitude = level * rough
    return jnp.stack([amplitude * jnp.cos(angle), amplitude * jnp.sin(angle)]).astype(jnp.bfloat16)


def draw_inverse(key, part):
    base = jax.random.fold_in(key, 41)
    diag_key, noise_key = jax.random.split(base, 2)
    spread = 0.025 / math.sqrt(UNK)
    diagonal = jnp.exp(jax.random.uniform(diag_key, (BLOCKS, UNK, 1), jnp.float32, math.log(0.07), math.log(0.14)))
    noise = spread * jnp.clip(jax.random.normal(noise_key, (2, BLOCKS, UNK, UNK), jnp.float32), -4.0, 4.0)
    unknown = jnp.arange(UNK, dtype=jnp.int32)
    identity_mask = (unknown[:, None] == unknown[None, :]).astype(jnp.float32)
    real_part = diagonal * identity_mask[None] + noise[0]
    return jnp.stack([real_part, noise[1]]).astype(jnp.bfloat16)


def setup_inputs(seed: int = 0) -> dict:
    arg_keys = jax.random.split(jax.random.key(seed), 6)
    inverse = draw_inverse(jax.random.fold_in(arg_keys[5], 71), 0)
    excite = draw_excite(jax.random.fold_in(arg_keys[5], 71), 0)
    coordinates = draw_coordinates(jax.random.fold_in(arg_keys[5], 71), 0)
    block_of_slot = jax.random.permutation(arg_keys[3], BLOCKS).astype(jnp.int32)
    panel_order = jax.random.permutation(arg_keys[4], BLOCKS).astype(jnp.int32)
    return dict(inverse=inverse, excite=excite, coordinates=coordinates, block_of_slot=block_of_slot, panel_order=panel_order)


SELF_REAL = 12.0
SELF_IMAG = -3.0
COUPLE = 2.0
WAVE = 1.3

def green_tile(test_pos, basis_pos):
    squared = jnp.zeros((test_pos.shape[1], basis_pos.shape[1]), jnp.int32)
    for which in range(3):
        spacing = test_pos[which][:, None] - basis_pos[which][None, :]
        squared = squared + spacing * spacing
    coincide = squared == 0
    distance = jnp.sqrt(jnp.maximum(squared, 1).astype(jnp.float32))
    scaled = COUPLE / distance
    angle_term = WAVE * distance
    real_part = jnp.where(coincide, jnp.float32(SELF_REAL), scaled * jnp.cos(angle_term))
    imag_part = jnp.where(coincide, jnp.float32(SELF_IMAG), -scaled * jnp.sin(angle_term))
    return (real_part.astype(jnp.bfloat16), imag_part.astype(jnp.bfloat16))

def solve_pivot(pivot, right):
    top = jnp.concatenate([pivot[0], -pivot[1]], axis=1)
    lower = jnp.concatenate([pivot[1], pivot[0]], axis=1)
    real_form = jnp.concatenate([top, lower], axis=0)
    stacked = jnp.concatenate([right[0], right[1]], axis=0)
    answer = jnp.linalg.solve(real_form, stacked)
    return (answer[:NCBF], answer[NCBF:])

def reference(inverse, excite, coordinates, block_of_slot, panel_order):
    upper_bound = lax.Precision.HIGHEST
    inv_wide = inverse.astype(jnp.float32)
    exc_wide = excite.astype(jnp.float32)
    basis_real = jnp.einsum('sur,src->suc', inv_wide[0], exc_wide[0], precision=upper_bound) - jnp.einsum('sur,src->suc', inv_wide[1], exc_wide[1], precision=upper_bound)
    basis_imag = jnp.einsum('sur,src->suc', inv_wide[0], exc_wide[1], precision=upper_bound) + jnp.einsum('sur,src->suc', inv_wide[1], exc_wide[0], precision=upper_bound)
    basis = jnp.stack([basis_real, basis_imag]).astype(jnp.bfloat16)
    slot_of_block = jnp.argsort(block_of_slot).astype(jnp.int32)
    grouped_per_block = basis[:, slot_of_block].astype(jnp.float32)
    all_pos = coordinates.reshape(3, BLOCKS * UNK)

    def one_row(block_a):
        test_pos = coordinates[:, block_a]
        greens_function_real, greens_function_imaginary = green_tile(test_pos, all_pos)
        greens_function_real = greens_function_real.astype(jnp.float32).reshape(UNK, BLOCKS, UNK)
        greens_function_imaginary = greens_function_imaginary.astype(jnp.float32).reshape(UNK, BLOCKS, UNK)
        product_real = jnp.einsum('kpn,pnj->pkj', greens_function_real, grouped_per_block[0], precision=upper_bound) - jnp.einsum('kpn,pnj->pkj', greens_function_imaginary, grouped_per_block[1], precision=upper_bound)
        product_imaginary = jnp.einsum('kpn,pnj->pkj', greens_function_real, grouped_per_block[1], precision=upper_bound) + jnp.einsum('kpn,pnj->pkj', greens_function_imaginary, grouped_per_block[0], precision=upper_bound)
        test_real = grouped_per_block[0, block_a]
        test_imag = grouped_per_block[1, block_a]
        row_real = jnp.einsum('mk,bmc->kbc', test_real, product_real, precision=upper_bound) + jnp.einsum('mk,bmc->kbc', test_imag, product_imaginary, precision=upper_bound)
        row_imag = jnp.einsum('mk,bmc->kbc', test_real, product_imaginary, precision=upper_bound) - jnp.einsum('mk,bmc->kbc', test_imag, product_real, precision=upper_bound)
        return jnp.stack([row_real, row_imag]).reshape(2, NCBF, ORDER)
    rows = lax.map(one_row, jnp.arange(BLOCKS, dtype=jnp.int32))
    system_matrix = jnp.transpose(rows, (1, 0, 2, 3)).reshape(2, ORDER, ORDER)

    def slot_rows(full):
        return full.reshape(2, BLOCKS, NCBF, ORDER)[:, block_of_slot].reshape(2, ORDER, ORDER)
    reduced = slot_rows(system_matrix)
    for step in range(PANELS):
        start = (panel_order[step] * NCBF).astype(jnp.int32)
        upper = lax.dynamic_slice_in_dim(system_matrix, start, NCBF, 1)
        column = lax.dynamic_slice_in_dim(system_matrix, start, NCBF, 2)
        pivot = lax.dynamic_slice_in_dim(upper, start, NCBF, 2)
        sol_real, sol_imag = solve_pivot(pivot, upper)
        upd_real = jnp.dot(column[0], sol_real, precision=upper_bound) - jnp.dot(column[1], sol_imag, precision=upper_bound)
        upd_imag = jnp.dot(column[0], sol_imag, precision=upper_bound) + jnp.dot(column[1], sol_real, precision=upper_bound)
        system_matrix = system_matrix - jnp.stack([upd_real, upd_imag])
    return (reduced, slot_rows(system_matrix))
```

```python
import functools

import jax
import jax.numpy as jnp
import numpy as np
from jax import lax
from jax.experimental import pallas as pl
from jax.experimental.pallas import tpu as pltpu
from jax.sharding import PartitionSpec as P

PANELS = 2
bf16 = jnp.bfloat16
f32 = jnp.float32
i32 = jnp.int32

SELF_REAL = 6.0
SELF_IMAG = -1.5
TURNS = 1.3 / (2 * np.pi)
SHIFT = float(1.5 * 2**23)
SIN = (4.44288283, -7.30824115, 3.60628896, -0.8457636, 0.10920575)
COS = (-1.4142135, 6.97885099, -5.73946117, 1.88356298, -0.31069819)
VMEM = pl.BlockSpec(memory_space=pltpu.VMEM)
SMEM = pl.BlockSpec(memory_space=pltpu.SMEM)
MB = 1 << 20


def horner(coefs, g):
    r = coefs[-1]
    for k in coefs[-2::-1]:
        r = r * g + k
    return r


def half_green(sq):
    inv_r = lax.rsqrt(sq)
    turns = (sq * inv_r) * TURNS
    f = turns - ((turns + SHIFT) - SHIFT)
    g = f * f
    s = horner(SIN, g) * f
    c = horner(COS, g)
    return inv_r - (s * s) * inv_r, (s * c) * inv_r


def basis_kernel(core_ref, inv_ref, exc_ref, own_ref, keep_ref, send_ref):
    er, ei = exc_ref[0, 0], exc_ref[1, 0]
    j = jnp.dot(inv_ref[0, 0], jnp.concatenate([er, ei], 1), preferred_element_type=f32)
    j += jnp.dot(inv_ref[1, 0], jnp.concatenate([-ei, er], 1), preferred_element_type=f32)
    rows, cols = j.shape[0], j.shape[1] // 2
    half = rows // 2
    jb = j.astype(bf16)
    for g in range(own_ref.shape[0]):
        own_ref[g, 0] = jb[:, :cols]
        own_ref[g, 1] = jb[:, cols:]
    mine = pl.multiple_of(core_ref[0] * half, half)
    other = pl.multiple_of((1 - core_ref[0]) * half, half)
    for part in range(2):
        keep_ref[part] = own_ref[0, part, pl.ds(mine, half), :]
        send_ref[part] = own_ref[0, part, pl.ds(other, half), :]


def basis_rows(core, inverse, excite, copies):
    rows, cols = inverse.shape[2], excite.shape[3]
    half = jax.ShapeDtypeStruct((2, rows // 2, cols), bf16)
    return pl.pallas_call(
        basis_kernel,
        out_shape=(jax.ShapeDtypeStruct((copies, 2, rows, cols), bf16), half, half),
        in_specs=[SMEM, VMEM, VMEM],
        out_specs=(VMEM, VMEM, VMEM),
        name="basis",
    )(core, inverse, excite)


def green_kernel(left_ids, right_ids, fl_ref, fr_ref, g_ref, sq_ref):
    rows, cols = sq_ref.shape
    sq_ref[...] = lax.dot_general(
        fl_ref[0], fr_ref[0], (((0,), (0,)), ((), ())), preferred_element_type=f32
    )

    def strip(i, _):
        r = pl.ds(pl.multiple_of(i * 8, 8), 8)
        re, im = half_green(sq_ref[r, :])
        g_ref[0, 0, r, :] = re.astype(bf16)
        g_ref[0, 1, r, :] = im.astype(bf16)
        return 0

    lax.fori_loop(0, rows // 8, strip, 0, unroll=4)
    tile, chunk = pl.program_id(0), pl.program_id(1)

    @pl.when(left_ids[tile] == right_ids[tile])
    def _():
        at = pl.ds(pl.multiple_of(chunk * rows, rows), rows)
        same = lax.broadcasted_iota(i32, (rows, rows), 0) == lax.broadcasted_iota(i32, (rows, rows), 1)
        for part, value in ((0, SELF_REAL), (1, SELF_IMAG)):
            block = g_ref[0, part, :, at].astype(f32)
            g_ref[0, part, :, at] = jnp.where(same, value, block).astype(bf16)


def green_tiles(left_ids, right_ids, feat_left, feat_right, name):
    tiles, unk = left_ids.shape[0], feat_left.shape[2]
    rows = 256
    depth = feat_left.shape[1]
    return pl.pallas_call(
        green_kernel,
        out_shape=jax.ShapeDtypeStruct((tiles, 2, unk, unk), bf16),
        grid_spec=pltpu.PrefetchScalarGridSpec(
            num_scalar_prefetch=2,
            grid=(tiles, unk // rows),
            in_specs=[
                pl.BlockSpec((1, depth, rows), lambda t, m, le, ri: (le[t], 0, m)),
                pl.BlockSpec((1, depth, unk), lambda t, m, le, ri: (ri[t], 0, 0)),
            ],
            out_specs=pl.BlockSpec((1, 2, rows, unk), lambda t, m, le, ri: (t, 0, m, 0)),
            scratch_shapes=[pltpu.VMEM((rows, unk), f32)],
        ),
        compiler_params=pltpu.CompilerParams(vmem_limit_bytes=16 * MB),
        cost_estimate=pl.CostEstimate(
            flops=tiles * unk * unk * 30, transcendentals=tiles * unk * unk, bytes_accessed=tiles * unk * unk * 4
        ),
        name=name,
    )(left_ids, right_ids, feat_left, feat_right)


def features(coordinates):
    pos = coordinates.astype(i32)
    norm = jnp.sum(pos * pos, axis=0)
    low = norm % 64
    high = norm - low
    one, zero = jnp.ones_like(norm), jnp.zeros_like(norm)
    x, y, z = pos[0], pos[1], pos[2]
    pad = [zero] * 9
    left = jnp.stack([-2 * x, -2 * y, -2 * z, high, low, one, one] + pad, axis=1)
    right = jnp.stack([x, y, z, one, one, high, low] + pad, axis=1)
    return left.astype(bf16), right.astype(bf16)


def coupling_kernel(first, left_at, core_ref, g_ref, *refs):
    if left_at is None:
        own_ref, mine_ref, other_ref, out_ref, copies_ref, lhs, top, bottom, acc = refs
    else:
        mine_ref, other_ref, out_ref, lhs, top, bottom, acc = refs
    tile, chunk = pl.program_id(0), pl.program_id(1)
    chunks = pl.num_programs(1)
    core = core_ref[0]
    groups, _, _, half, cols = mine_ref.shape
    rows = g_ref.shape[2]

    def rows_of(g, part):
        return pl.ds(pl.multiple_of(g * 2 * half + part * half, half), half)

    @pl.when((tile == 0) & (chunk == 0))
    def _():
        if left_at is None:
            for g in range(groups):
                r = pl.ds(g * 2 * half, 2 * half)
                lhs[r, :cols] = own_ref[g, 0]
                lhs[r, cols:] = own_ref[g, 1]
        else:
            for g in range(groups):
                for src, part in ((mine_ref, core), (other_ref, 1 - core)):
                    r = rows_of(g, part)
                    lhs[r, :cols] = src[g, left_at + core, 0]
                    lhs[r, cols:] = src[g, left_at + core, 1]

    @pl.when(chunk == 0)
    def _():
        acc[...] = jnp.zeros_like(acc)
        for g in range(groups):
            for src, part in ((mine_ref, core), (other_ref, 1 - core)):
                r = rows_of(g, part)
                jr, ji = src[g, first + tile, 0], src[g, first + tile, 1]
                top[r, :cols] = jr
                top[r, cols:] = ji
                bottom[r, :cols] = -ji
                bottom[r, cols:] = jr

    y = jnp.dot(g_ref[0, 0], top[...], preferred_element_type=f32)
    y += jnp.dot(g_ref[0, 1], bottom[...], preferred_element_type=f32)
    y_hi = y.astype(bf16)
    y_lo = (y - y_hi.astype(f32)).astype(bf16)
    left = lhs[pl.ds(pl.multiple_of(chunk * rows, rows), rows), :]
    over_rows = (((0,), (0,)), ((), ()))
    acc[...] += lax.dot_general(left, y_hi, over_rows, preferred_element_type=f32) + lax.dot_general(
        left, y_lo, over_rows, preferred_element_type=f32
    )

    @pl.when(chunk == chunks - 1)
    def _():
        re = 2.0 * (acc[:cols, :cols] + acc[cols:, cols:])
        im = 2.0 * (acc[:cols, cols:] - acc[cols:, :cols])
        out_ref[0] = re
        out_ref[1] = im
        if left_at is None:
            for k in range(copies_ref.shape[0]):
                copies_ref[k, 0] = re.astype(bf16)
                copies_ref[k, 1] = im.astype(bf16)


def couplings(core, green, own, mine, other, first, left_at, name):
    tiles, _, unk, _ = green.shape
    cols = mine.shape[4]
    rows = 256
    copies = 8
    whole = lambda x: pl.BlockSpec(x.shape, lambda t, m: (0,) * x.ndim)
    args = ([own] if left_at is None else []) + [mine, other]
    out_shape = [jax.ShapeDtypeStruct((2, cols, tiles * cols), f32)]
    out_specs = [pl.BlockSpec((2, cols, cols), lambda t, m: (0, 0, t))]
    if left_at is None:
        out_shape.append(jax.ShapeDtypeStruct((copies, 2, cols, tiles * cols), bf16))
        out_specs.append(pl.BlockSpec((copies, 2, cols, cols), lambda t, m: (0, 0, 0, t)))
    return pl.pallas_call(
        functools.partial(coupling_kernel, first, left_at),
        out_shape=out_shape,
        grid=(tiles, unk // rows),
        in_specs=[SMEM, pl.BlockSpec((1, 2, rows, unk), lambda t, m: (t, 0, m, 0))] + [whole(x) for x in args],
        out_specs=out_specs,
        scratch_shapes=[
            pltpu.VMEM((unk, 2 * cols), bf16),
            pltpu.VMEM((unk, 2 * cols), bf16),
            pltpu.VMEM((unk, 2 * cols), bf16),
            pltpu.VMEM((2 * cols, 2 * cols), f32),
        ],
        compiler_params=pltpu.CompilerParams(vmem_limit_bytes=24 * MB),
        cost_estimate=pl.CostEstimate(
            flops=tiles * unk * unk * 2048, transcendentals=0, bytes_accessed=tiles * unk * unk * 4
        ),
        name=name,
    )(core, green, *args)


SIZE = 64


def turned(x):
    lane = lax.broadcasted_iota(i32, x.shape, x.ndim - 1)
    rolled = pltpu.roll(x, SIZE, x.ndim - 1)
    return jnp.where(lane < SIZE, -rolled, rolled)


def small_inverse(block):
    tiles = [block[8 * t : 8 * t + 8] for t in range(SIZE // 8)]
    lane = lax.broadcasted_iota(i32, (8, 2 * SIZE), 1)
    sub = lax.broadcasted_iota(i32, (8, 2 * SIZE), 0)
    lane1 = lax.broadcasted_iota(i32, (1, 2 * SIZE), 1)
    for k in range(SIZE):
        t, s = divmod(k, 8)
        cr = [jnp.broadcast_to(x[:, k : k + 1], x.shape) for x in tiles]
        ci = [jnp.broadcast_to(x[:, SIZE + k : SIZE + k + 1], x.shape) for x in tiles]
        pr, pi = cr[t][s : s + 1], ci[t][s : s + 1]
        scale = 1.0 / (pr * pr + pi * pi)
        qr, qi = pr * scale, -(pi * scale)
        row = tiles[t][s : s + 1]
        row = jnp.where(lane1 == k, 1.0, jnp.where(lane1 == SIZE + k, 0.0, row))
        row_t = turned(row)
        new = row * qr + row_t * qi
        new_t = row_t * qr - row * qi
        new = jnp.broadcast_to(new, (8, 2 * SIZE))
        new_t = jnp.broadcast_to(new_t, (8, 2 * SIZE))
        gone = (lane == k) | (lane == SIZE + k)
        tiles = [jnp.where(gone, 0.0, x) - a * new - b * new_t for x, a, b in zip(tiles, cr, ci)]
        tiles[t] = jnp.where(sub == s, new, tiles[t])
    return jnp.concatenate(tiles, 0)


def inverse_kernel(core_ref, mine_ref, other_ref, out_ref, a_ref):
    core = core_ref[0]
    rows = mine_ref.shape[1]
    blocks = a_ref.shape[0]
    for src, part in ((mine_ref, core), (other_ref, 1 - core)):
        r = pl.ds(pl.multiple_of(part * rows, rows), rows)
        for j in range(blocks):
            c = slice(j * SIZE, (j + 1) * SIZE)
            a_ref[j, r, :] = jnp.concatenate([src[0][:, c], src[1][:, c]], 1)
    high = lax.Precision.HIGHEST

    def step(kb, _):
        r = pl.ds(pl.multiple_of(kb * SIZE, SIZE), SIZE)
        inv = small_inverse(a_ref[kb, r, :])
        col = a_ref[kb]
        a_ref[kb] = jnp.zeros_like(col)
        lane = lax.broadcasted_iota(i32, (SIZE, 2 * SIZE), 1)
        row = lax.broadcasted_iota(i32, (SIZE, 2 * SIZE), 0)
        a_ref[kb, r, :] = jnp.where(lane == row, 1.0, 0.0)
        panel = jnp.concatenate([a_ref[j, r, :] for j in range(blocks)], 1)
        flip = jnp.concatenate([turned(a_ref[j, r, :]) for j in range(blocks)], 1)
        prod = jnp.dot(inv, jnp.concatenate([panel, flip], 0), precision=high, preferred_element_type=f32)
        parts = [prod[:, 2 * SIZE * j : 2 * SIZE * (j + 1)] for j in range(blocks)]
        full = jnp.concatenate([prod, jnp.concatenate([turned(x) for x in parts], 1)], 0)
        upd = jnp.dot(col, full, precision=high, preferred_element_type=f32)
        for j in range(blocks):
            a_ref[j] = a_ref[j] - upd[:, 2 * SIZE * j : 2 * SIZE * (j + 1)]
            a_ref[j, r, :] = parts[j]
        return 0

    lax.fori_loop(0, blocks, step, 0)
    for part in range(2):
        out_ref[part] = jnp.concatenate(
            [a_ref[j][:, part * SIZE : (part + 1) * SIZE] for j in range(blocks)], 1
        )


def pivot_inverse(core, mine, other):
    order = 2 * mine.shape[1]
    return pl.pallas_call(
        inverse_kernel,
        out_shape=jax.ShapeDtypeStruct((2, order, order), f32),
        in_specs=[SMEM, VMEM, VMEM],
        out_specs=VMEM,
        scratch_shapes=[pltpu.VMEM((order // SIZE, order, 2 * SIZE), f32)],
        cost_estimate=pl.CostEstimate(flops=int(12e9), transcendentals=0, bytes_accessed=1 << 20),
        name="pivot_inverse",
    )(core, mine, other)


def split3(x):
    hi = x.astype(bf16)
    rest = x - hi.astype(f32)
    mid = rest.astype(bf16)
    low = (rest - mid.astype(f32)).astype(bf16)
    return hi, mid, low


def schur_kernel(info, inv_ref, mine_ref, other_ref, c0_ref, c1_ref, r_ref, out_ref):
    core = info[0]
    funcs = mine_ref.shape[2]
    b = []
    for p in range(PANELS):
        local = info[1 + p] == core
        b.append([jnp.where(local, mine_ref[p, k].astype(f32), other_ref[p, k].astype(f32)).astype(bf16) for k in range(2)])
    br = jnp.concatenate([b[p][0] for p in range(PANELS)], 0)
    bi = jnp.concatenate([b[p][1] for p in range(PANELS)], 0)
    right = jnp.concatenate([jnp.concatenate([br, bi], 1), jnp.concatenate([-bi, br], 1)], 0)
    w = jnp.zeros((PANELS * funcs, right.shape[1]), f32)
    for x in split3(jnp.concatenate([inv_ref[0], inv_ref[1]], 1)):
        w += jnp.dot(x, right, preferred_element_type=f32)
    cols = w.shape[1] // 2
    w_hi = w.astype(bf16)
    w_lo = (w - w_hi.astype(f32)).astype(bf16)
    cr = jnp.concatenate([c0_ref[0, 0], c1_ref[0, 0]], 1)
    ci = jnp.concatenate([c0_ref[0, 1], c1_ref[0, 1]], 1)
    left = jnp.concatenate([cr, ci], 0)
    prod = jnp.dot(left, w_hi, preferred_element_type=f32) + jnp.dot(left, w_lo, preferred_element_type=f32)
    rows = cr.shape[0]
    out_ref[0] = r_ref[0] - (prod[:rows, :cols] - prod[rows:, cols:])
    out_ref[1] = r_ref[1] - (prod[:rows, cols:] + prod[rows:, :cols])


def schur_tile(info, inv, mine, other, column, reduced):
    funcs = mine.shape[2]
    whole = lambda x: pl.BlockSpec(x.shape, lambda i, s: (0,) * x.ndim)

    def at(p):
        return lambda i, s: (s[3 + p], 0, 0, s[5 + p])

    return pl.pallas_call(
        schur_kernel,
        out_shape=jax.ShapeDtypeStruct(reduced.shape, f32),
        grid_spec=pltpu.PrefetchScalarGridSpec(
            num_scalar_prefetch=1,
            grid=(1,),
            in_specs=[
                whole(inv),
                whole(mine),
                whole(other),
                pl.BlockSpec((1, 2, funcs, funcs), at(0)),
                pl.BlockSpec((1, 2, funcs, funcs), at(1)),
                whole(reduced),
            ],
            out_specs=whole(reduced),
        ),
        name="schur",
    )(info, inv, mine, other, column, column, reduced)


def on_device(inverse, excite, coordinates, block_of_slot, panel_order):
    blk_size, grp_size = lax.axis_size("blk"), lax.axis_size("grp")
    blocks = block_of_slot.shape[0]
    slot, grp = lax.axis_index("blk"), lax.axis_index("grp")
    core = slot % 2
    slabs = blocks // grp_size
    swap = [(i, i ^ 1) for i in range(blk_size)]
    same_core = [list(range(c, blk_size, 2)) for c in range(2)]
    core1 = core.reshape(1)

    def spread(x, axis, groups=None):
        return lax.all_to_all(x, axis, split_axis=0, concat_axis=0, tiled=True, axis_index_groups=groups)

    order = jnp.arange(blocks, dtype=i32)
    slot_of = jnp.sum(jnp.where(block_of_slot[None, :] == order[:, None], order[None, :], 0), axis=1)
    own_id = jnp.sum(jnp.where(order == slot, block_of_slot, 0))
    pivots = panel_order[:PANELS]
    feat_left, feat_right = features(coordinates)

    own8, keep, send = basis_rows(core1, inverse, excite, grp_size)
    own_full = spread(own8, "grp")
    got = lax.ppermute(send, "blk", swap)
    pair = jnp.broadcast_to(jnp.stack([keep, got])[None], (blk_size // 2, 2, *keep.shape))
    sliced = spread(pair, "blk", same_core)
    sliced = sliced.reshape(blk_size, *keep.shape)

    green_main = green_tiles(
        jnp.broadcast_to(own_id, (slabs,)), grp * slabs + jnp.arange(slabs, dtype=i32), feat_left, feat_right, "green_main"
    )
    pivot_mine = jnp.sum(jnp.where(jnp.arange(PANELS) == core, pivots, 0))
    green_pivot = green_tiles(jnp.broadcast_to(pivot_mine, (PANELS,)), pivots, feat_left, feat_right, "green_pivot")

    wanted = jnp.concatenate(
        [order.reshape(grp_size, slabs), jnp.broadcast_to(pivots[None], (grp_size, PANELS))], axis=1
    )
    from_slot = jnp.sum(jnp.where(wanted[:, :, None] == order, slot_of, 0), axis=2)
    place = (from_slot // 2) * 2 + (from_slot % 2 + core) % 2
    mine = spread(jnp.take(sliced, place.reshape(-1), axis=0).reshape(*place.shape, *keep.shape), "grp")
    other = lax.ppermute(mine, "blk", swap)

    reduced, copies = couplings(core1, green_main, own_full, mine, other, 0, None, "main")
    (pivot_rows,) = couplings(core1, green_pivot, None, mine, other, slabs, slabs, "pivot")

    column = spread(copies, "grp")
    rows = spread(copies, "blk", same_core)
    pivot_slot = jnp.sum(jnp.where(pivots[:, None] == order, slot_of, 0), axis=1)
    row_mine = jnp.stack([lax.dynamic_index_in_dim(rows, pivot_slot[p] // 2, 0, keepdims=False) for p in range(PANELS)])
    row_other = lax.ppermute(row_mine, "blk", swap)
    inv = pivot_inverse(core1, pivot_rows, lax.ppermute(pivot_rows, "blk", swap))
    info = jnp.concatenate([core1, pivot_slot % 2, pivots // slabs, pivots % slabs]).astype(i32)
    schur = schur_tile(info, inv, row_mine, row_other, column, reduced)
    return (reduced, schur)


def solution(mesh):
    placed = (P(None, "blk", "grp", None), P(None, "blk", None, None), P(), P(), P())
    return jax.shard_map(
        on_device,
        mesh=mesh,
        in_specs=placed,
        out_specs=(P(None, "blk", "grp"), P(None, "blk", "grp")),
        check_vma=False,
    )
```

```python
import functools

import jax
import jax.numpy as jnp
import numpy as np
from jax import lax
from jax.experimental import pallas as pl
from jax.experimental.pallas import tpu as pltpu
from jax.sharding import PartitionSpec as P


PANELS = 2
bf16 = jnp.bfloat16
f32 = jnp.float32
i32 = jnp.int32

SELF_REAL = 6.0
SELF_IMAG = -1.5
TURNS = 1.3 / (2 * np.pi)
SHIFT = float(1.5 * 2**23)
SIN = (4.44288283, -7.30824115, 3.60628896, -0.8457636, 0.10920575)
COS = (-1.4142135, 6.97885099, -5.73946117, 1.88356298, -0.31069819)
VMEM = pl.BlockSpec(memory_space=pltpu.VMEM)
SMEM = pl.BlockSpec(memory_space=pltpu.SMEM)
MB = 1 << 20


def horner(coefs, g):
    r = coefs[-1]
    for k in coefs[-2::-1]:
        r = r * g + k
    return r


def half_green(sq):
    inv_r = lax.rsqrt(sq)
    turns = (sq * inv_r) * TURNS
    f = turns - ((turns + SHIFT) - SHIFT)
    g = f * f
    s = horner(SIN, g) * f
    c = horner(COS, g)
    return inv_r - (s * s) * inv_r, (s * c) * inv_r


def basis_kernel(core_ref, inv_ref, exc_ref, keep_ref, send_ref, both):
    er, ei = exc_ref[0, 0], exc_ref[1, 0]
    j = jnp.dot(inv_ref[0, 0], jnp.concatenate([er, ei], 1), preferred_element_type=f32)
    j += jnp.dot(inv_ref[1, 0], jnp.concatenate([-ei, er], 1), preferred_element_type=f32)
    rows, cols = j.shape[0], j.shape[1] // 2
    half = rows // 2
    both[...] = j.astype(bf16)
    mine = pl.multiple_of(core_ref[0] * half, half)
    other = pl.multiple_of((1 - core_ref[0]) * half, half)
    for part in range(2):
        keep_ref[part] = both[pl.ds(mine, half), part * cols : (part + 1) * cols]
        send_ref[part] = both[pl.ds(other, half), part * cols : (part + 1) * cols]


def basis_rows(core, inverse, excite):
    rows, cols = inverse.shape[2], excite.shape[3]
    half = jax.ShapeDtypeStruct((2, rows // 2, cols), bf16)
    return pl.pallas_call(
        basis_kernel,
        out_shape=(half, half),
        in_specs=[SMEM, VMEM, VMEM],
        out_specs=(VMEM, VMEM),
        scratch_shapes=[pltpu.VMEM((rows, 2 * cols), bf16)],
        compiler_params=pltpu.CompilerParams(vmem_limit_bytes=8 * MB),
        name="basis",
    )(core, inverse, excite)


def green_kernel(left_ids, right_ids, fl_ref, fr_ref, g_ref, sq_ref):
    rows, _ = sq_ref.shape
    sq_ref[...] = lax.dot_general(
        fl_ref[0], fr_ref[0], (((0,), (0,)), ((), ())), preferred_element_type=f32
    )

    def strip(i, _):
        r = pl.ds(pl.multiple_of(i * 8, 8), 8)
        re, im = half_green(sq_ref[r, :])
        g_ref[0, 0, r, :] = re.astype(bf16)
        g_ref[0, 1, r, :] = im.astype(bf16)
        return 0

    lax.fori_loop(0, rows // 8, strip, 0, unroll=4)
    tile, chunk = pl.program_id(0), pl.program_id(1)

    @pl.when(left_ids[tile] == right_ids[tile])
    def _():
        at = pl.ds(pl.multiple_of(chunk * rows, rows), rows)
        same = lax.broadcasted_iota(i32, (rows, rows), 0) == lax.broadcasted_iota(i32, (rows, rows), 1)
        for part, value in ((0, SELF_REAL), (1, SELF_IMAG)):
            block = g_ref[0, part, :, at].astype(f32)
            g_ref[0, part, :, at] = jnp.where(same, value, block).astype(bf16)


def green_tiles(left_ids, right_ids, feat_left, feat_right):
    tiles, unk = left_ids.shape[0], feat_left.shape[2]
    rows = 256
    depth = feat_left.shape[1]
    return pl.pallas_call(
        green_kernel,
        out_shape=pltpu.HBM((tiles, 2, unk, unk), bf16),
        grid_spec=pltpu.PrefetchScalarGridSpec(
            num_scalar_prefetch=2,
            grid=(tiles, unk // rows),
            in_specs=[
                pl.BlockSpec((1, depth, rows), lambda t, m, le, ri: (le[t], 0, m)),
                pl.BlockSpec((1, depth, unk), lambda t, m, le, ri: (ri[t], 0, 0)),
            ],
            out_specs=pl.BlockSpec((1, 2, rows, unk), lambda t, m, le, ri: (t, 0, m, 0)),
            scratch_shapes=[pltpu.VMEM((rows, unk), f32)],
        ),
        compiler_params=pltpu.CompilerParams(vmem_limit_bytes=10 * MB),
        cost_estimate=pl.CostEstimate(
            flops=tiles * unk * unk * 30, transcendentals=tiles * unk * unk, bytes_accessed=tiles * unk * unk * 4
        ),
    )(left_ids, right_ids, feat_left, feat_right)


def features(coordinates):
    pos = coordinates.astype(i32)
    norm = jnp.sum(pos * pos, axis=0)
    low = norm % 64
    high = norm - low
    one, zero = jnp.ones_like(norm), jnp.zeros_like(norm)
    x, y, z = pos[0], pos[1], pos[2]
    pad = [zero] * 9
    left = jnp.stack([-2 * x, -2 * y, -2 * z, high, low, one, one] + pad, axis=1)
    right = jnp.stack([x, y, z, one, one, high, low] + pad, axis=1)
    return left.astype(bf16), right.astype(bf16)


def coupling_kernel(first, left_at, core_ref, g_ref, *refs):
    if left_at is None:
        mine_ref, other_ref, out_ref, copies_ref, lhs, top, bottom, acc = refs
    else:
        mine_ref, other_ref, out_ref, lhs, top, bottom, acc = refs
    tile, chunk = pl.program_id(0), pl.program_id(1)
    chunks = pl.num_programs(1)
    core = core_ref[0]
    groups, _, _, half, cols = mine_ref.shape
    rows = g_ref.shape[2]

    def rows_of(g, part):
        return pl.ds(pl.multiple_of(g * 2 * half + part * half, half), half)

    @pl.when((tile == 0) & (chunk == 0))
    def _():
        for g in range(groups):
            for src, part, entry in ((mine_ref, core, 0), (other_ref, 1 - core, 1)):
                at = left_at + core if left_at is not None else mine_ref.shape[1] - 2 + entry
                r = rows_of(g, part)
                lhs[r, :cols] = src[g, at, 0]
                lhs[r, cols:] = src[g, at, 1]

    @pl.when(chunk == 0)
    def _():
        acc[...] = jnp.zeros_like(acc)
        for g in range(groups):
            for src, part in ((mine_ref, core), (other_ref, 1 - core)):
                r = rows_of(g, part)
                jr, ji = src[g, first + tile, 0], src[g, first + tile, 1]
                top[r, :cols] = jr
                top[r, cols:] = ji
                bottom[r, :cols] = -ji
                bottom[r, cols:] = jr

    y = jnp.dot(g_ref[0, 0], top[...], preferred_element_type=f32)
    y += jnp.dot(g_ref[0, 1], bottom[...], preferred_element_type=f32)
    y_hi = y.astype(bf16)
    y_lo = (y - y_hi.astype(f32)).astype(bf16)
    left = lhs[pl.ds(pl.multiple_of(chunk * rows, rows), rows), :]
    over_rows = (((0,), (0,)), ((), ()))
    acc[...] += lax.dot_general(left, y_hi, over_rows, preferred_element_type=f32) + lax.dot_general(
        left, y_lo, over_rows, preferred_element_type=f32
    )

    @pl.when(chunk == chunks - 1)
    def _():
        re = 2.0 * (acc[:cols, :cols] + acc[cols:, cols:])
        im = 2.0 * (acc[:cols, cols:] - acc[cols:, :cols])
        out_ref[0] = re
        out_ref[1] = im
        if left_at is None:
            for k in range(copies_ref.shape[0]):
                copies_ref[k, 0] = re.astype(bf16)
                copies_ref[k, 1] = im.astype(bf16)


def couplings(core, green, mine, other, first, left_at):
    tiles, _, unk, _ = green.shape
    cols = mine.shape[4]
    rows = 256
    copies = 8
    whole = lambda x: pl.BlockSpec(x.shape, lambda t, m: (0,) * x.ndim)
    args = [mine, other]
    out_shape = [jax.ShapeDtypeStruct((2, cols, tiles * cols), f32)]
    out_specs = [pl.BlockSpec((2, cols, cols), lambda t, m: (0, 0, t))]
    if left_at is None:
        out_shape.append(jax.ShapeDtypeStruct((copies, 2, cols, tiles * cols), bf16))
        out_specs.append(pl.BlockSpec((copies, 2, cols, cols), lambda t, m: (0, 0, 0, t)))
    return pl.pallas_call(
        functools.partial(coupling_kernel, first, left_at),
        out_shape=out_shape,
        grid=(tiles, unk // rows),
        in_specs=[SMEM, pl.BlockSpec((1, 2, rows, unk), lambda t, m: (t, 0, m, 0))] + [whole(x) for x in args],
        out_specs=out_specs,
        scratch_shapes=[
            pltpu.VMEM((unk, 2 * cols), bf16),
            pltpu.VMEM((unk, 2 * cols), bf16),
            pltpu.VMEM((unk, 2 * cols), bf16),
            pltpu.VMEM((2 * cols, 2 * cols), f32),
        ],
        compiler_params=pltpu.CompilerParams(vmem_limit_bytes=12 * MB),
        cost_estimate=pl.CostEstimate(
            flops=tiles * unk * unk * 2048, transcendentals=0, bytes_accessed=tiles * unk * unk * 4
        ),
    )(core, pltpu.with_memory_space_constraint(green, pltpu.HBM), *args)


SIZE = 64


def turned(x):
    lane = lax.broadcasted_iota(i32, x.shape, x.ndim - 1)
    rolled = pltpu.roll(x, SIZE, x.ndim - 1)
    return jnp.where(lane < SIZE, -rolled, rolled)


def small_inverse(block):
    tiles = [block[8 * t : 8 * t + 8] for t in range(SIZE // 8)]
    lane = lax.broadcasted_iota(i32, (8, 2 * SIZE), 1)
    sub = lax.broadcasted_iota(i32, (8, 2 * SIZE), 0)
    lane1 = lax.broadcasted_iota(i32, (1, 2 * SIZE), 1)
    for k in range(SIZE):
        t, s = divmod(k, 8)
        cr = [jnp.broadcast_to(x[:, k : k + 1], x.shape) for x in tiles]
        ci = [jnp.broadcast_to(x[:, SIZE + k : SIZE + k + 1], x.shape) for x in tiles]
        pr, pi = cr[t][s : s + 1], ci[t][s : s + 1]
        scale = 1.0 / (pr * pr + pi * pi)
        qr, qi = pr * scale, -(pi * scale)
        row = tiles[t][s : s + 1]
        row = jnp.where(lane1 == k, 1.0, jnp.where(lane1 == SIZE + k, 0.0, row))
        row_t = turned(row)
        new = row * qr + row_t * qi
        new_t = row_t * qr - row * qi
        new = jnp.broadcast_to(new, (8, 2 * SIZE))
        new_t = jnp.broadcast_to(new_t, (8, 2 * SIZE))
        gone = (lane == k) | (lane == SIZE + k)
        tiles = [jnp.where(gone, 0.0, x) - a * new - b * new_t for x, a, b in zip(tiles, cr, ci)]
        tiles[t] = jnp.where(sub == s, new, tiles[t])
    return jnp.concatenate(tiles, 0)


def inverse_kernel(core_ref, mine_ref, other_ref, out_ref, a_ref):
    core = core_ref[0]
    rows = mine_ref.shape[1]
    blocks = a_ref.shape[0]
    for src, part in ((mine_ref, core), (other_ref, 1 - core)):
        r = pl.ds(pl.multiple_of(part * rows, rows), rows)
        for j in range(blocks):
            c = slice(j * SIZE, (j + 1) * SIZE)
            a_ref[j, r, :] = jnp.concatenate([src[0][:, c], src[1][:, c]], 1)
    high = lax.Precision.HIGHEST

    def step(kb, _):
        r = pl.ds(pl.multiple_of(kb * SIZE, SIZE), SIZE)
        inv = small_inverse(a_ref[kb, r, :])
        col = a_ref[kb]
        a_ref[kb] = jnp.zeros_like(col)
        lane = lax.broadcasted_iota(i32, (SIZE, 2 * SIZE), 1)
        row = lax.broadcasted_iota(i32, (SIZE, 2 * SIZE), 0)
        a_ref[kb, r, :] = jnp.where(lane == row, 1.0, 0.0)
        panel = jnp.concatenate([a_ref[j, r, :] for j in range(blocks)], 1)
        flip = jnp.concatenate([turned(a_ref[j, r, :]) for j in range(blocks)], 1)
        prod = jnp.dot(inv, jnp.concatenate([panel, flip], 0), precision=high, preferred_element_type=f32)
        parts = [prod[:, 2 * SIZE * j : 2 * SIZE * (j + 1)] for j in range(blocks)]
        full = jnp.concatenate([prod, jnp.concatenate([turned(x) for x in parts], 1)], 0)
        upd = jnp.dot(col, full, precision=high, preferred_element_type=f32)
        for j in range(blocks):
            a_ref[j] = a_ref[j] - upd[:, 2 * SIZE * j : 2 * SIZE * (j + 1)]
            a_ref[j, r, :] = parts[j]
        return 0

    lax.fori_loop(0, blocks, step, 0)
    for part in range(2):
        out_ref[part] = jnp.concatenate(
            [a_ref[j][:, part * SIZE : (part + 1) * SIZE] for j in range(blocks)], 1
        )


def pivot_inverse(core, mine, other):
    order = 2 * mine.shape[1]
    return pl.pallas_call(
        inverse_kernel,
        out_shape=jax.ShapeDtypeStruct((2, order, order), f32),
        in_specs=[SMEM, VMEM, VMEM],
        out_specs=VMEM,
        scratch_shapes=[pltpu.VMEM((order // SIZE, order, 2 * SIZE), f32)],
        compiler_params=pltpu.CompilerParams(vmem_limit_bytes=12 * MB),
        cost_estimate=pl.CostEstimate(flops=int(12e9), transcendentals=0, bytes_accessed=1 << 20),
        name="pivot_inverse",
    )(core, mine, other)


def split3(x):
    hi = x.astype(bf16)
    rest = x - hi.astype(f32)
    mid = rest.astype(bf16)
    low = (rest - mid.astype(f32)).astype(bf16)
    return hi, mid, low


def schur_kernel(info, inv_ref, mine_ref, other_ref, c_ref, r_ref, out_ref):
    core = info[0]
    funcs = mine_ref.shape[2]
    b = []
    for p in range(PANELS):
        local = info[1 + p] == core
        b.append([jnp.where(local, mine_ref[p, k].astype(f32), other_ref[p, k].astype(f32)).astype(bf16) for k in range(2)])
    br = jnp.concatenate([b[p][0] for p in range(PANELS)], 0)
    bi = jnp.concatenate([b[p][1] for p in range(PANELS)], 0)
    right = jnp.concatenate([jnp.concatenate([br, bi], 1), jnp.concatenate([-bi, br], 1)], 0)
    w = jnp.zeros((PANELS * funcs, right.shape[1]), f32)
    for x in split3(jnp.concatenate([inv_ref[0], inv_ref[1]], 1)):
        w += jnp.dot(x, right, preferred_element_type=f32)
    cols = w.shape[1] // 2
    w_hi = w.astype(bf16)
    w_lo = (w - w_hi.astype(f32)).astype(bf16)
    cr = jnp.concatenate([c_ref[0, 0], c_ref[1, 0]], 1)
    ci = jnp.concatenate([c_ref[0, 1], c_ref[1, 1]], 1)
    left = jnp.concatenate([cr, ci], 0)
    prod = jnp.dot(left, w_hi, preferred_element_type=f32) + jnp.dot(left, w_lo, preferred_element_type=f32)
    rows = cr.shape[0]
    out_ref[0] = r_ref[0] - (prod[:rows, :cols] - prod[rows:, cols:])
    out_ref[1] = r_ref[1] - (prod[:rows, cols:] + prod[rows:, :cols])


def schur_tile(info, inv, mine, other, column, reduced):
    return pl.pallas_call(
        schur_kernel,
        out_shape=jax.ShapeDtypeStruct(reduced.shape, f32),
        in_specs=[SMEM] + [VMEM] * 5,
        out_specs=VMEM,
        compiler_params=pltpu.CompilerParams(vmem_limit_bytes=12 * MB),
        name="schur",
    )(info, inv, mine, other, column, reduced)


def on_device(inverse, excite, coordinates, block_of_slot, panel_order):
    blk_size, grp_size = lax.axis_size("blk"), lax.axis_size("grp")
    blocks = block_of_slot.shape[0]
    slot, grp = lax.axis_index("blk"), lax.axis_index("grp")
    core = slot % 2
    slabs = blocks // grp_size
    cols = excite.shape[3]
    swap = [(i, i ^ 1) for i in range(blk_size)]
    same_core = [list(range(c, blk_size, 2)) for c in range(2)]
    core1 = core.reshape(1)

    def spread(x, axis, groups=None):
        return lax.all_to_all(x, axis, split_axis=0, concat_axis=0, tiled=True, axis_index_groups=groups)

    order = jnp.arange(blocks, dtype=i32)
    slot_of = jnp.sum(jnp.where(block_of_slot[None, :] == order[:, None], order[None, :], 0), axis=1)
    own_id = jnp.sum(jnp.where(order == slot, block_of_slot, 0))
    pivots = panel_order[:PANELS]
    feat_left, feat_right = features(coordinates)

    keep, send = basis_rows(core1, inverse, excite)
    got = lax.ppermute(send, "blk", swap)
    pair1 = jnp.stack([keep, got])
    pair = jnp.broadcast_to(pair1[None], (blk_size // 2, *pair1.shape))
    sliced = spread(pair, "blk", same_core)
    sliced = sliced.reshape(blk_size, *keep.shape)

    green_main = green_tiles(
        jnp.broadcast_to(own_id, (slabs,)), grp * slabs + jnp.arange(slabs, dtype=i32), feat_left, feat_right
    )
    pivot_mine = jnp.sum(jnp.where(jnp.arange(PANELS) == core, pivots, 0))
    green_pivot = green_tiles(jnp.broadcast_to(pivot_mine, (PANELS,)), pivots, feat_left, feat_right)

    wanted = jnp.concatenate(
        [order.reshape(grp_size, slabs), jnp.broadcast_to(pivots[None], (grp_size, PANELS))], axis=1
    )
    from_slot = jnp.sum(jnp.where(wanted[:, :, None] == order, slot_of, 0), axis=2)
    pair_slots = jnp.stack([slot, slot + 1 - 2 * core])
    from_slot = jnp.concatenate([from_slot, jnp.broadcast_to(pair_slots[None], (grp_size, 2))], axis=1)
    place = (from_slot // 2) * 2 + (from_slot % 2 + core) % 2
    picked = sliced.at[place.reshape(-1)].get(mode="promise_in_bounds").reshape(*place.shape, *keep.shape)
    mine = spread(picked, "grp")
    other = lax.ppermute(mine, "blk", swap)

    reduced, copies = couplings(core1, green_main, mine, other, 0, None)
    (pivot_rows,) = couplings(core1, green_pivot, mine, other, slabs, slabs)

    column_at = pivots // slabs
    mine_of = jnp.stack(
        [lax.dynamic_slice_in_dim(copies[0], (pivots[p] % slabs) * cols, cols, 2) for p in range(PANELS)]
    )
    bit = 1
    while bit < grp_size:
        came = lax.ppermute(mine_of, "grp", [(g, g ^ bit) for g in range(grp_size)])
        take = ((grp ^ column_at) & bit) != 0
        mine_of = jnp.where(take[:, None, None, None], came, mine_of)
        bit *= 2
    column = mine_of
    rows = spread(copies, "blk", same_core)
    pivot_slot = jnp.sum(jnp.where(pivots[:, None] == order, slot_of, 0), axis=1)
    row_mine = jnp.stack([lax.dynamic_index_in_dim(rows, pivot_slot[p] // 2, 0, keepdims=False) for p in range(PANELS)])
    row_other = lax.ppermute(row_mine, "blk", swap)
    inv = pivot_inverse(core1, pivot_rows, lax.ppermute(pivot_rows, "blk", swap))
    info = jnp.concatenate([core1, pivot_slot % 2]).astype(i32)
    schur = schur_tile(info, inv, row_mine, row_other, column, reduced)
    return (reduced, schur)


def solution(mesh):
    placed = (P(None, "blk", "grp", None), P(None, "blk", None, None), P(), P(), P())
    return jax.shard_map(
        on_device,
        mesh=mesh,
        in_specs=placed,
        out_specs=(P(None, "blk", "grp"), P(None, "blk", "grp")),
        check_vma=False,
    )
```

```python
import functools

import jax
import jax.numpy as jnp
import numpy as np
from jax import lax
from jax.experimental import pallas as pl
from jax.experimental.pallas import tpu as pltpu
from jax.sharding import PartitionSpec as P


PANELS = 2
bf16 = jnp.bfloat16
f32 = jnp.float32
i32 = jnp.int32

SELF_REAL = 6.0
SELF_IMAG = -1.5
TURNS = 1.3 / (2 * np.pi)
SHIFT = float(1.5 * 2**23)
SIN = (4.44288283, -7.30824115, 3.60628896, -0.8457636, 0.10920575)
COS = (-1.4142135, 6.97885099, -5.73946117, 1.88356298, -0.31069819)
VMEM = pl.BlockSpec(memory_space=pltpu.VMEM)
SMEM = pl.BlockSpec(memory_space=pltpu.SMEM)
MB = 1 << 20
COUPLE_ROWS = 512
GREEN_ROWS = 512
STRIPS = 4


def horner(coefs, g):
    r = coefs[-1]
    for k in coefs[-2::-1]:
        r = r * g + k
    return r


def half_green(sq):
    inv_r = lax.rsqrt(sq)
    turns = (sq * inv_r) * TURNS
    f = turns - ((turns + SHIFT) - SHIFT)
    g = f * f
    s = horner(SIN, g) * f
    c = horner(COS, g)
    scaled = s * inv_r
    return inv_r - s * scaled, c * scaled


def basis_kernel(core_ref, inv_ref, exc_ref, own_ref, keep_ref, send_ref, both):
    er, ei = exc_ref[0, 0], exc_ref[1, 0]
    j = jnp.dot(inv_ref[0, 0], jnp.concatenate([er, ei], 1), preferred_element_type=f32)
    j += jnp.dot(inv_ref[1, 0], jnp.concatenate([-ei, er], 1), preferred_element_type=f32)
    rows, cols = j.shape[0], j.shape[1] // 2
    half = rows // 2
    both[...] = j.astype(bf16)
    mine = pl.multiple_of(core_ref[0] * half, half)
    other = pl.multiple_of((1 - core_ref[0]) * half, half)
    for part in range(2):
        own_ref[0, part] = both[:, part * cols : (part + 1) * cols]
        keep_ref[part] = both[pl.ds(mine, half), part * cols : (part + 1) * cols]
        send_ref[part] = both[pl.ds(other, half), part * cols : (part + 1) * cols]


def basis_rows(core, inverse, excite):
    rows, cols = inverse.shape[2], excite.shape[3]
    half = jax.ShapeDtypeStruct((2, rows // 2, cols), bf16)
    return pl.pallas_call(
        basis_kernel,
        out_shape=(jax.ShapeDtypeStruct((1, 2, rows, cols), bf16), half, half),
        in_specs=[SMEM, VMEM, VMEM],
        out_specs=(VMEM, VMEM, VMEM),
        scratch_shapes=[pltpu.VMEM((rows, 2 * cols), bf16)],
        compiler_params=pltpu.CompilerParams(vmem_limit_bytes=8 * MB),
        name="basis",
    )(core, inverse, excite)


def features(coords_ref, block, left):
    x, y, z = [coords_ref[d, pl.ds(block, 1), :] for d in range(3)]
    norm = x * x + y * y + z * z
    low = norm & 63
    high = norm - low
    one, zero = jnp.ones_like(norm), jnp.zeros_like(norm)
    rows = [-2 * x, -2 * y, -2 * z, high, low, one, one] if left else [x, y, z, one, one, high, low]
    return jnp.concatenate([v.astype(f32) for v in rows + [zero]], 0).astype(bf16)


def green_kernel(first, at_ref, blocks_ref, panel_ref, coords_ref, *refs):
    g_ref, fl_ref, fr_ref, sq_ref = refs[-4:]
    rows, _ = sq_ref.shape
    tile, chunk = pl.program_id(0) + first, pl.program_id(1)
    own, grp, core = blocks_ref[at_ref[0]], at_ref[1], at_ref[2]
    main = tile < 2
    left = jnp.where(main, own, panel_ref[core])
    right = jnp.where(main, grp * 2 + tile, panel_ref[jnp.maximum(tile - 2, 0)])

    @pl.when(chunk == 0)
    def _():
        fl_ref[...] = features(coords_ref, left, True)
        fr_ref[...] = features(coords_ref, right, False)

    at = pl.ds(pl.multiple_of(chunk * rows, rows), rows)
    sq_ref[...] = lax.dot_general(
        fl_ref[:, at], fr_ref[...], (((0,), (0,)), ((), ())), preferred_element_type=f32
    )

    def strip(i, _):
        r = pl.ds(pl.multiple_of(i * 8, 8), 8)
        re, im = half_green(sq_ref[r, :])
        g_ref[0, 0, r, :] = re.astype(bf16)
        g_ref[0, 1, r, :] = im.astype(bf16)
        return 0

    lax.fori_loop(0, rows // 8, strip, 0, unroll=STRIPS)

    @pl.when(left == right)
    def _():
        same = lax.broadcasted_iota(i32, (rows, rows), 0) == lax.broadcasted_iota(i32, (rows, rows), 1)
        for part, value in ((0, SELF_REAL), (1, SELF_IMAG)):
            block = g_ref[0, part, :, at].astype(f32)
            g_ref[0, part, :, at] = jnp.where(same, value, block).astype(bf16)


def green_tiles(at, blocks, panel, coordinates, first, count, tiles, held):
    unk = coordinates.shape[2]
    rows = GREEN_ROWS
    return pl.pallas_call(
        functools.partial(green_kernel, first),
        out_shape=pltpu.HBM((tiles, 2, unk, unk), bf16),
        grid=(count, unk // rows),
        in_specs=[SMEM, SMEM, SMEM, pl.BlockSpec(coordinates.shape, lambda t, m: (0, 0, 0))]
        + [pl.BlockSpec(memory_space=pltpu.HBM)] * len(held),
        out_specs=pl.BlockSpec((1, 2, rows, unk), lambda t, m: (t + first, 0, m, 0)),
        scratch_shapes=[pltpu.VMEM((8, unk), bf16), pltpu.VMEM((8, unk), bf16), pltpu.VMEM((rows, unk), f32)],
        input_output_aliases={4: 0} if held else {},
        compiler_params=pltpu.CompilerParams(vmem_limit_bytes=10 * MB),
        cost_estimate=pl.CostEstimate(
            flops=count * unk * unk * 30, transcendentals=count * unk * unk, bytes_accessed=count * unk * unk * 4
        ),
    )(at, blocks, panel, coordinates, *held)


def coupling_kernel(pivot, at_ref, panel_ref, g_ref, mine_ref, other_ref, *refs):
    if pivot:
        out_ref, lhs, stage, top, bottom, acc = refs
    else:
        pieces = refs[:4]
        out_ref, copies_ref, column_ref, lhs, stage, top, bottom, acc = refs[5:]
    tile, chunk = pl.program_id(0), pl.program_id(1)
    chunks = pl.num_programs(1)
    grp, core = at_ref[1], at_ref[2]
    groups, _, _, half, cols = mine_ref.shape
    rows = g_ref.shape[2]
    first = 2 if pivot else 0
    halves = ((mine_ref, core), (other_ref, 1 - core))

    def rows_of(g, part):
        return pl.ds(pl.multiple_of(g * 2 * half + part * half, half), half)

    @pl.when((tile == 0) & (chunk == 0))
    def _():
        if pivot:
            for g in range(groups):
                for src, part in halves:
                    r = rows_of(g, part)
                    stage[r, :cols] = src[g, first + core, 0]
                    stage[r, cols:] = src[g, first + core, 1]
        else:
            step = 0
            for piece in pieces:
                for k in range(piece.shape[0]):
                    r = pl.ds(pl.multiple_of((grp ^ step) * 2 * half, 2 * half), 2 * half)
                    stage[r, :cols] = piece[k, 0]
                    stage[r, cols:] = piece[k, 1]
                    step += 1
        lhs[...] = stage[...].T

    @pl.when(chunk == 0)
    def _():
        acc[...] = jnp.zeros_like(acc)
        for g in range(groups):
            for src, part in halves:
                r = rows_of(g, part)
                jr, ji = src[g, first + tile, 0], src[g, first + tile, 1]
                top[r, :cols] = jr
                top[r, cols:] = ji
                bottom[r, :cols] = -ji
                bottom[r, cols:] = jr

    y = jnp.dot(g_ref[0, 0], top[...], preferred_element_type=f32)
    y += jnp.dot(g_ref[0, 1], bottom[...], preferred_element_type=f32)
    y_hi = y.astype(bf16)
    y_lo = (y - y_hi.astype(f32)).astype(bf16)
    left = lhs[:, pl.ds(pl.multiple_of(chunk * rows, rows), rows)]
    acc[...] += jnp.dot(left, y_hi, preferred_element_type=f32) + jnp.dot(left, y_lo, preferred_element_type=f32)

    @pl.when(chunk == chunks - 1)
    def _():
        both = (2.0 * (acc[:cols, :cols] + acc[cols:, cols:]), 2.0 * (acc[:cols, cols:] - acc[cols:, :cols]))
        for part, value in enumerate(both):
            out_ref[part] = value
            if not pivot:
                for k in range(copies_ref.shape[0]):
                    copies_ref[k, part] = value.astype(bf16)
                for p in range(PANELS):
                    here = panel_ref[p] == grp * 2 + tile

                    @pl.when(here | (tile == 0))
                    def _():
                        column_ref[p, part] = value.astype(bf16)


def couplings(at, panel, green, mine, other, pieces, after, pivot):
    _, _, unk, _ = green.shape
    cols = mine.shape[4]
    tiles = 2
    first = 2 if pivot else 0
    rows = COUPLE_ROWS
    copies = 8
    whole = lambda x: pl.BlockSpec(x.shape, lambda t, m: (0,) * x.ndim)
    out_shape = [jax.ShapeDtypeStruct((2, cols, tiles * cols), f32)]
    out_specs = [pl.BlockSpec((2, cols, cols), lambda t, m: (0, 0, t))]
    if not pivot:
        out_shape.append(jax.ShapeDtypeStruct((copies, 2, cols, tiles * cols), bf16))
        out_specs.append(pl.BlockSpec((copies, 2, cols, cols), lambda t, m: (0, 0, 0, t)))
        out_shape.append(jax.ShapeDtypeStruct((PANELS, 2, cols, cols), bf16))
        out_specs.append(pl.BlockSpec((PANELS, 2, cols, cols), lambda t, m: (0, 0, 0, 0)))
    return pl.pallas_call(
        functools.partial(coupling_kernel, pivot),
        out_shape=out_shape,
        grid=(tiles, unk // rows),
        in_specs=[SMEM, SMEM, pl.BlockSpec((1, 2, rows, unk), lambda t, m: (t + first, 0, m, 0))]
        + [whole(x) for x in (mine, other, *pieces)]
        + [pl.BlockSpec(memory_space=pl.ANY)] * len(after),
        out_specs=out_specs,
        scratch_shapes=[
            pltpu.VMEM((2 * cols, unk), bf16),
            pltpu.VMEM((unk, 2 * cols), bf16),
            pltpu.VMEM((unk, 2 * cols), bf16),
            pltpu.VMEM((unk, 2 * cols), bf16),
            pltpu.VMEM((2 * cols, 2 * cols), f32),
        ],
        compiler_params=pltpu.CompilerParams(vmem_limit_bytes=20 * MB),
        cost_estimate=pl.CostEstimate(
            flops=tiles * unk * unk * 2048, transcendentals=0, bytes_accessed=tiles * unk * unk * 4
        ),
    )(at, panel, pltpu.with_memory_space_constraint(green, pltpu.HBM), mine, other, *pieces, *after)


WIDE = 128
PANEL = 32


def small_exchange(ar, ai, sub):
    ar, ai = list(ar), list(ai)
    for s in range(8):
        row = lambda x: jnp.broadcast_to(x[s : s + 1], x.shape)
        pr, pi = row(ar[s]), row(ai[s])
        scale = 1.0 / (pr * pr + pi * pi)
        qr, qi = pr * scale, pi * scale
        br, bi = ar[s], ai[s]
        for m in range(8):
            if m == s:
                vr, vi = -qr, qi
                xr, xi = br * qr + bi * qi, bi * qr - br * qi
            else:
                cr, ci = row(ar[m]), row(ai[m])
                wr, wi = br * cr - bi * ci, br * ci + bi * cr
                vr, vi = cr * qr + ci * qi, ci * qr - cr * qi
                xr, xi = ar[m] - (wr * qr + wi * qi), ai[m] - (wi * qr - wr * qi)
            ar[m], ai[m] = jnp.where(sub == s, -vr, xr), jnp.where(sub == s, -vi, xi)
    return ar, ai


def times(ar, ai, xr, xi, spread):
    nr = ni = None
    for m in range(8):
        cr, ci = spread(xr[m : m + 1]), spread(xi[m : m + 1])
        r, i = ar[m] * cr - ai[m] * ci, ar[m] * ci + ai[m] * cr
        nr, ni = (r, i) if nr is None else (nr + r, ni + i)
    return nr, ni


def inverse_kernel(kb, at_ref, first_ref, second_ref, re_ref, im_ref, rhs_ref):
    if kb == 0:
        core = at_ref[2]
        rows = first_ref.shape[1]
        for src, part in ((first_ref, core), (second_ref, 1 - core)):
            r = pl.ds(pl.multiple_of(part * rows, rows), rows)
            for h in range(2):
                re_ref[h, r, :] = src[0][:, h * WIDE : (h + 1) * WIDE]
                im_ref[h, r, :] = src[1][:, h * WIDE : (h + 1) * WIDE]
    else:
        re_ref[...] = first_ref[...]
        im_ref[...] = second_ref[...]
    rhs_ref[...] = jnp.zeros_like(rhs_ref)
    lane = lax.broadcasted_iota(i32, (8, WIDE), 1)
    sub = lax.broadcasted_iota(i32, (8, WIDE), 0)
    spread = lambda x: jnp.broadcast_to(x, (8, WIDE))
    groups = PANEL // 8

    order = (kb, 1 - kb)
    for t in range(WIDE // PANEL):
        r = slice(kb * WIDE + t * PANEL, kb * WIDE + (t + 1) * PANEL)
        block = [(re_ref[h, r, :], im_ref[h, r, :]) for h in order]
        tr = [[b[0][8 * g : 8 * g + 8] for g in range(groups)] for b in block]
        ti = [[b[1][8 * g : 8 * g + 8] for g in range(groups)] for b in block]
        for gs in range(groups):
            first = t * PANEL + 8 * gs
            ar = [[spread(x[:, first + m : first + m + 1]) for m in range(8)] for x in tr[0]]
            ai = [[spread(x[:, first + m : first + m + 1]) for m in range(8)] for x in ti[0]]
            dr, di = small_exchange(ar[gs], ai[gs], sub)
            within = (lane >= first) & (lane < first + 8)
            unit = jnp.where(lane == sub + first, -1.0, 0.0)
            xr = [jnp.where(within, unit, tr[0][gs]), tr[1][gs]]
            xi = [jnp.where(within, 0.0, ti[0][gs]), ti[1][gs]]
            for h in range(2):
                nr, ni = times(dr, di, xr[h], xi[h], spread)
                tr[h][gs], ti[h][gs] = -nr, -ni
            for g in range(groups):
                if g == gs:
                    continue
                for h in range(2):
                    nr, ni = times(ar[g], ai[g], tr[h][gs], ti[h][gs], spread)
                    yr, yi = tr[h][g], ti[h][g]
                    if h == 0:
                        yr, yi = jnp.where(within, 0.0, yr), jnp.where(within, 0.0, yi)
                    tr[h][g], ti[h][g] = yr + nr, yi + ni
        pr = jnp.concatenate([jnp.concatenate(tr[h], 0) for h in range(2)], 1)
        pi = jnp.concatenate([jnp.concatenate(ti[h], 0) for h in range(2)], 1)
        top, low = slice(t * PANEL, (t + 1) * PANEL), slice(WIDE + t * PANEL, WIDE + (t + 1) * PANEL)
        rhs_ref[top, :] = jnp.concatenate([pr, pi], 1)
        rhs_ref[low, :] = jnp.concatenate([-pi, pr], 1)
        old = jnp.concatenate([re_ref[kb], im_ref[kb]], 1)
        upd = jnp.dot(old, rhs_ref[...], precision=lax.Precision.HIGHEST, preferred_element_type=f32)
        rhs_ref[top, :] = jnp.zeros((PANEL, 4 * WIDE), f32)
        rhs_ref[low, :] = jnp.zeros((PANEL, 4 * WIDE), f32)
        wide_lane = lax.broadcasted_iota(i32, upd[:, :WIDE].shape, 1)
        gone = (wide_lane >= t * PANEL) & (wide_lane < (t + 1) * PANEL)
        re_ref[kb] = jnp.where(gone, 0.0, re_ref[kb]) + upd[:, :WIDE]
        im_ref[kb] = jnp.where(gone, 0.0, im_ref[kb]) + upd[:, 2 * WIDE : 3 * WIDE]
        re_ref[1 - kb] += upd[:, WIDE : 2 * WIDE]
        im_ref[1 - kb] += upd[:, 3 * WIDE :]
        for n, h in enumerate(order):
            re_ref[h, r, :] = pr[:, n * WIDE : (n + 1) * WIDE]
            im_ref[h, r, :] = pi[:, n * WIDE : (n + 1) * WIDE]


def pivot_exchange(kb, at, first, second):
    order = PANELS * WIDE
    part = jax.ShapeDtypeStruct((2, order, WIDE), f32)
    return pl.pallas_call(
        functools.partial(inverse_kernel, kb),
        out_shape=(part, part),
        in_specs=[SMEM, VMEM, VMEM],
        out_specs=(VMEM, VMEM),
        scratch_shapes=[pltpu.VMEM((2 * WIDE, 4 * WIDE), f32)],
        compiler_params=pltpu.CompilerParams(vmem_limit_bytes=12 * MB),
        cost_estimate=pl.CostEstimate(flops=int(6e9), transcendentals=0, bytes_accessed=1 << 20),
    )(at, first, second)


def split3(x):
    hi = x.astype(bf16)
    rest = x - hi.astype(f32)
    mid = rest.astype(bf16)
    low = (rest - mid.astype(f32)).astype(bf16)
    return hi, mid, low


def schur_kernel(info, re_ref, im_ref, mine_ref, other_ref, c_ref, r_ref, out_ref):
    core = info[0]
    funcs = mine_ref.shape[2]
    b = []
    for p in range(PANELS):
        local = info[1 + p] == core
        b.append([jnp.where(local, mine_ref[p, k].astype(f32), other_ref[p, k].astype(f32)).astype(bf16) for k in range(2)])
    br = jnp.concatenate([b[p][0] for p in range(PANELS)], 0)
    bi = jnp.concatenate([b[p][1] for p in range(PANELS)], 0)
    right = jnp.concatenate([jnp.concatenate([br, bi], 1), jnp.concatenate([-bi, br], 1)], 0)
    w = jnp.zeros((PANELS * funcs, right.shape[1]), f32)
    for x in split3(jnp.concatenate([re_ref[0], re_ref[1], im_ref[0], im_ref[1]], 1)):
        w += jnp.dot(x, right, preferred_element_type=f32)
    cols = w.shape[1] // 2
    w_hi = w.astype(bf16)
    w_lo = (w - w_hi.astype(f32)).astype(bf16)
    cr = jnp.concatenate([c_ref[0, 0], c_ref[1, 0]], 1)
    ci = jnp.concatenate([c_ref[0, 1], c_ref[1, 1]], 1)
    left = jnp.concatenate([cr, ci], 0)
    prod = jnp.dot(left, w_hi, preferred_element_type=f32) + jnp.dot(left, w_lo, preferred_element_type=f32)
    rows = cr.shape[0]
    out_ref[0] = r_ref[0] - (prod[:rows, :cols] - prod[rows:, cols:])
    out_ref[1] = r_ref[1] - (prod[:rows, cols:] + prod[rows:, :cols])


def schur_tile(info, re, im, mine, other, column, reduced):
    return pl.pallas_call(
        schur_kernel,
        out_shape=jax.ShapeDtypeStruct(reduced.shape, f32),
        in_specs=[SMEM] + [VMEM] * 6,
        out_specs=VMEM,
        compiler_params=pltpu.CompilerParams(vmem_limit_bytes=12 * MB),
        name="schur",
    )(info, re, im, mine, other, column, reduced)


def on_device(inverse, excite, coordinates, block_of_slot, panel_order):
    blk_size, grp_size = lax.axis_size("blk"), lax.axis_size("grp")
    blocks = block_of_slot.shape[0]
    slot, grp = lax.axis_index("blk").astype(i32), lax.axis_index("grp").astype(i32)
    core = slot % 2
    slabs = blocks // grp_size
    swap = [(i, i ^ 1) for i in range(blk_size)]
    same_core = [list(range(c, blk_size, 2)) for c in range(2)]
    at = jnp.stack([slot, grp, core])

    def spread(x, axis, groups=None):
        return lax.all_to_all(x, axis, split_axis=0, concat_axis=0, tiled=True, axis_index_groups=groups)

    order = jnp.arange(blocks, dtype=i32)
    slot_of = jnp.sum(jnp.where(block_of_slot[None, :] == order[:, None], order[None, :], 0), axis=1)
    pivots = panel_order[:PANELS]

    own, keep, send = basis_rows(core.reshape(1), inverse, excite)
    got = lax.ppermute(send, "blk", swap)
    pair = jnp.stack([keep, got])
    pair = jnp.broadcast_to(pair[None], (blk_size // 2, *pair.shape))
    sliced = spread(pair, "blk", same_core)
    sliced = sliced.reshape(blk_size, *keep.shape)

    pieces, held, bit = [own], own, 1
    while bit < grp_size:
        pieces.append(lax.ppermute(held, "grp", [(g, g ^ bit) for g in range(grp_size)]))
        bit *= 2
        if bit < grp_size:
            held = jnp.concatenate([held, pieces[-1]], 0)

    green = green_tiles(at, block_of_slot, panel_order, coordinates, 0, 1, 2 + PANELS, [])
    green = green_tiles(at, block_of_slot, panel_order, coordinates, 1, 1, 2 + PANELS, [green])
    green = green_tiles(at, block_of_slot, panel_order, coordinates, 2, PANELS, 2 + PANELS, [green])

    wanted = jnp.concatenate(
        [order.reshape(grp_size, slabs), jnp.broadcast_to(pivots[None], (grp_size, PANELS))], axis=1
    )
    from_slot = jnp.sum(jnp.where(wanted[:, :, None] == order, slot_of, 0), axis=2)
    place = (from_slot // 2) * 2 + (from_slot % 2 + core) % 2
    picked = sliced.at[place.reshape(-1)].get(mode="promise_in_bounds").reshape(*place.shape, *keep.shape)
    mine = spread(picked, "grp")
    other = lax.ppermute(mine, "blk", swap)

    (pivot_rows,) = couplings(at, panel_order, green, mine, other, [], [], True)
    pivot_other = lax.ppermute(pivot_rows, "blk", swap)
    reduced, copies, column = couplings(at, panel_order, green, mine, other, pieces, [pivot_rows], False)

    rows = spread(copies, "blk", same_core)
    column_at = pivots // slabs
    bit = 1
    while bit < grp_size:
        came = lax.ppermute(column, "grp", [(g, g ^ bit) for g in range(grp_size)])
        take = ((grp ^ column_at) & bit) != 0
        column = jnp.where(take[:, None, None, None], came, column)
        bit *= 2
    pivot_slot = jnp.sum(jnp.where(pivots[:, None] == order, slot_of, 0), axis=1)
    row_mine = jnp.stack([lax.dynamic_index_in_dim(rows, pivot_slot[p] // 2, 0, keepdims=False) for p in range(PANELS)])
    row_other = lax.ppermute(row_mine, "blk", swap)
    core1 = core.reshape(1)
    re, im = pivot_exchange(0, at, pivot_rows, pivot_other)
    re, im = pivot_exchange(1, at, re, im)
    info = jnp.concatenate([core1, pivot_slot % 2]).astype(i32)
    schur = schur_tile(info, re, im, row_mine, row_other, column, reduced)
    return (reduced, schur)


def solution(mesh):
    placed = (P(None, "blk", "grp", None), P(None, "blk", None, None), P(), P(), P())
    return jax.shard_map(
        on_device,
        mesh=mesh,
        in_specs=placed,
        out_specs=(P(None, "blk", "grp"), P(None, "blk", "grp")),
        check_vma=False,
    )
```

```python
import functools

import jax
import jax.numpy as jnp
import numpy as np
from jax import lax
from jax.experimental import pallas as pl
from jax.experimental.pallas import tpu as pltpu
from jax.sharding import PartitionSpec as P


PANELS = 2
bf16 = jnp.bfloat16
f32 = jnp.float32
i32 = jnp.int32

SELF_REAL = 6.0
SELF_IMAG = -1.5
TURNS = 1.3 / (2 * np.pi)
SHIFT = float(1.5 * 2**23)
SIN = (4.44288283, -7.30824115, 3.60628896, -0.8457636, 0.10920575)
COS = (-1.4142135, 6.97885099, -5.73946117, 1.88356298, -0.31069819)
VMEM = pl.BlockSpec(memory_space=pltpu.VMEM)
SMEM = pl.BlockSpec(memory_space=pltpu.SMEM)
MB = 1 << 20
COUPLE_ROWS = 512
GREEN_ROWS = 512
STRIPS = 4


def horner(coefs, g):
    r = coefs[-1]
    for k in coefs[-2::-1]:
        r = r * g + k
    return r


def half_green(sq):
    inv_r = lax.rsqrt(sq)
    turns = (sq * inv_r) * TURNS
    f = turns - ((turns + SHIFT) - SHIFT)
    g = f * f
    s = horner(SIN, g) * f
    c = horner(COS, g)
    scaled = s * inv_r
    return inv_r - s * scaled, c * scaled


def basis_kernel(inv_ref, exc_ref, own_ref, halves_ref):
    er, ei = exc_ref[0, 0], exc_ref[1, 0]
    j = jnp.dot(inv_ref[0, 0], jnp.concatenate([er, ei], 1), preferred_element_type=f32)
    j += jnp.dot(inv_ref[1, 0], jnp.concatenate([-ei, er], 1), preferred_element_type=f32)
    cols, half = j.shape[1] // 2, j.shape[0] // 2
    jb = j.astype(bf16)
    for part in range(2):
        own_ref[0, part] = jb[:, part * cols : (part + 1) * cols]
        for k in range(halves_ref.shape[0]):
            halves_ref[k, part] = jb[(k % 2) * half : (k % 2 + 1) * half, part * cols : (part + 1) * cols]


def basis_rows(inverse, excite, devices):
    rows, cols = inverse.shape[2], excite.shape[3]
    return pl.pallas_call(
        basis_kernel,
        out_shape=(
            jax.ShapeDtypeStruct((1, 2, rows, cols), bf16),
            jax.ShapeDtypeStruct((devices, 2, rows // 2, cols), bf16),
        ),
        in_specs=[VMEM, VMEM],
        out_specs=(VMEM, VMEM),
        compiler_params=pltpu.CompilerParams(vmem_limit_bytes=8 * MB),
        name="basis",
    )(inverse, excite)


def features(coords_ref, block, left):
    x, y, z = [coords_ref[d, pl.ds(block, 1), :] for d in range(3)]
    norm = x * x + y * y + z * z
    low = norm & 63
    high = norm - low
    one, zero = jnp.ones_like(norm), jnp.zeros_like(norm)
    rows = [-2 * x, -2 * y, -2 * z, high, low, one, one] if left else [x, y, z, one, one, high, low]
    return jnp.concatenate([v.astype(f32) for v in rows + [zero]], 0).astype(bf16)


def green_kernel(tiles, at_ref, coords_ref, *refs):
    g_ref, fl_ref, fr_ref, sq_ref = refs[-4:]
    rows, _ = sq_ref.shape
    tile, chunk = pl.program_id(0) + tiles, pl.program_id(1)
    blocks = coords_ref.shape[1]
    own, grp, core = at_ref[3 + at_ref[0]], at_ref[1], at_ref[2]
    main = tile < 2
    left = jnp.where(main, own, at_ref[3 + blocks + core])
    right = jnp.where(main, grp * 2 + tile, at_ref[3 + blocks + jnp.maximum(tile - 2, 0)])

    @pl.when(chunk == 0)
    def _():
        fl_ref[...] = features(coords_ref, left, True)
        fr_ref[...] = features(coords_ref, right, False)

    at = pl.ds(pl.multiple_of(chunk * rows, rows), rows)
    sq_ref[...] = lax.dot_general(
        fl_ref[:, at], fr_ref[...], (((0,), (0,)), ((), ())), preferred_element_type=f32
    )

    def strip(i, _):
        r = pl.ds(pl.multiple_of(i * 8, 8), 8)
        re, im = half_green(sq_ref[r, :])
        g_ref[0, 0, r, :] = re.astype(bf16)
        g_ref[0, 1, r, :] = im.astype(bf16)
        return 0

    lax.fori_loop(0, rows // 8, strip, 0, unroll=STRIPS)

    @pl.when(left == right)
    def _():
        same = lax.broadcasted_iota(i32, (rows, rows), 0) == lax.broadcasted_iota(i32, (rows, rows), 1)
        for part, value in ((0, SELF_REAL), (1, SELF_IMAG)):
            block = g_ref[0, part, :, at].astype(f32)
            g_ref[0, part, :, at] = jnp.where(same, value, block).astype(bf16)


def green_tiles(at, coordinates, first, count, tiles, held):
    unk = coordinates.shape[2]
    rows = GREEN_ROWS
    return pl.pallas_call(
        functools.partial(green_kernel, first),
        out_shape=pltpu.HBM((tiles, 2, unk, unk), bf16),
        grid=(count, unk // rows),
        in_specs=[SMEM, pl.BlockSpec(coordinates.shape, lambda t, m: (0, 0, 0))]
        + [pl.BlockSpec(memory_space=pltpu.HBM)] * len(held),
        out_specs=pl.BlockSpec((1, 2, rows, unk), lambda t, m: (t + first, 0, m, 0)),
        scratch_shapes=[pltpu.VMEM((8, unk), bf16), pltpu.VMEM((8, unk), bf16), pltpu.VMEM((rows, unk), f32)],
        input_output_aliases={2: 0} if held else {},
        compiler_params=pltpu.CompilerParams(vmem_limit_bytes=10 * MB),
        cost_estimate=pl.CostEstimate(
            flops=count * unk * unk * 30, transcendentals=count * unk * unk, bytes_accessed=count * unk * unk * 4
        ),
    )(at, pltpu.with_memory_space_constraint(coordinates, pltpu.HBM), *held)


def coupling_kernel(pivot, panel_at, at_ref, g_ref, mine_ref, other_ref, *refs):
    if pivot:
        out_ref, lhs, stage, top, bottom, acc = refs
    else:
        pieces = refs[:4]
        out_ref, copies_ref, column_ref, lhs, stage, top, bottom, acc = refs[5:]
    tile, chunk = pl.program_id(0), pl.program_id(1)
    chunks = pl.num_programs(1)
    grp, core = at_ref[1], at_ref[2]
    groups, _, _, half, cols = mine_ref.shape
    rows = g_ref.shape[2]
    first = 2 if pivot else 0
    halves = ((mine_ref, core), (other_ref, 1 - core))

    def rows_of(g, part):
        return pl.ds(pl.multiple_of(g * 2 * half + part * half, half), half)

    @pl.when((tile == 0) & (chunk == 0))
    def _():
        if pivot:
            for g in range(groups):
                for src, part in halves:
                    r = rows_of(g, part)
                    stage[r, :cols] = src[g, first + core, 0]
                    stage[r, cols:] = src[g, first + core, 1]
        else:
            step = 0
            for piece in pieces:
                for k in range(piece.shape[0]):
                    r = pl.ds(pl.multiple_of((grp ^ step) * 2 * half, 2 * half), 2 * half)
                    stage[r, :cols] = piece[k, 0]
                    stage[r, cols:] = piece[k, 1]
                    step += 1
        lhs[...] = stage[...].T

    @pl.when(chunk == 0)
    def _():
        acc[...] = jnp.zeros_like(acc)
        for g in range(groups):
            for src, part in halves:
                r = rows_of(g, part)
                jr, ji = src[g, first + tile, 0], src[g, first + tile, 1]
                top[r, :cols] = jr
                top[r, cols:] = ji
                bottom[r, :cols] = -ji
                bottom[r, cols:] = jr

    y = jnp.dot(g_ref[0, 0], top[...], preferred_element_type=f32)
    y += jnp.dot(g_ref[0, 1], bottom[...], preferred_element_type=f32)
    y_hi = y.astype(bf16)
    y_lo = (y - y_hi.astype(f32)).astype(bf16)
    left = lhs[:, pl.ds(pl.multiple_of(chunk * rows, rows), rows)]
    acc[...] += jnp.dot(left, y_hi, preferred_element_type=f32) + jnp.dot(left, y_lo, preferred_element_type=f32)

    @pl.when(chunk == chunks - 1)
    def _():
        both = (2.0 * (acc[:cols, :cols] + acc[cols:, cols:]), 2.0 * (acc[:cols, cols:] - acc[cols:, :cols]))
        for part, value in enumerate(both):
            out_ref[part] = value
            if not pivot:
                for k in range(copies_ref.shape[0]):
                    copies_ref[k, part] = value.astype(bf16)
                for p in range(PANELS):
                    here = at_ref[panel_at + p] == grp * 2 + tile

                    @pl.when(here | (tile == 0))
                    def _():
                        column_ref[p, part] = value.astype(bf16)


def couplings(at, blocks, green, mine, other, pieces, after, pivot):
    _, _, unk, _ = green.shape
    cols = mine.shape[4]
    tiles = 2
    first = 2 if pivot else 0
    rows = COUPLE_ROWS
    copies = 8
    whole = lambda x: pl.BlockSpec(x.shape, lambda t, m: (0,) * x.ndim)
    out_shape = [jax.ShapeDtypeStruct((2, cols, tiles * cols), f32)]
    out_specs = [pl.BlockSpec((2, cols, cols), lambda t, m: (0, 0, t))]
    if not pivot:
        out_shape.append(jax.ShapeDtypeStruct((copies, 2, cols, tiles * cols), bf16))
        out_specs.append(pl.BlockSpec((copies, 2, cols, cols), lambda t, m: (0, 0, 0, t)))
        out_shape.append(jax.ShapeDtypeStruct((PANELS, 2, cols, cols), bf16))
        out_specs.append(pl.BlockSpec((PANELS, 2, cols, cols), lambda t, m: (0, 0, 0, 0)))
    return pl.pallas_call(
        functools.partial(coupling_kernel, pivot, 3 + blocks),
        out_shape=out_shape,
        grid=(tiles, unk // rows),
        in_specs=[SMEM, pl.BlockSpec((1, 2, rows, unk), lambda t, m: (t + first, 0, m, 0))]
        + [whole(x) for x in (mine, other, *pieces)]
        + [pl.BlockSpec(memory_space=pl.ANY)] * len(after),
        out_specs=out_specs,
        scratch_shapes=[
            pltpu.VMEM((2 * cols, unk), bf16),
            pltpu.VMEM((unk, 2 * cols), bf16),
            pltpu.VMEM((unk, 2 * cols), bf16),
            pltpu.VMEM((unk, 2 * cols), bf16),
            pltpu.VMEM((2 * cols, 2 * cols), f32),
        ],
        compiler_params=pltpu.CompilerParams(vmem_limit_bytes=20 * MB),
        cost_estimate=pl.CostEstimate(
            flops=tiles * unk * unk * 2048, transcendentals=0, bytes_accessed=tiles * unk * unk * 4
        ),
    )(at, pltpu.with_memory_space_constraint(green, pltpu.HBM), mine, other, *pieces, *after)


WIDE = 128
PANEL = 32


def small_exchange(ar, ai, sub):
    ar, ai = list(ar), list(ai)
    for s in range(8):
        row = lambda x: jnp.broadcast_to(x[s : s + 1], x.shape)
        pr, pi = row(ar[s]), row(ai[s])
        scale = 1.0 / (pr * pr + pi * pi)
        qr, qi = pr * scale, pi * scale
        br, bi = ar[s], ai[s]
        for m in range(8):
            if m == s:
                vr, vi = -qr, qi
                xr, xi = br * qr + bi * qi, bi * qr - br * qi
            else:
                cr, ci = row(ar[m]), row(ai[m])
                wr, wi = br * cr - bi * ci, br * ci + bi * cr
                vr, vi = cr * qr + ci * qi, ci * qr - cr * qi
                xr, xi = ar[m] - (wr * qr + wi * qi), ai[m] - (wi * qr - wr * qi)
            ar[m], ai[m] = jnp.where(sub == s, -vr, xr), jnp.where(sub == s, -vi, xi)
    return ar, ai


def times(ar, ai, xr, xi, spread):
    nr = ni = None
    for m in range(8):
        cr, ci = spread(xr[m : m + 1]), spread(xi[m : m + 1])
        r, i = ar[m] * cr - ai[m] * ci, ar[m] * ci + ai[m] * cr
        nr, ni = (r, i) if nr is None else (nr + r, ni + i)
    return nr, ni


def inverse_kernel(kb, at_ref, first_ref, second_ref, re_ref, im_ref, rhs_ref):
    if kb == 0:
        core = at_ref[2]
        rows = first_ref.shape[1]
        for src, part in ((first_ref, core), (second_ref, 1 - core)):
            r = pl.ds(pl.multiple_of(part * rows, rows), rows)
            for h in range(2):
                re_ref[h, r, :] = src[0][:, h * WIDE : (h + 1) * WIDE]
                im_ref[h, r, :] = src[1][:, h * WIDE : (h + 1) * WIDE]
    else:
        re_ref[...] = first_ref[...]
        im_ref[...] = second_ref[...]
    rhs_ref[...] = jnp.zeros_like(rhs_ref)
    lane = lax.broadcasted_iota(i32, (8, WIDE), 1)
    sub = lax.broadcasted_iota(i32, (8, WIDE), 0)
    spread = lambda x: jnp.broadcast_to(x, (8, WIDE))
    groups = PANEL // 8

    order = (kb, 1 - kb)
    for t in range(WIDE // PANEL):
        r = slice(kb * WIDE + t * PANEL, kb * WIDE + (t + 1) * PANEL)
        block = [(re_ref[h, r, :], im_ref[h, r, :]) for h in order]
        tr = [[b[0][8 * g : 8 * g + 8] for g in range(groups)] for b in block]
        ti = [[b[1][8 * g : 8 * g + 8] for g in range(groups)] for b in block]
        for gs in range(groups):
            first = t * PANEL + 8 * gs
            ar = [[spread(x[:, first + m : first + m + 1]) for m in range(8)] for x in tr[0]]
            ai = [[spread(x[:, first + m : first + m + 1]) for m in range(8)] for x in ti[0]]
            dr, di = small_exchange(ar[gs], ai[gs], sub)
            within = (lane >= first) & (lane < first + 8)
            unit = jnp.where(lane == sub + first, -1.0, 0.0)
            xr = [jnp.where(within, unit, tr[0][gs]), tr[1][gs]]
            xi = [jnp.where(within, 0.0, ti[0][gs]), ti[1][gs]]
            for h in range(2):
                nr, ni = times(dr, di, xr[h], xi[h], spread)
                tr[h][gs], ti[h][gs] = -nr, -ni
            for g in range(groups):
                if g == gs:
                    continue
                for h in range(2):
                    nr, ni = times(ar[g], ai[g], tr[h][gs], ti[h][gs], spread)
                    yr, yi = tr[h][g], ti[h][g]
                    if h == 0:
                        yr, yi = jnp.where(within, 0.0, yr), jnp.where(within, 0.0, yi)
                    tr[h][g], ti[h][g] = yr + nr, yi + ni
        pr = jnp.concatenate([jnp.concatenate(tr[h], 0) for h in range(2)], 1)
        pi = jnp.concatenate([jnp.concatenate(ti[h], 0) for h in range(2)], 1)
        top, low = slice(t * PANEL, (t + 1) * PANEL), slice(WIDE + t * PANEL, WIDE + (t + 1) * PANEL)
        rhs_ref[top, :] = jnp.concatenate([pr, pi], 1)
        rhs_ref[low, :] = jnp.concatenate([-pi, pr], 1)
        old = jnp.concatenate([re_ref[kb], im_ref[kb]], 1)
        upd = jnp.dot(old, rhs_ref[...], precision=lax.Precision.HIGHEST, preferred_element_type=f32)
        rhs_ref[top, :] = jnp.zeros((PANEL, 4 * WIDE), f32)
        rhs_ref[low, :] = jnp.zeros((PANEL, 4 * WIDE), f32)
        wide_lane = lax.broadcasted_iota(i32, upd[:, :WIDE].shape, 1)
        gone = (wide_lane >= t * PANEL) & (wide_lane < (t + 1) * PANEL)
        re_ref[kb] = jnp.where(gone, 0.0, re_ref[kb]) + upd[:, :WIDE]
        im_ref[kb] = jnp.where(gone, 0.0, im_ref[kb]) + upd[:, 2 * WIDE : 3 * WIDE]
        re_ref[1 - kb] += upd[:, WIDE : 2 * WIDE]
        im_ref[1 - kb] += upd[:, 3 * WIDE :]
        for n, h in enumerate(order):
            re_ref[h, r, :] = pr[:, n * WIDE : (n + 1) * WIDE]
            im_ref[h, r, :] = pi[:, n * WIDE : (n + 1) * WIDE]


def pivot_exchange(kb, at, first, second):
    order = PANELS * WIDE
    part = jax.ShapeDtypeStruct((2, order, WIDE), f32)
    return pl.pallas_call(
        functools.partial(inverse_kernel, kb),
        out_shape=(part, part),
        in_specs=[SMEM, VMEM, VMEM],
        out_specs=(VMEM, VMEM),
        scratch_shapes=[pltpu.VMEM((2 * WIDE, 4 * WIDE), f32)],
        compiler_params=pltpu.CompilerParams(vmem_limit_bytes=12 * MB),
        cost_estimate=pl.CostEstimate(flops=int(6e9), transcendentals=0, bytes_accessed=1 << 20),
    )(at, first, second)


def split3(x):
    hi = x.astype(bf16)
    rest = x - hi.astype(f32)
    mid = rest.astype(bf16)
    low = (rest - mid.astype(f32)).astype(bf16)
    return hi, mid, low


def schur_kernel(info, re_ref, im_ref, mine_ref, other_ref, c_ref, r_ref, out_ref):
    core = info[0]
    funcs = mine_ref.shape[2]
    b = []
    for p in range(PANELS):
        local = info[1 + p] == core
        b.append([jnp.where(local, mine_ref[p, k].astype(f32), other_ref[p, k].astype(f32)).astype(bf16) for k in range(2)])
    br = jnp.concatenate([b[p][0] for p in range(PANELS)], 0)
    bi = jnp.concatenate([b[p][1] for p in range(PANELS)], 0)
    right = jnp.concatenate([jnp.concatenate([br, bi], 1), jnp.concatenate([-bi, br], 1)], 0)
    w = jnp.zeros((PANELS * funcs, right.shape[1]), f32)
    for x in split3(jnp.concatenate([re_ref[0], re_ref[1], im_ref[0], im_ref[1]], 1)):
        w += jnp.dot(x, right, preferred_element_type=f32)
    cols = w.shape[1] // 2
    w_hi = w.astype(bf16)
    w_lo = (w - w_hi.astype(f32)).astype(bf16)
    cr = jnp.concatenate([c_ref[0, 0], c_ref[1, 0]], 1)
    ci = jnp.concatenate([c_ref[0, 1], c_ref[1, 1]], 1)
    left = jnp.concatenate([cr, ci], 0)
    prod = jnp.dot(left, w_hi, preferred_element_type=f32) + jnp.dot(left, w_lo, preferred_element_type=f32)
    rows = cr.shape[0]
    out_ref[0] = r_ref[0] - (prod[:rows, :cols] - prod[rows:, cols:])
    out_ref[1] = r_ref[1] - (prod[:rows, cols:] + prod[rows:, :cols])


def schur_tile(info, re, im, mine, other, column, reduced):
    return pl.pallas_call(
        schur_kernel,
        out_shape=jax.ShapeDtypeStruct(reduced.shape, f32),
        in_specs=[SMEM] + [VMEM] * 6,
        out_specs=VMEM,
        compiler_params=pltpu.CompilerParams(vmem_limit_bytes=12 * MB),
        name="schur",
    )(info, re, im, mine, other, column, reduced)


def on_device(inverse, excite, coordinates, block_of_slot, panel_order):
    blk_size, grp_size = lax.axis_size("blk"), lax.axis_size("grp")
    blocks = block_of_slot.shape[0]
    slot, grp = lax.axis_index("blk").astype(i32), lax.axis_index("grp").astype(i32)
    core = slot % 2
    slabs = blocks // grp_size
    swap = [(i, i ^ 1) for i in range(blk_size)]
    same_core = [list(range(c, blk_size, 2)) for c in range(2)]
    at = jnp.concatenate([jnp.stack([slot, grp, core]), block_of_slot, panel_order])

    def spread(x, axis, groups=None):
        return lax.all_to_all(x, axis, split_axis=0, concat_axis=0, tiled=True, axis_index_groups=groups)

    order = jnp.arange(blocks, dtype=i32)
    slot_of = jnp.sum(jnp.where(block_of_slot[None, :] == order[:, None], order[None, :], 0), axis=1)
    pivots = panel_order[:PANELS]

    own, halves = basis_rows(inverse, excite, blk_size)
    sliced = spread(halves, "blk")

    pieces, held, bit = [own], own, 1
    while bit < grp_size:
        pieces.append(lax.ppermute(held, "grp", [(g, g ^ bit) for g in range(grp_size)]))
        bit *= 2
        if bit < grp_size:
            held = jnp.concatenate([held, pieces[-1]], 0)

    tiles = slabs + PANELS
    green = green_tiles(at, coordinates, 0, 1, tiles, [])
    green = green_tiles(at, coordinates, 2, PANELS, tiles, [green])
    green = green_tiles(at, coordinates, 1, 1, tiles, [green])

    wanted = jnp.concatenate(
        [order.reshape(grp_size, slabs), jnp.broadcast_to(pivots[None], (grp_size, PANELS))], axis=1
    )
    from_slot = jnp.sum(jnp.where(wanted[:, :, None] == order, slot_of, 0), axis=2)
    picked = sliced.at[from_slot.reshape(-1)].get(mode="promise_in_bounds")
    picked = picked.reshape(*from_slot.shape, *sliced.shape[1:])
    mine = spread(picked, "grp")
    other = lax.ppermute(mine, "blk", swap)

    (pivot_rows,) = couplings(at, blocks, green, mine, other, [], [], True)
    pivot_other = lax.ppermute(pivot_rows, "blk", swap)
    reduced, copies, column = couplings(at, blocks, green, mine, other, pieces, [pivot_rows], False)

    rows = spread(copies, "blk", same_core)
    column_at = pivots // slabs
    bit = 1
    while bit < grp_size:
        came = lax.ppermute(column, "grp", [(g, g ^ bit) for g in range(grp_size)])
        take = ((grp ^ column_at) & bit) != 0
        column = jnp.where(take[:, None, None, None], came, column)
        bit *= 2
    pivot_slot = jnp.sum(jnp.where(pivots[:, None] == order, slot_of, 0), axis=1)
    row_mine = jnp.stack([lax.dynamic_index_in_dim(rows, pivot_slot[p] // 2, 0, keepdims=False) for p in range(PANELS)])
    row_other = lax.ppermute(row_mine, "blk", swap)
    core1 = core.reshape(1)
    re, im = pivot_exchange(0, at, pivot_rows, pivot_other)
    re, im = pivot_exchange(1, at, re, im)
    info = jnp.concatenate([core1, pivot_slot % 2]).astype(i32)
    schur = schur_tile(info, re, im, row_mine, row_other, column, reduced)
    return (reduced, schur)


def solution(mesh):
    placed = (P(None, "blk", "grp", None), P(None, "blk", None, None), P(), P(), P())
    return jax.shard_map(
        on_device,
        mesh=mesh,
        in_specs=placed,
        out_specs=(P(None, "blk", "grp"), P(None, "blk", "grp")),
        check_vma=False,
    )
```

```python
import functools

import jax
import jax.numpy as jnp
import numpy as np
from jax import lax
from jax.experimental import pallas as pl
from jax.experimental.pallas import tpu as pltpu
from jax.sharding import PartitionSpec as P


PANELS = 2
bf16 = jnp.bfloat16
f32 = jnp.float32
i32 = jnp.int32

SELF_REAL = 6.0
SELF_IMAG = -1.5
TURNS = 1.3 / (2 * np.pi)
SHIFT = float(1.5 * 2**23)
SIN = (4.44288283, -7.30824115, 3.60628896, -0.8457636, 0.10920575)
COS = (-1.4142135, 6.97885099, -5.73946117, 1.88356298, -0.31069819)
VMEM = pl.BlockSpec(memory_space=pltpu.VMEM)
SMEM = pl.BlockSpec(memory_space=pltpu.SMEM)
MB = 1 << 20
COUPLE_ROWS = 512
GREEN_ROWS = 512
STRIPS = 4


def horner(coefs, g):
    r = coefs[-1]
    for k in coefs[-2::-1]:
        r = r * g + k
    return r


def half_green(sq):
    inv_r = lax.rsqrt(sq)
    turns = (sq * inv_r) * TURNS
    f = turns - ((turns + SHIFT) - SHIFT)
    g = f * f
    s = horner(SIN, g) * f
    c = horner(COS, g)
    scaled = s * inv_r
    return inv_r - s * scaled, c * scaled


def basis_kernel(inv_ref, exc_ref, own_ref, halves_ref):
    er, ei = exc_ref[0, 0], exc_ref[1, 0]
    j = jnp.dot(inv_ref[0, 0], jnp.concatenate([er, ei], 1), preferred_element_type=f32)
    j += jnp.dot(inv_ref[1, 0], jnp.concatenate([-ei, er], 1), preferred_element_type=f32)
    cols, half = j.shape[1] // 2, j.shape[0] // 2
    jb = j.astype(bf16)
    for part in range(2):
        own_ref[0, part] = jb[:, part * cols : (part + 1) * cols]
        for k in range(halves_ref.shape[0]):
            halves_ref[k, part] = jb[(k % 2) * half : (k % 2 + 1) * half, part * cols : (part + 1) * cols]


def basis_rows(inverse, excite, devices):
    rows, cols = inverse.shape[2], excite.shape[3]
    return pl.pallas_call(
        basis_kernel,
        out_shape=(
            jax.ShapeDtypeStruct((1, 2, rows, cols), bf16),
            jax.ShapeDtypeStruct((devices, 2, rows // 2, cols), bf16),
        ),
        in_specs=[VMEM, VMEM],
        out_specs=(VMEM, VMEM),
        compiler_params=pltpu.CompilerParams(vmem_limit_bytes=8 * MB),
        name="basis",
    )(inverse, excite)


def slot_with(at, block, blocks):
    slot = 0
    for s in range(blocks):
        slot = slot + jnp.where(at[3 + s] == block, s, 0)
    return slot


def gather_kernel(at_ref, rows_ref, out_ref, slot_ref):
    blocks = rows_ref.shape[0]
    for s in range(blocks):
        slot_ref[at_ref[3 + s]] = s
    groups, entries = out_ref.shape[:2]
    slabs = entries - PANELS
    for p in range(PANELS):
        value = rows_ref[slot_ref[at_ref[3 + blocks + p]]]
        for g in range(groups):
            out_ref[g, slabs + p] = value
    for g in range(groups):
        for e in range(slabs):
            out_ref[g, e] = rows_ref[slot_ref[g * slabs + e]]


def gathered(at, rows, groups, slabs):
    return pl.pallas_call(
        gather_kernel,
        out_shape=jax.ShapeDtypeStruct((groups, slabs + PANELS, *rows.shape[1:]), rows.dtype),
        in_specs=[SMEM, VMEM],
        out_specs=VMEM,
        scratch_shapes=[pltpu.SMEM((rows.shape[0],), i32)],
        compiler_params=pltpu.CompilerParams(vmem_limit_bytes=8 * MB),
        name="gathered",
    )(at, rows)


def pick_kernel(at_ref, row_ref, out_ref):
    out_ref[...] = row_ref[...]


def pivot_tiles(at, rows, blocks):
    shape = (1, *rows.shape[1:])
    return pl.pallas_call(
        pick_kernel,
        out_shape=jax.ShapeDtypeStruct((PANELS, *rows.shape[1:]), rows.dtype),
        grid_spec=pltpu.PrefetchScalarGridSpec(
            num_scalar_prefetch=1,
            grid=(PANELS,),
            in_specs=[pl.BlockSpec(shape, lambda p, at: (slot_with(at, at[3 + blocks + p], blocks) // 2, 0, 0, 0))],
            out_specs=pl.BlockSpec(shape, lambda p, at: (p, 0, 0, 0)),
        ),
        compiler_params=pltpu.CompilerParams(vmem_limit_bytes=8 * MB),
        name="pivot_tiles",
    )(at, rows)


def features(coords_ref, block, left):
    x, y, z = [coords_ref[d, pl.ds(block, 1), :] for d in range(3)]
    norm = x * x + y * y + z * z
    low = norm & 63
    high = norm - low
    one, zero = jnp.ones_like(norm), jnp.zeros_like(norm)
    rows = [-2 * x, -2 * y, -2 * z, high, low, one, one] if left else [x, y, z, one, one, high, low]
    return jnp.concatenate([v.astype(f32) for v in rows + [zero]], 0).astype(bf16)


def green_kernel(tiles, at_ref, coords_ref, *refs):
    g_ref, fl_ref, fr_ref, sq_ref = refs[-4:]
    rows, _ = sq_ref.shape
    tile, chunk = pl.program_id(0) + tiles, pl.program_id(1)
    blocks = coords_ref.shape[1]
    own, grp, core = at_ref[3 + at_ref[0]], at_ref[1], at_ref[2]
    main = tile < 2
    left = jnp.where(main, own, at_ref[3 + blocks + core])
    right = jnp.where(main, grp * 2 + tile, at_ref[3 + blocks + jnp.maximum(tile - 2, 0)])

    @pl.when(chunk == 0)
    def _():
        fl_ref[...] = features(coords_ref, left, True)
        fr_ref[...] = features(coords_ref, right, False)

    at = pl.ds(pl.multiple_of(chunk * rows, rows), rows)
    sq_ref[...] = lax.dot_general(
        fl_ref[:, at], fr_ref[...], (((0,), (0,)), ((), ())), preferred_element_type=f32
    )

    def strip(i, _):
        r = pl.ds(pl.multiple_of(i * 8, 8), 8)
        re, im = half_green(sq_ref[r, :])
        g_ref[0, 0, r, :] = re.astype(bf16)
        g_ref[0, 1, r, :] = im.astype(bf16)
        return 0

    lax.fori_loop(0, rows // 8, strip, 0, unroll=STRIPS)

    @pl.when(left == right)
    def _():
        same = lax.broadcasted_iota(i32, (rows, rows), 0) == lax.broadcasted_iota(i32, (rows, rows), 1)
        for part, value in ((0, SELF_REAL), (1, SELF_IMAG)):
            block = g_ref[0, part, :, at].astype(f32)
            g_ref[0, part, :, at] = jnp.where(same, value, block).astype(bf16)


def green_tiles(at, coordinates, first, count, tiles, held):
    unk = coordinates.shape[2]
    rows = GREEN_ROWS
    return pl.pallas_call(
        functools.partial(green_kernel, first),
        out_shape=pltpu.HBM((tiles, 2, unk, unk), bf16),
        grid=(count, unk // rows),
        in_specs=[SMEM, pl.BlockSpec(coordinates.shape, lambda t, m: (0, 0, 0))]
        + [pl.BlockSpec(memory_space=pltpu.HBM)] * len(held),
        out_specs=pl.BlockSpec((1, 2, rows, unk), lambda t, m: (t + first, 0, m, 0)),
        scratch_shapes=[pltpu.VMEM((8, unk), bf16), pltpu.VMEM((8, unk), bf16), pltpu.VMEM((rows, unk), f32)],
        input_output_aliases={2: 0} if held else {},
        compiler_params=pltpu.CompilerParams(vmem_limit_bytes=10 * MB),
        cost_estimate=pl.CostEstimate(
            flops=count * unk * unk * 30, transcendentals=count * unk * unk, bytes_accessed=count * unk * unk * 4
        ),
    )(at, pltpu.with_memory_space_constraint(coordinates, pltpu.HBM), *held)


def coupling_kernel(pivot, panel_at, at_ref, g_ref, mine_ref, other_ref, *refs):
    if pivot:
        out_ref, lhs, stage, top, bottom, acc = refs
    else:
        pieces = refs[:4]
        out_ref, copies_ref, column_ref, lhs, stage, top, bottom, acc = refs[5:]
    tile, chunk = pl.program_id(0), pl.program_id(1)
    chunks = pl.num_programs(1)
    grp, core = at_ref[1], at_ref[2]
    groups, _, _, half, cols = mine_ref.shape
    rows = g_ref.shape[2]
    first = 2 if pivot else 0
    halves = ((mine_ref, core), (other_ref, 1 - core))

    def rows_of(g, part):
        return pl.ds(pl.multiple_of(g * 2 * half + part * half, half), half)

    @pl.when((tile == 0) & (chunk == 0))
    def _():
        if pivot:
            for g in range(groups):
                for src, part in halves:
                    r = rows_of(g, part)
                    stage[r, :cols] = src[g, first + core, 0]
                    stage[r, cols:] = src[g, first + core, 1]
        else:
            step = 0
            for piece in pieces:
                for k in range(piece.shape[0]):
                    r = pl.ds(pl.multiple_of((grp ^ step) * 2 * half, 2 * half), 2 * half)
                    stage[r, :cols] = piece[k, 0]
                    stage[r, cols:] = piece[k, 1]
                    step += 1
        lhs[...] = stage[...].T

    @pl.when(chunk == 0)
    def _():
        acc[...] = jnp.zeros_like(acc)
        for g in range(groups):
            for src, part in halves:
                r = rows_of(g, part)
                jr, ji = src[g, first + tile, 0], src[g, first + tile, 1]
                top[r, :cols] = jr
                top[r, cols:] = ji
                bottom[r, :cols] = -ji
                bottom[r, cols:] = jr

    y = jnp.dot(g_ref[0, 0], top[...], preferred_element_type=f32)
    y += jnp.dot(g_ref[0, 1], bottom[...], preferred_element_type=f32)
    y_hi = y.astype(bf16)
    y_lo = (y - y_hi.astype(f32)).astype(bf16)
    left = lhs[:, pl.ds(pl.multiple_of(chunk * rows, rows), rows)]
    acc[...] += jnp.dot(left, y_hi, preferred_element_type=f32) + jnp.dot(left, y_lo, preferred_element_type=f32)

    @pl.when(chunk == chunks - 1)
    def _():
        both = (2.0 * (acc[:cols, :cols] + acc[cols:, cols:]), 2.0 * (acc[:cols, cols:] - acc[cols:, :cols]))
        for part, value in enumerate(both):
            out_ref[part] = value
            if not pivot:
                for k in range(copies_ref.shape[0]):
                    copies_ref[k, part] = value.astype(bf16)
                for p in range(PANELS):
                    here = at_ref[panel_at + p] == grp * 2 + tile

                    @pl.when(here | (tile == 0))
                    def _():
                        column_ref[p, part] = value.astype(bf16)


def couplings(at, blocks, green, mine, other, pieces, after, pivot):
    _, _, unk, _ = green.shape
    cols = mine.shape[4]
    tiles = 2
    first = 2 if pivot else 0
    rows = COUPLE_ROWS
    copies = 8
    whole = lambda x: pl.BlockSpec(x.shape, lambda t, m: (0,) * x.ndim)
    out_shape = [jax.ShapeDtypeStruct((2, cols, tiles * cols), f32)]
    out_specs = [pl.BlockSpec((2, cols, cols), lambda t, m: (0, 0, t))]
    if not pivot:
        out_shape.append(jax.ShapeDtypeStruct((copies, 2, cols, tiles * cols), bf16))
        out_specs.append(pl.BlockSpec((copies, 2, cols, cols), lambda t, m: (0, 0, 0, t)))
        out_shape.append(jax.ShapeDtypeStruct((PANELS, 2, cols, cols), bf16))
        out_specs.append(pl.BlockSpec((PANELS, 2, cols, cols), lambda t, m: (0, 0, 0, 0)))
    return pl.pallas_call(
        functools.partial(coupling_kernel, pivot, 3 + blocks),
        out_shape=out_shape,
        grid=(tiles, unk // rows),
        in_specs=[SMEM, pl.BlockSpec((1, 2, rows, unk), lambda t, m: (t + first, 0, m, 0))]
        + [whole(x) for x in (mine, other, *pieces)]
        + [pl.BlockSpec(memory_space=pl.ANY)] * len(after),
        out_specs=out_specs,
        scratch_shapes=[
            pltpu.VMEM((2 * cols, unk), bf16),
            pltpu.VMEM((unk, 2 * cols), bf16),
            pltpu.VMEM((unk, 2 * cols), bf16),
            pltpu.VMEM((unk, 2 * cols), bf16),
            pltpu.VMEM((2 * cols, 2 * cols), f32),
        ],
        compiler_params=pltpu.CompilerParams(vmem_limit_bytes=20 * MB),
        cost_estimate=pl.CostEstimate(
            flops=tiles * unk * unk * 2048, transcendentals=0, bytes_accessed=tiles * unk * unk * 4
        ),
    )(at, pltpu.with_memory_space_constraint(green, pltpu.HBM), mine, other, *pieces, *after)


WIDE = 128
PANEL = 32


def small_exchange(ar, ai, sub):
    ar, ai = list(ar), list(ai)
    for s in range(8):
        row = lambda x: jnp.broadcast_to(x[s : s + 1], x.shape)
        pr, pi = row(ar[s]), row(ai[s])
        scale = 1.0 / (pr * pr + pi * pi)
        qr, qi = pr * scale, pi * scale
        br, bi = ar[s], ai[s]
        for m in range(8):
            if m == s:
                vr, vi = -qr, qi
                xr, xi = br * qr + bi * qi, bi * qr - br * qi
            else:
                cr, ci = row(ar[m]), row(ai[m])
                wr, wi = br * cr - bi * ci, br * ci + bi * cr
                vr, vi = cr * qr + ci * qi, ci * qr - cr * qi
                xr, xi = ar[m] - (wr * qr + wi * qi), ai[m] - (wi * qr - wr * qi)
            ar[m], ai[m] = jnp.where(sub == s, -vr, xr), jnp.where(sub == s, -vi, xi)
    return ar, ai


def times(ar, ai, xr, xi, spread):
    nr = ni = None
    for m in range(8):
        cr, ci = spread(xr[m : m + 1]), spread(xi[m : m + 1])
        r, i = ar[m] * cr - ai[m] * ci, ar[m] * ci + ai[m] * cr
        nr, ni = (r, i) if nr is None else (nr + r, ni + i)
    return nr, ni


def inverse_kernel(kb, at_ref, first_ref, second_ref, re_ref, im_ref, rhs_ref):
    if kb == 0:
        core = at_ref[2]
        rows = first_ref.shape[1]
        for src, part in ((first_ref, core), (second_ref, 1 - core)):
            r = pl.ds(pl.multiple_of(part * rows, rows), rows)
            for h in range(2):
                re_ref[h, r, :] = src[0][:, h * WIDE : (h + 1) * WIDE]
                im_ref[h, r, :] = src[1][:, h * WIDE : (h + 1) * WIDE]
    else:
        re_ref[...] = first_ref[...]
        im_ref[...] = second_ref[...]
    rhs_ref[...] = jnp.zeros_like(rhs_ref)
    lane = lax.broadcasted_iota(i32, (8, WIDE), 1)
    sub = lax.broadcasted_iota(i32, (8, WIDE), 0)
    spread = lambda x: jnp.broadcast_to(x, (8, WIDE))
    groups = PANEL // 8

    order = (kb, 1 - kb)
    for t in range(WIDE // PANEL):
        r = slice(kb * WIDE + t * PANEL, kb * WIDE + (t + 1) * PANEL)
        block = [(re_ref[h, r, :], im_ref[h, r, :]) for h in order]
        tr = [[b[0][8 * g : 8 * g + 8] for g in range(groups)] for b in block]
        ti = [[b[1][8 * g : 8 * g + 8] for g in range(groups)] for b in block]
        for gs in range(groups):
            first = t * PANEL + 8 * gs
            ar = [[spread(x[:, first + m : first + m + 1]) for m in range(8)] for x in tr[0]]
            ai = [[spread(x[:, first + m : first + m + 1]) for m in range(8)] for x in ti[0]]
            dr, di = small_exchange(ar[gs], ai[gs], sub)
            within = (lane >= first) & (lane < first + 8)
            unit = jnp.where(lane == sub + first, -1.0, 0.0)
            xr = [jnp.where(within, unit, tr[0][gs]), tr[1][gs]]
            xi = [jnp.where(within, 0.0, ti[0][gs]), ti[1][gs]]
            for h in range(2):
                nr, ni = times(dr, di, xr[h], xi[h], spread)
                tr[h][gs], ti[h][gs] = -nr, -ni
            for g in range(groups):
                if g == gs:
                    continue
                for h in range(2):
                    nr, ni = times(ar[g], ai[g], tr[h][gs], ti[h][gs], spread)
                    yr, yi = tr[h][g], ti[h][g]
                    if h == 0:
                        yr, yi = jnp.where(within, 0.0, yr), jnp.where(within, 0.0, yi)
                    tr[h][g], ti[h][g] = yr + nr, yi + ni
        pr = jnp.concatenate([jnp.concatenate(tr[h], 0) for h in range(2)], 1)
        pi = jnp.concatenate([jnp.concatenate(ti[h], 0) for h in range(2)], 1)
        top, low = slice(t * PANEL, (t + 1) * PANEL), slice(WIDE + t * PANEL, WIDE + (t + 1) * PANEL)
        rhs_ref[top, :] = jnp.concatenate([pr, pi], 1)
        rhs_ref[low, :] = jnp.concatenate([-pi, pr], 1)
        old = jnp.concatenate([re_ref[kb], im_ref[kb]], 1)
        upd = jnp.dot(old, rhs_ref[...], precision=lax.Precision.HIGHEST, preferred_element_type=f32)
        rhs_ref[top, :] = jnp.zeros((PANEL, 4 * WIDE), f32)
        rhs_ref[low, :] = jnp.zeros((PANEL, 4 * WIDE), f32)
        wide_lane = lax.broadcasted_iota(i32, upd[:, :WIDE].shape, 1)
        gone = (wide_lane >= t * PANEL) & (wide_lane < (t + 1) * PANEL)
        re_ref[kb] = jnp.where(gone, 0.0, re_ref[kb]) + upd[:, :WIDE]
        im_ref[kb] = jnp.where(gone, 0.0, im_ref[kb]) + upd[:, 2 * WIDE : 3 * WIDE]
        re_ref[1 - kb] += upd[:, WIDE : 2 * WIDE]
        im_ref[1 - kb] += upd[:, 3 * WIDE :]
        for n, h in enumerate(order):
            re_ref[h, r, :] = pr[:, n * WIDE : (n + 1) * WIDE]
            im_ref[h, r, :] = pi[:, n * WIDE : (n + 1) * WIDE]


def pivot_exchange(kb, at, first, second):
    order = PANELS * WIDE
    part = jax.ShapeDtypeStruct((2, order, WIDE), f32)
    return pl.pallas_call(
        functools.partial(inverse_kernel, kb),
        out_shape=(part, part),
        in_specs=[SMEM, VMEM, VMEM],
        out_specs=(VMEM, VMEM),
        scratch_shapes=[pltpu.VMEM((2 * WIDE, 4 * WIDE), f32)],
        compiler_params=pltpu.CompilerParams(vmem_limit_bytes=12 * MB),
        cost_estimate=pl.CostEstimate(flops=int(6e9), transcendentals=0, bytes_accessed=1 << 20),
    )(at, first, second)


def split3(x):
    hi = x.astype(bf16)
    rest = x - hi.astype(f32)
    mid = rest.astype(bf16)
    low = (rest - mid.astype(f32)).astype(bf16)
    return hi, mid, low


def schur_kernel(blocks, at, re_ref, im_ref, mine_ref, other_ref, c_ref, r_ref, out_ref):
    core = at[2]
    funcs = mine_ref.shape[2]
    b = []
    for p in range(PANELS):
        local = slot_with(at, at[3 + blocks + p], blocks) % 2 == core
        b.append([jnp.where(local, mine_ref[p, k].astype(f32), other_ref[p, k].astype(f32)).astype(bf16) for k in range(2)])
    br = jnp.concatenate([b[p][0] for p in range(PANELS)], 0)
    bi = jnp.concatenate([b[p][1] for p in range(PANELS)], 0)
    right = jnp.concatenate([jnp.concatenate([br, bi], 1), jnp.concatenate([-bi, br], 1)], 0)
    w = jnp.zeros((PANELS * funcs, right.shape[1]), f32)
    for x in split3(jnp.concatenate([re_ref[0], re_ref[1], im_ref[0], im_ref[1]], 1)):
        w += jnp.dot(x, right, preferred_element_type=f32)
    cols = w.shape[1] // 2
    w_hi = w.astype(bf16)
    w_lo = (w - w_hi.astype(f32)).astype(bf16)
    cr = jnp.concatenate([c_ref[0, 0], c_ref[1, 0]], 1)
    ci = jnp.concatenate([c_ref[0, 1], c_ref[1, 1]], 1)
    left = jnp.concatenate([cr, ci], 0)
    prod = jnp.dot(left, w_hi, preferred_element_type=f32) + jnp.dot(left, w_lo, preferred_element_type=f32)
    rows = cr.shape[0]
    out_ref[0] = r_ref[0] - (prod[:rows, :cols] - prod[rows:, cols:])
    out_ref[1] = r_ref[1] - (prod[:rows, cols:] + prod[rows:, :cols])


def schur_tile(at, blocks, re, im, mine, other, column, reduced):
    return pl.pallas_call(
        functools.partial(schur_kernel, blocks),
        out_shape=jax.ShapeDtypeStruct(reduced.shape, f32),
        in_specs=[SMEM] + [VMEM] * 6,
        out_specs=VMEM,
        compiler_params=pltpu.CompilerParams(vmem_limit_bytes=12 * MB),
        name="schur",
    )(at, re, im, mine, other, column, reduced)


def on_device(inverse, excite, coordinates, block_of_slot, panel_order):
    blk_size, grp_size = lax.axis_size("blk"), lax.axis_size("grp")
    blocks = block_of_slot.shape[0]
    slot, grp = lax.axis_index("blk").astype(i32), lax.axis_index("grp").astype(i32)
    core = slot % 2
    slabs = blocks // grp_size
    swap = [(i, i ^ 1) for i in range(blk_size)]
    same_core = [list(range(c, blk_size, 2)) for c in range(2)]
    at = jnp.concatenate([jnp.stack([slot, grp, core]), block_of_slot, panel_order])

    def spread(x, axis, groups=None):
        return lax.all_to_all(x, axis, split_axis=0, concat_axis=0, tiled=True, axis_index_groups=groups)

    pivots = panel_order[:PANELS]

    own, halves = basis_rows(inverse, excite, blk_size)
    sliced = spread(halves, "blk")

    pieces, held, bit = [own], own, 1
    while bit < grp_size:
        pieces.append(lax.ppermute(held, "grp", [(g, g ^ bit) for g in range(grp_size)]))
        bit *= 2
        if bit < grp_size:
            held = jnp.concatenate([held, pieces[-1]], 0)

    tiles = slabs + PANELS
    green = green_tiles(at, coordinates, 0, 1, tiles, [])
    green = green_tiles(at, coordinates, 2, PANELS, tiles, [green])
    green = green_tiles(at, coordinates, 1, 1, tiles, [green])

    picked = gathered(at, sliced, grp_size, slabs)
    mine = spread(picked, "grp")
    other = lax.ppermute(mine, "blk", swap)

    (pivot_rows,) = couplings(at, blocks, green, mine, other, [], [], True)
    pivot_other = lax.ppermute(pivot_rows, "blk", swap)
    reduced, copies, column = couplings(at, blocks, green, mine, other, pieces, [pivot_rows], False)

    rows = spread(copies, "blk", same_core)
    column_at = pivots // slabs
    bit = 1
    while bit < grp_size:
        came = lax.ppermute(column, "grp", [(g, g ^ bit) for g in range(grp_size)])
        take = ((grp ^ column_at) & bit) != 0
        column = jnp.where(take[:, None, None, None], came, column)
        bit *= 2
    row_mine = pivot_tiles(at, rows, blocks)
    row_other = lax.ppermute(row_mine, "blk", swap)
    re, im = pivot_exchange(0, at, pivot_rows, pivot_other)
    re, im = pivot_exchange(1, at, re, im)
    schur = schur_tile(at, blocks, re, im, row_mine, row_other, column, reduced)
    return (reduced, schur)


def solution(mesh):
    placed = (P(None, "blk", "grp", None), P(None, "blk", None, None), P(), P(), P())
    return jax.shard_map(
        on_device,
        mesh=mesh,
        in_specs=placed,
        out_specs=(P(None, "blk", "grp"), P(None, "blk", "grp")),
        check_vma=False,
    )
```

```python
import functools

import jax
import jax.numpy as jnp
import numpy as np
from jax import lax
from jax.experimental import pallas as pl
from jax.experimental.pallas import tpu as pltpu
from jax.sharding import PartitionSpec as P


PANELS = 2
bf16 = jnp.bfloat16
f32 = jnp.float32
i32 = jnp.int32

SELF_REAL = 6.0
SELF_IMAG = -1.5
TURNS = 1.3 / (2 * np.pi)
SHIFT = float(1.5 * 2**23)
SIN = (4.44288283, -7.30824115, 3.60628896, -0.8457636, 0.10920575)
COS = (-1.4142135, 6.97885099, -5.73946117, 1.88356298, -0.31069819)
VMEM = pl.BlockSpec(memory_space=pltpu.VMEM)
SMEM = pl.BlockSpec(memory_space=pltpu.SMEM)
MB = 1 << 20
COUPLE_ROWS = 1024
STRIPS = 8


def horner(coefs, g):
    r = coefs[-1]
    for k in coefs[-2::-1]:
        r = r * g + k
    return r


def half_green(sq):
    inv_r = lax.rsqrt(sq)
    turns = (sq * inv_r) * TURNS
    f = turns - ((turns + SHIFT) - SHIFT)
    g = f * f
    s = horner(SIN, g) * f
    c = horner(COS, g)
    scaled = s * inv_r
    return inv_r - s * scaled, c * scaled


def basis_kernel(inv_ref, exc_ref, own_ref, halves_ref):
    er, ei = exc_ref[0, 0], exc_ref[1, 0]
    j = jnp.dot(inv_ref[0, 0], jnp.concatenate([er, ei], 1), preferred_element_type=f32)
    j += jnp.dot(inv_ref[1, 0], jnp.concatenate([-ei, er], 1), preferred_element_type=f32)
    cols, half = j.shape[1] // 2, j.shape[0] // 2
    jb = j.astype(bf16)
    for part in range(2):
        own_ref[0, part] = jb[:, part * cols : (part + 1) * cols]
        for k in range(halves_ref.shape[0]):
            halves_ref[k, part] = jb[(k % 2) * half : (k % 2 + 1) * half, part * cols : (part + 1) * cols]


def basis_rows(inverse, excite, devices):
    rows, cols = inverse.shape[2], excite.shape[3]
    return pl.pallas_call(
        basis_kernel,
        out_shape=(
            jax.ShapeDtypeStruct((1, 2, rows, cols), bf16),
            jax.ShapeDtypeStruct((devices, 2, rows // 2, cols), bf16),
        ),
        grid=(1,),
        in_specs=[pl.BlockSpec(x.shape, lambda i: (0, 0, 0, 0)) for x in (inverse, excite)],
        out_specs=(VMEM, VMEM),
        compiler_params=pltpu.CompilerParams(vmem_limit_bytes=8 * MB),
        name="basis",
    )(*[pltpu.with_memory_space_constraint(x, pltpu.HBM) for x in (inverse, excite)])


def slot_with(at, block, blocks):
    slot = 0
    for s in range(blocks):
        slot = slot + jnp.where(at[3 + s] == block, s, 0)
    return slot


def gather_kernel(at_ref, rows_ref, out_ref, slot_ref):
    blocks = rows_ref.shape[0]
    for s in range(blocks):
        slot_ref[at_ref[3 + s]] = s
    groups, entries = out_ref.shape[:2]
    slabs = entries - PANELS
    for p in range(PANELS):
        value = rows_ref[slot_ref[at_ref[3 + blocks + p]]]
        for g in range(groups):
            out_ref[g, slabs + p] = value
    for g in range(groups):
        for e in range(slabs):
            out_ref[g, e] = rows_ref[slot_ref[g * slabs + e]]


def gathered(at, rows, groups, slabs):
    return pl.pallas_call(
        gather_kernel,
        out_shape=jax.ShapeDtypeStruct((groups, slabs + PANELS, *rows.shape[1:]), rows.dtype),
        in_specs=[SMEM, VMEM],
        out_specs=VMEM,
        scratch_shapes=[pltpu.SMEM((rows.shape[0],), i32)],
        compiler_params=pltpu.CompilerParams(vmem_limit_bytes=8 * MB),
        name="gathered",
    )(at, rows)


def pick_kernel(at_ref, row_ref, out_ref):
    out_ref[...] = row_ref[...]


def pivot_tiles(at, rows, blocks):
    shape = (1, *rows.shape[1:])
    return pl.pallas_call(
        pick_kernel,
        out_shape=jax.ShapeDtypeStruct((PANELS, *rows.shape[1:]), rows.dtype),
        grid_spec=pltpu.PrefetchScalarGridSpec(
            num_scalar_prefetch=1,
            grid=(PANELS,),
            in_specs=[pl.BlockSpec(shape, lambda p, at: (slot_with(at, at[3 + blocks + p], blocks) // 2, 0, 0, 0))],
            out_specs=pl.BlockSpec(shape, lambda p, at: (p, 0, 0, 0)),
        ),
        compiler_params=pltpu.CompilerParams(vmem_limit_bytes=8 * MB),
        name="pivot_tiles",
    )(at, rows)


def features(coords_ref, block, left):
    x, y, z = [coords_ref[d, pl.ds(block, 1), :] for d in range(3)]
    norm = x * x + y * y + z * z
    low = norm & 63
    high = norm - low
    one, zero = jnp.ones_like(norm), jnp.zeros_like(norm)
    rows = [-2 * x, -2 * y, -2 * z, high, low, one, one] if left else [x, y, z, one, one, high, low]
    return jnp.concatenate([v.astype(f32) for v in rows + [zero]], 0).astype(bf16)


def green_kernel(first, whole, carried, at_ref, coords_ref, *refs):
    sources, g_ref, targets = refs[:carried], refs[carried], refs[carried + 1 : 2 * carried + 1]
    fl_ref, fr_ref, sq_ref, *sems = refs[2 * carried + 1 :]
    copies = [pltpu.make_async_copy(a, b, sem) for a, b, sem in zip(sources, targets, sems)]
    for copy in copies:
        copy.start()
    rows, _ = sq_ref.shape
    local, chunk = pl.program_id(0), pl.program_id(1)
    tile = local + first
    blocks = coords_ref.shape[1]
    own, grp, core = at_ref[3 + at_ref[0]], at_ref[1], at_ref[2]
    main = tile < 2
    left = jnp.where(main, own, at_ref[3 + blocks + core])
    right = jnp.where(main, grp * 2 + tile, at_ref[3 + blocks + jnp.maximum(tile - 2, 0)])
    held, base = (local, chunk * rows) if whole else (0, 0)

    @pl.when(chunk == 0)
    def _():
        fl_ref[...] = features(coords_ref, left, True)
        fr_ref[...] = features(coords_ref, right, False)

    at = pl.ds(pl.multiple_of(chunk * rows, rows), rows)
    sq_ref[...] = lax.dot_general(
        fl_ref[:, at], fr_ref[...], (((0,), (0,)), ((), ())), preferred_element_type=f32
    )

    def strip(i, _):
        re, im = half_green(sq_ref[pl.ds(pl.multiple_of(i * 8, 8), 8), :])
        r = pl.ds(pl.multiple_of(base + i * 8, 8), 8)
        g_ref[held, 0, r, :] = re.astype(bf16)
        g_ref[held, 1, r, :] = im.astype(bf16)
        return 0

    lax.fori_loop(0, rows // 8, strip, 0, unroll=STRIPS)

    @pl.when(left == right)
    def _():
        size = 256
        same = lax.broadcasted_iota(i32, (size, size), 0) == lax.broadcasted_iota(i32, (size, size), 1)
        for k in range(rows // size):
            r = pl.ds(pl.multiple_of(base + k * size, size), size)
            c = pl.ds(pl.multiple_of(chunk * rows + k * size, size), size)
            for part, value in ((0, SELF_REAL), (1, SELF_IMAG)):
                block = g_ref[held, part, r, c].astype(f32)
                g_ref[held, part, r, c] = jnp.where(same, value, block).astype(bf16)

    for copy in copies:
        copy.wait()


def green_tiles(at, coordinates, first, count, whole, carry=()):
    unk = coordinates.shape[2]
    rows = unk if whole else unk // 2
    shape = (count, 2, unk, unk)
    return pl.pallas_call(
        functools.partial(green_kernel, first, whole, len(carry)),
        out_shape=[(pltpu.VMEM if whole else pltpu.HBM)(shape, bf16)] + [pltpu.VMEM(x.shape, x.dtype) for x in carry],
        grid=(count, unk // rows),
        in_specs=[SMEM, pl.BlockSpec(coordinates.shape, lambda t, m: (0, 0, 0))]
        + [pl.BlockSpec(memory_space=pltpu.HBM)] * len(carry),
        out_specs=[VMEM if whole else pl.BlockSpec((1, 2, rows, unk), lambda t, m: (t, 0, m, 0))] + [VMEM] * len(carry),
        scratch_shapes=[pltpu.VMEM((8, unk), bf16), pltpu.VMEM((8, unk), bf16), pltpu.VMEM((rows, unk), f32)]
        + [pltpu.SemaphoreType.DMA] * len(carry),
        compiler_params=pltpu.CompilerParams(vmem_limit_bytes=10 * MB),
        cost_estimate=pl.CostEstimate(
            flops=count * unk * unk * 30, transcendentals=count * unk * unk, bytes_accessed=count * unk * unk * 4
        ),
    )(at, *[pltpu.with_memory_space_constraint(x, pltpu.HBM) for x in (coordinates, *carry)])


def add_tile(y, left, acc):
    y_hi = y.astype(bf16)
    y_lo = (y - y_hi.astype(f32)).astype(bf16)
    acc[...] += jnp.dot(left, y_hi, preferred_element_type=f32) + jnp.dot(left, y_lo, preferred_element_type=f32)


def coupling_kernel(pivot, panel_at, greens, at_ref, *refs):
    g_refs, refs = refs[:greens], refs[greens:]
    mine_ref, other_ref, refs = refs[0], refs[1], refs[2:]
    if pivot:
        out_ref, lhs, stage, top, bottom, acc = refs
    else:
        pieces = refs[:4]
        out_ref, copies_ref, column_ref, lhs, stage, top, bottom, acc = refs[5:]
    tile, chunk = pl.program_id(0), pl.program_id(1)
    chunks = pl.num_programs(1)
    grp, core = at_ref[1], at_ref[2]
    groups, _, _, half, cols = mine_ref.shape
    rows = COUPLE_ROWS
    first = 2 if pivot else 0
    halves = ((mine_ref, core), (other_ref, 1 - core))

    def rows_of(g, part):
        return pl.ds(pl.multiple_of(g * 2 * half + part * half, half), half)

    @pl.when((tile == 0) & (chunk == 0))
    def _():
        if pivot:
            for g in range(groups):
                for src, part in halves:
                    r = rows_of(g, part)
                    stage[r, :cols] = src[g, first + core, 0]
                    stage[r, cols:] = src[g, first + core, 1]
        else:
            step = 0
            for piece in pieces:
                for k in range(piece.shape[0]):
                    r = pl.ds(pl.multiple_of((grp ^ step) * 2 * half, 2 * half), 2 * half)
                    stage[r, :cols] = piece[k, 0]
                    stage[r, cols:] = piece[k, 1]
                    step += 1
        lhs[...] = stage[...].T

    @pl.when(chunk == 0)
    def _():
        acc[...] = jnp.zeros_like(acc)
        for g in range(groups):
            for src, part in halves:
                r = rows_of(g, part)
                jr, ji = src[g, first + tile, 0], src[g, first + tile, 1]
                top[r, :cols] = jr
                top[r, cols:] = ji
                bottom[r, :cols] = -ji
                bottom[r, cols:] = jr

    at_rows = pl.ds(pl.multiple_of(chunk * rows, rows), rows)

    def product(g_ref, held):
        y = jnp.dot(g_ref[held, 0, at_rows, :], top[...], preferred_element_type=f32)
        return y + jnp.dot(g_ref[held, 1, at_rows, :], bottom[...], preferred_element_type=f32)

    if greens == 1:
        add_tile(product(g_refs[0], tile), lhs[:, at_rows], acc)
    else:
        for n, g_ref in enumerate(g_refs):

            @pl.when(tile == n)
            def _():
                add_tile(product(g_ref, 0), lhs[:, at_rows], acc)

    @pl.when(chunk == chunks - 1)
    def _():
        both = (2.0 * (acc[:cols, :cols] + acc[cols:, cols:]), 2.0 * (acc[:cols, cols:] - acc[cols:, :cols]))
        for part, value in enumerate(both):
            out_ref[part] = value
            if not pivot:
                for k in range(copies_ref.shape[0]):
                    copies_ref[k, part] = value.astype(bf16)
                for p in range(PANELS):
                    here = at_ref[panel_at + p] == grp * 2 + tile

                    @pl.when(here | (tile == 0))
                    def _():
                        column_ref[p, part] = value.astype(bf16)


def couplings(at, blocks, greens, mine, other, pieces, after, pivot):
    unk = greens[0].shape[2]
    cols = mine.shape[4]
    tiles = 2
    rows = COUPLE_ROWS
    copies = 8
    whole = lambda x: pl.BlockSpec(x.shape, lambda t, m: (0,) * x.ndim)
    out_shape = [jax.ShapeDtypeStruct((2, cols, tiles * cols), f32)]
    out_specs = [pl.BlockSpec((2, cols, cols), lambda t, m: (0, 0, t))]
    if not pivot:
        out_shape.append(jax.ShapeDtypeStruct((copies, 2, cols, tiles * cols), bf16))
        out_specs.append(pl.BlockSpec((copies, 2, cols, cols), lambda t, m: (0, 0, 0, t)))
        out_shape.append(jax.ShapeDtypeStruct((PANELS, 2, cols, cols), bf16))
        out_specs.append(pl.BlockSpec((PANELS, 2, cols, cols), lambda t, m: (0, 0, 0, 0)))
    return pl.pallas_call(
        functools.partial(coupling_kernel, pivot, 3 + blocks, len(greens)),
        out_shape=out_shape,
        grid=(tiles, unk // rows),
        in_specs=[SMEM] + [VMEM] * len(greens)
        + [whole(x) for x in (mine, other, *pieces)]
        + [pl.BlockSpec(memory_space=pl.ANY)] * len(after),
        out_specs=out_specs,
        scratch_shapes=[
            pltpu.VMEM((2 * cols, unk), bf16),
            pltpu.VMEM((unk, 2 * cols), bf16),
            pltpu.VMEM((unk, 2 * cols), bf16),
            pltpu.VMEM((unk, 2 * cols), bf16),
            pltpu.VMEM((2 * cols, 2 * cols), f32),
        ],
        compiler_params=pltpu.CompilerParams(vmem_limit_bytes=16 * MB),
        cost_estimate=pl.CostEstimate(
            flops=tiles * unk * unk * 2048, transcendentals=0, bytes_accessed=tiles * unk * unk * 4
        ),
    )(at, *greens, mine, other, *pieces, *after)


WIDE = 128
PANEL = 32


def small_exchange(ar, ai, sub):
    ar, ai = list(ar), list(ai)
    for s in range(8):
        row = lambda x: jnp.broadcast_to(x[s : s + 1], x.shape)
        pr, pi = row(ar[s]), row(ai[s])
        scale = 1.0 / (pr * pr + pi * pi)
        qr, qi = pr * scale, pi * scale
        br, bi = ar[s], ai[s]
        for m in range(8):
            if m == s:
                vr, vi = -qr, qi
                xr, xi = br * qr + bi * qi, bi * qr - br * qi
            else:
                cr, ci = row(ar[m]), row(ai[m])
                wr, wi = br * cr - bi * ci, br * ci + bi * cr
                vr, vi = cr * qr + ci * qi, ci * qr - cr * qi
                xr, xi = ar[m] - (wr * qr + wi * qi), ai[m] - (wi * qr - wr * qi)
            ar[m], ai[m] = jnp.where(sub == s, -vr, xr), jnp.where(sub == s, -vi, xi)
    return ar, ai


def times(ar, ai, xr, xi, spread):
    nr = ni = None
    for m in range(8):
        cr, ci = spread(xr[m : m + 1]), spread(xi[m : m + 1])
        r, i = ar[m] * cr - ai[m] * ci, ar[m] * ci + ai[m] * cr
        nr, ni = (r, i) if nr is None else (nr + r, ni + i)
    return nr, ni


def inverse_kernel(kb, at_ref, first_ref, second_ref, re_ref, im_ref, rhs_ref):
    if kb == 0:
        core = at_ref[2]
        rows = first_ref.shape[1]
        for src, part in ((first_ref, core), (second_ref, 1 - core)):
            r = pl.ds(pl.multiple_of(part * rows, rows), rows)
            for h in range(2):
                re_ref[h, r, :] = src[0][:, h * WIDE : (h + 1) * WIDE]
                im_ref[h, r, :] = src[1][:, h * WIDE : (h + 1) * WIDE]
    else:
        re_ref[...] = first_ref[...]
        im_ref[...] = second_ref[...]
    rhs_ref[...] = jnp.zeros_like(rhs_ref)
    lane = lax.broadcasted_iota(i32, (8, WIDE), 1)
    sub = lax.broadcasted_iota(i32, (8, WIDE), 0)
    spread = lambda x: jnp.broadcast_to(x, (8, WIDE))
    groups = PANEL // 8

    order = (kb, 1 - kb)
    for t in range(WIDE // PANEL):
        r = slice(kb * WIDE + t * PANEL, kb * WIDE + (t + 1) * PANEL)
        block = [(re_ref[h, r, :], im_ref[h, r, :]) for h in order]
        tr = [[b[0][8 * g : 8 * g + 8] for g in range(groups)] for b in block]
        ti = [[b[1][8 * g : 8 * g + 8] for g in range(groups)] for b in block]
        for gs in range(groups):
            first = t * PANEL + 8 * gs
            ar = [[spread(x[:, first + m : first + m + 1]) for m in range(8)] for x in tr[0]]
            ai = [[spread(x[:, first + m : first + m + 1]) for m in range(8)] for x in ti[0]]
            dr, di = small_exchange(ar[gs], ai[gs], sub)
            within = (lane >= first) & (lane < first + 8)
            unit = jnp.where(lane == sub + first, -1.0, 0.0)
            xr = [jnp.where(within, unit, tr[0][gs]), tr[1][gs]]
            xi = [jnp.where(within, 0.0, ti[0][gs]), ti[1][gs]]
            for h in range(2):
                nr, ni = times(dr, di, xr[h], xi[h], spread)
                tr[h][gs], ti[h][gs] = -nr, -ni
            for g in range(groups):
                if g == gs:
                    continue
                for h in range(2):
                    nr, ni = times(ar[g], ai[g], tr[h][gs], ti[h][gs], spread)
                    yr, yi = tr[h][g], ti[h][g]
                    if h == 0:
                        yr, yi = jnp.where(within, 0.0, yr), jnp.where(within, 0.0, yi)
                    tr[h][g], ti[h][g] = yr + nr, yi + ni
        pr = jnp.concatenate([jnp.concatenate(tr[h], 0) for h in range(2)], 1)
        pi = jnp.concatenate([jnp.concatenate(ti[h], 0) for h in range(2)], 1)
        top, low = slice(t * PANEL, (t + 1) * PANEL), slice(WIDE + t * PANEL, WIDE + (t + 1) * PANEL)
        rhs_ref[top, :] = jnp.concatenate([pr, pi], 1)
        rhs_ref[low, :] = jnp.concatenate([-pi, pr], 1)
        old = jnp.concatenate([re_ref[kb], im_ref[kb]], 1)
        upd = jnp.dot(old, rhs_ref[...], precision=lax.Precision.HIGHEST, preferred_element_type=f32)
        rhs_ref[top, :] = jnp.zeros((PANEL, 4 * WIDE), f32)
        rhs_ref[low, :] = jnp.zeros((PANEL, 4 * WIDE), f32)
        wide_lane = lax.broadcasted_iota(i32, upd[:, :WIDE].shape, 1)
        gone = (wide_lane >= t * PANEL) & (wide_lane < (t + 1) * PANEL)
        re_ref[kb] = jnp.where(gone, 0.0, re_ref[kb]) + upd[:, :WIDE]
        im_ref[kb] = jnp.where(gone, 0.0, im_ref[kb]) + upd[:, 2 * WIDE : 3 * WIDE]
        re_ref[1 - kb] += upd[:, WIDE : 2 * WIDE]
        im_ref[1 - kb] += upd[:, 3 * WIDE :]
        for n, h in enumerate(order):
            re_ref[h, r, :] = pr[:, n * WIDE : (n + 1) * WIDE]
            im_ref[h, r, :] = pi[:, n * WIDE : (n + 1) * WIDE]


def pivot_exchange(kb, at, first, second):
    order = PANELS * WIDE
    part = jax.ShapeDtypeStruct((2, order, WIDE), f32)
    return pl.pallas_call(
        functools.partial(inverse_kernel, kb),
        out_shape=(part, part),
        in_specs=[SMEM, VMEM, VMEM],
        out_specs=(VMEM, VMEM),
        scratch_shapes=[pltpu.VMEM((2 * WIDE, 4 * WIDE), f32)],
        compiler_params=pltpu.CompilerParams(vmem_limit_bytes=12 * MB),
        cost_estimate=pl.CostEstimate(flops=int(6e9), transcendentals=0, bytes_accessed=1 << 20),
    )(at, first, second)


def split3(x):
    hi = x.astype(bf16)
    rest = x - hi.astype(f32)
    mid = rest.astype(bf16)
    low = (rest - mid.astype(f32)).astype(bf16)
    return hi, mid, low


def schur_kernel(blocks, at, re_ref, im_ref, mine_ref, other_ref, c_ref, r_ref, out_ref):
    core = at[2]
    funcs = mine_ref.shape[2]
    b = []
    for p in range(PANELS):
        local = slot_with(at, at[3 + blocks + p], blocks) % 2 == core
        b.append([jnp.where(local, mine_ref[p, k].astype(f32), other_ref[p, k].astype(f32)).astype(bf16) for k in range(2)])
    br = jnp.concatenate([b[p][0] for p in range(PANELS)], 0)
    bi = jnp.concatenate([b[p][1] for p in range(PANELS)], 0)
    right = jnp.concatenate([jnp.concatenate([br, bi], 1), jnp.concatenate([-bi, br], 1)], 0)
    w = jnp.zeros((PANELS * funcs, right.shape[1]), f32)
    for x in split3(jnp.concatenate([re_ref[0], re_ref[1], im_ref[0], im_ref[1]], 1)):
        w += jnp.dot(x, right, preferred_element_type=f32)
    cols = w.shape[1] // 2
    w_hi = w.astype(bf16)
    w_lo = (w - w_hi.astype(f32)).astype(bf16)
    cr = jnp.concatenate([c_ref[0, 0], c_ref[1, 0]], 1)
    ci = jnp.concatenate([c_ref[0, 1], c_ref[1, 1]], 1)
    left = jnp.concatenate([cr, ci], 0)
    prod = jnp.dot(left, w_hi, preferred_element_type=f32) + jnp.dot(left, w_lo, preferred_element_type=f32)
    rows = cr.shape[0]
    out_ref[0] = r_ref[0] - (prod[:rows, :cols] - prod[rows:, cols:])
    out_ref[1] = r_ref[1] - (prod[:rows, cols:] + prod[rows:, :cols])


def schur_tile(at, blocks, re, im, mine, other, column, reduced):
    return pl.pallas_call(
        functools.partial(schur_kernel, blocks),
        out_shape=jax.ShapeDtypeStruct(reduced.shape, f32),
        in_specs=[SMEM] + [VMEM] * 6,
        out_specs=VMEM,
        compiler_params=pltpu.CompilerParams(vmem_limit_bytes=12 * MB),
        name="schur",
    )(at, re, im, mine, other, column, reduced)


def on_device(inverse, excite, coordinates, block_of_slot, panel_order):
    blk_size, grp_size = lax.axis_size("blk"), lax.axis_size("grp")
    blocks = block_of_slot.shape[0]
    slot, grp = lax.axis_index("blk").astype(i32), lax.axis_index("grp").astype(i32)
    core = slot % 2
    slabs = blocks // grp_size
    swap = [(i, i ^ 1) for i in range(blk_size)]
    same_core = [list(range(c, blk_size, 2)) for c in range(2)]
    at = jnp.concatenate([jnp.stack([slot, grp, core]), block_of_slot, panel_order])

    def spread(x, axis, groups=None):
        return lax.all_to_all(x, axis, split_axis=0, concat_axis=0, tiled=True, axis_index_groups=groups)

    pivots = panel_order[:PANELS]

    own, halves = basis_rows(inverse, excite, blk_size)
    sliced = spread(halves, "blk")

    pieces, held, bit = [own], own, 1
    while bit < grp_size:
        pieces.append(lax.ppermute(held, "grp", [(g, g ^ bit) for g in range(grp_size)]))
        bit *= 2
        if bit < grp_size:
            held = jnp.concatenate([held, pieces[-1]], 0)

    (green_first,) = green_tiles(at, coordinates, 0, 1, False)
    (green_pivot,) = green_tiles(at, coordinates, 2, PANELS, False)
    green_second, green_first, green_pivot = green_tiles(at, coordinates, 1, 1, True, [green_first, green_pivot])

    picked = gathered(at, sliced, grp_size, slabs)
    mine = spread(picked, "grp")
    other = lax.ppermute(mine, "blk", swap)

    (pivot_rows,) = couplings(at, blocks, [green_pivot], mine, other, [], [], True)
    pivot_other = lax.ppermute(pivot_rows, "blk", swap)
    reduced, copies, column = couplings(at, blocks, [green_first, green_second], mine, other, pieces, [pivot_rows], False)

    rows = spread(copies, "blk", same_core)
    column_at = pivots // slabs
    bit = 1
    while bit < grp_size:
        came = lax.ppermute(column, "grp", [(g, g ^ bit) for g in range(grp_size)])
        take = ((grp ^ column_at) & bit) != 0
        column = jnp.where(take[:, None, None, None], came, column)
        bit *= 2
    row_mine = pivot_tiles(at, rows, blocks)
    row_other = lax.ppermute(row_mine, "blk", swap)
    re, im = pivot_exchange(0, at, pivot_rows, pivot_other)
    re, im = pivot_exchange(1, at, re, im)
    schur = schur_tile(at, blocks, re, im, row_mine, row_other, column, reduced)
    return (reduced, schur)


def solution(mesh):
    placed = (P(None, "blk", "grp", None), P(None, "blk", None, None), P(), P(), P())
    return jax.shard_map(
        on_device,
        mesh=mesh,
        in_specs=placed,
        out_specs=(P(None, "blk", "grp"), P(None, "blk", "grp")),
        check_vma=False,
    )
```

```python
import functools

import jax
import jax.numpy as jnp
import numpy as np
from jax import lax
from jax.experimental import pallas as pl
from jax.experimental.pallas import tpu as pltpu
from jax.sharding import PartitionSpec as P


PANELS = 2
bf16 = jnp.bfloat16
f32 = jnp.float32
i32 = jnp.int32

SELF_REAL = 6.0
SELF_IMAG = -1.5
TURNS = 1.3 / (2 * np.pi)
SHIFT = float(1.5 * 2**23)
SIN = (4.44288283, -7.30824115, 3.60628896, -0.8457636, 0.10920575)
COS = (-1.4142135, 6.97885099, -5.73946117, 1.88356298, -0.31069819)
VMEM = pl.BlockSpec(memory_space=pltpu.VMEM)
SMEM = pl.BlockSpec(memory_space=pltpu.SMEM)
MB = 1 << 20
COUPLE_ROWS = 1024
STRIPS = 8


def horner(coefs, g):
    r = coefs[-1]
    for k in coefs[-2::-1]:
        r = r * g + k
    return r


def half_green(sq):
    inv_r = lax.rsqrt(sq)
    turns = (sq * inv_r) * TURNS
    f = turns - ((turns + SHIFT) - SHIFT)
    g = f * f
    s = horner(SIN, g) * f
    c = horner(COS, g)
    scaled = s * inv_r
    return inv_r - s * scaled, c * scaled


def basis_kernel(inv_ref, exc_ref, own_ref, halves_ref):
    er, ei = exc_ref[0, 0], exc_ref[1, 0]
    j = jnp.dot(inv_ref[0, 0], jnp.concatenate([er, ei], 1), preferred_element_type=f32)
    j += jnp.dot(inv_ref[1, 0], jnp.concatenate([-ei, er], 1), preferred_element_type=f32)
    cols, half = j.shape[1] // 2, j.shape[0] // 2
    jb = j.astype(bf16)
    for part in range(2):
        own_ref[0, part] = jb[:, part * cols : (part + 1) * cols]
        for k in range(halves_ref.shape[0]):
            halves_ref[k, part] = jb[(k % 2) * half : (k % 2 + 1) * half, part * cols : (part + 1) * cols]


def basis_rows(inverse, excite, devices):
    rows, cols = inverse.shape[2], excite.shape[3]
    return pl.pallas_call(
        basis_kernel,
        out_shape=(
            jax.ShapeDtypeStruct((1, 2, rows, cols), bf16),
            jax.ShapeDtypeStruct((devices, 2, rows // 2, cols), bf16),
        ),
        grid=(1,),
        in_specs=[pl.BlockSpec(x.shape, lambda i: (0, 0, 0, 0)) for x in (inverse, excite)],
        out_specs=(VMEM, VMEM),
        compiler_params=pltpu.CompilerParams(vmem_limit_bytes=8 * MB),
        name="basis",
    )(*[pltpu.with_memory_space_constraint(x, pltpu.HBM) for x in (inverse, excite)])


def slot_with(at, block, blocks):
    slot = 0
    for s in range(blocks):
        slot = slot + jnp.where(at[3 + s] == block, s, 0)
    return slot


def gather_kernel(at_ref, rows_ref, out_ref, slot_ref):
    blocks = rows_ref.shape[0]
    for s in range(blocks):
        slot_ref[at_ref[3 + s]] = s
    groups, entries = out_ref.shape[:2]
    slabs = entries - PANELS
    for p in range(PANELS):
        value = rows_ref[slot_ref[at_ref[3 + blocks + p]]]
        for g in range(groups):
            out_ref[g, slabs + p] = value
    for g in range(groups):
        for e in range(slabs):
            out_ref[g, e] = rows_ref[slot_ref[g * slabs + e]]


def gathered(at, rows, groups, slabs):
    return pl.pallas_call(
        gather_kernel,
        out_shape=jax.ShapeDtypeStruct((groups, slabs + PANELS, *rows.shape[1:]), rows.dtype),
        in_specs=[SMEM, VMEM],
        out_specs=VMEM,
        scratch_shapes=[pltpu.SMEM((rows.shape[0],), i32)],
        compiler_params=pltpu.CompilerParams(vmem_limit_bytes=8 * MB),
        name="gathered",
    )(at, rows)


def pick_kernel(at_ref, row_ref, out_ref):
    out_ref[...] = row_ref[...]


def pivot_tiles(at, rows, blocks):
    shape = (1, *rows.shape[1:])
    return pl.pallas_call(
        pick_kernel,
        out_shape=jax.ShapeDtypeStruct((PANELS, *rows.shape[1:]), rows.dtype),
        grid_spec=pltpu.PrefetchScalarGridSpec(
            num_scalar_prefetch=1,
            grid=(PANELS,),
            in_specs=[pl.BlockSpec(shape, lambda p, at: (slot_with(at, at[3 + blocks + p], blocks) // 2, 0, 0, 0))],
            out_specs=pl.BlockSpec(shape, lambda p, at: (p, 0, 0, 0)),
        ),
        compiler_params=pltpu.CompilerParams(vmem_limit_bytes=8 * MB),
        name="pivot_tiles",
    )(at, rows)


def features(coords_ref, block, left):
    x, y, z = [coords_ref[d, pl.ds(block, 1), :] for d in range(3)]
    norm = x * x + y * y + z * z
    low = norm & 63
    high = norm - low
    one, zero = jnp.ones_like(norm), jnp.zeros_like(norm)
    rows = [-2 * x, -2 * y, -2 * z, high, low, one, one] if left else [x, y, z, one, one, high, low]
    return jnp.concatenate([v.astype(f32) for v in rows + [zero]], 0).astype(bf16)


def green_kernel(first, whole, carried, at_ref, coords_ref, *refs):
    sources, g_ref, targets = refs[:carried], refs[carried], refs[carried + 1 : 2 * carried + 1]
    fl_ref, fr_ref, sq_ref, *sems = refs[2 * carried + 1 :]
    copies = [pltpu.make_async_copy(a, b, sem) for a, b, sem in zip(sources, targets, sems)]
    for copy in copies:
        copy.start()
    rows, _ = sq_ref.shape
    local, chunk = pl.program_id(0), pl.program_id(1)
    tile = local + first
    blocks = coords_ref.shape[1]
    own, grp, core = at_ref[3 + at_ref[0]], at_ref[1], at_ref[2]
    main = tile < 2
    left = jnp.where(main, own, at_ref[3 + blocks + core])
    right = jnp.where(main, grp * 2 + tile, at_ref[3 + blocks + jnp.maximum(tile - 2, 0)])
    held, base = (local, chunk * rows) if whole else (0, 0)

    @pl.when(chunk == 0)
    def _():
        fl_ref[...] = features(coords_ref, left, True)
        fr_ref[...] = features(coords_ref, right, False)

    at = pl.ds(pl.multiple_of(chunk * rows, rows), rows)
    sq_ref[...] = lax.dot_general(
        fl_ref[:, at], fr_ref[...], (((0,), (0,)), ((), ())), preferred_element_type=f32
    )

    def strip(i, _):
        re, im = half_green(sq_ref[pl.ds(pl.multiple_of(i * 8, 8), 8), :])
        r = pl.ds(pl.multiple_of(base + i * 8, 8), 8)
        g_ref[held, 0, r, :] = re.astype(bf16)
        g_ref[held, 1, r, :] = im.astype(bf16)
        return 0

    lax.fori_loop(0, rows // 8, strip, 0, unroll=STRIPS)

    @pl.when(left == right)
    def _():
        size = 256
        same = lax.broadcasted_iota(i32, (size, size), 0) == lax.broadcasted_iota(i32, (size, size), 1)
        for k in range(rows // size):
            r = pl.ds(pl.multiple_of(base + k * size, size), size)
            c = pl.ds(pl.multiple_of(chunk * rows + k * size, size), size)
            for part, value in ((0, SELF_REAL), (1, SELF_IMAG)):
                block = g_ref[held, part, r, c].astype(f32)
                g_ref[held, part, r, c] = jnp.where(same, value, block).astype(bf16)

    for copy in copies:
        copy.wait()


def green_tiles(at, coordinates, first, count, whole, carry=()):
    unk = coordinates.shape[2]
    rows = unk if whole else unk // 2
    shape = (count, 2, unk, unk)
    return pl.pallas_call(
        functools.partial(green_kernel, first, whole, len(carry)),
        out_shape=[(pltpu.VMEM if whole else pltpu.HBM)(shape, bf16)] + [pltpu.VMEM(x.shape, x.dtype) for x in carry],
        grid=(count, unk // rows),
        in_specs=[SMEM, pl.BlockSpec(coordinates.shape, lambda t, m: (0, 0, 0))]
        + [pl.BlockSpec(memory_space=pltpu.HBM)] * len(carry),
        out_specs=[VMEM if whole else pl.BlockSpec((1, 2, rows, unk), lambda t, m: (t, 0, m, 0))] + [VMEM] * len(carry),
        scratch_shapes=[pltpu.VMEM((8, unk), bf16), pltpu.VMEM((8, unk), bf16), pltpu.VMEM((rows, unk), f32)]
        + [pltpu.SemaphoreType.DMA] * len(carry),
        compiler_params=pltpu.CompilerParams(vmem_limit_bytes=10 * MB),
        cost_estimate=pl.CostEstimate(
            flops=count * unk * unk * 30, transcendentals=count * unk * unk, bytes_accessed=count * unk * unk * 4
        ),
    )(at, *[pltpu.with_memory_space_constraint(x, pltpu.HBM) for x in (coordinates, *carry)])


def add_tile(y, left, acc):
    y_hi = y.astype(bf16)
    y_lo = (y - y_hi.astype(f32)).astype(bf16)
    acc[...] += jnp.dot(left, y_hi, preferred_element_type=f32) + jnp.dot(left, y_lo, preferred_element_type=f32)


def coupling_kernel(pivot, panel_at, greens, at_ref, *refs):
    g_refs, refs = refs[:greens], refs[greens:]
    mine_ref, other_ref, refs = refs[0], refs[1], refs[2:]
    if pivot:
        out_ref, lhs, stage, top, bottom, acc = refs
    else:
        pieces = refs[:4]
        out_ref, copies_ref, column_ref, lhs, stage, top, bottom, acc = refs[5:]
    tile, chunk = pl.program_id(0), pl.program_id(1)
    chunks = pl.num_programs(1)
    grp, core = at_ref[1], at_ref[2]
    groups, _, _, half, cols = mine_ref.shape
    rows = COUPLE_ROWS
    first = 2 if pivot else 0
    halves = ((mine_ref, core), (other_ref, 1 - core))

    def rows_of(g, part):
        return pl.ds(pl.multiple_of(g * 2 * half + part * half, half), half)

    @pl.when((tile == 0) & (chunk == 0))
    def _():
        if pivot:
            for g in range(groups):
                for src, part in halves:
                    r = rows_of(g, part)
                    stage[r, :cols] = src[g, first + core, 0]
                    stage[r, cols:] = src[g, first + core, 1]
        else:
            step = 0
            for piece in pieces:
                for k in range(piece.shape[0]):
                    r = pl.ds(pl.multiple_of((grp ^ step) * 2 * half, 2 * half), 2 * half)
                    stage[r, :cols] = piece[k, 0]
                    stage[r, cols:] = piece[k, 1]
                    step += 1
        lhs[...] = stage[...].T

    @pl.when(chunk == 0)
    def _():
        acc[...] = jnp.zeros_like(acc)
        for g in range(groups):
            for src, part in halves:
                r = rows_of(g, part)
                jr, ji = src[g, first + tile, 0], src[g, first + tile, 1]
                top[r, :cols] = jr
                top[r, cols:] = ji
                bottom[r, :cols] = -ji
                bottom[r, cols:] = jr

    at_rows = pl.ds(pl.multiple_of(chunk * rows, rows), rows)

    def product(g_ref, held):
        y = jnp.dot(g_ref[held, 0, at_rows, :], top[...], preferred_element_type=f32)
        return y + jnp.dot(g_ref[held, 1, at_rows, :], bottom[...], preferred_element_type=f32)

    if greens == 1:
        add_tile(product(g_refs[0], tile), lhs[:, at_rows], acc)
    else:
        for n, g_ref in enumerate(g_refs):

            @pl.when(tile == n)
            def _():
                add_tile(product(g_ref, 0), lhs[:, at_rows], acc)

    @pl.when(chunk == chunks - 1)
    def _():
        both = (2.0 * (acc[:cols, :cols] + acc[cols:, cols:]), 2.0 * (acc[:cols, cols:] - acc[cols:, :cols]))
        for part, value in enumerate(both):
            out_ref[part] = value
            if not pivot:
                for k in range(copies_ref.shape[0]):
                    copies_ref[k, part] = value.astype(bf16)
                for p in range(PANELS):
                    here = at_ref[panel_at + p] == grp * 2 + tile

                    @pl.when(here | (tile == 0))
                    def _():
                        column_ref[p, part] = value.astype(bf16)


def couplings(at, blocks, greens, mine, other, pieces, after, pivot):
    unk = greens[0].shape[2]
    cols = mine.shape[4]
    tiles = 2
    rows = COUPLE_ROWS
    copies = 8
    whole = lambda x: pl.BlockSpec(x.shape, lambda t, m: (0,) * x.ndim)
    out_shape = [jax.ShapeDtypeStruct((2, cols, tiles * cols), f32)]
    out_specs = [pl.BlockSpec((2, cols, cols), lambda t, m: (0, 0, t))]
    if not pivot:
        out_shape.append(jax.ShapeDtypeStruct((copies, 2, cols, tiles * cols), bf16))
        out_specs.append(pl.BlockSpec((copies, 2, cols, cols), lambda t, m: (0, 0, 0, t)))
        out_shape.append(jax.ShapeDtypeStruct((PANELS, 2, cols, cols), bf16))
        out_specs.append(pl.BlockSpec((PANELS, 2, cols, cols), lambda t, m: (0, 0, 0, 0)))
    return pl.pallas_call(
        functools.partial(coupling_kernel, pivot, 3 + blocks, len(greens)),
        out_shape=out_shape,
        grid=(tiles, unk // rows),
        in_specs=[SMEM] + [VMEM] * len(greens)
        + [whole(x) for x in (mine, other, *pieces)]
        + [pl.BlockSpec(memory_space=pl.ANY)] * len(after),
        out_specs=out_specs,
        scratch_shapes=[
            pltpu.VMEM((2 * cols, unk), bf16),
            pltpu.VMEM((unk, 2 * cols), bf16),
            pltpu.VMEM((unk, 2 * cols), bf16),
            pltpu.VMEM((unk, 2 * cols), bf16),
            pltpu.VMEM((2 * cols, 2 * cols), f32),
        ],
        compiler_params=pltpu.CompilerParams(vmem_limit_bytes=16 * MB),
        cost_estimate=pl.CostEstimate(
            flops=tiles * unk * unk * 2048, transcendentals=0, bytes_accessed=tiles * unk * unk * 4
        ),
    )(at, *greens, mine, other, *pieces, *after)


WIDE = 128
PANEL = 64


def small_exchange(ar, ai, sub):
    ar, ai = list(ar), list(ai)
    for s in range(8):
        row = lambda x: jnp.broadcast_to(x[s : s + 1], x.shape)
        pr, pi = row(ar[s]), row(ai[s])
        scale = 1.0 / (pr * pr + pi * pi)
        qr, qi = pr * scale, pi * scale
        br, bi = ar[s], ai[s]
        for m in range(8):
            if m == s:
                vr, vi = -qr, qi
                xr, xi = br * qr + bi * qi, bi * qr - br * qi
            else:
                cr, ci = row(ar[m]), row(ai[m])
                vr, vi = cr * qr + ci * qi, ci * qr - cr * qi
                xr, xi = ar[m] - (br * vr - bi * vi), ai[m] - (br * vi + bi * vr)
            ar[m], ai[m] = jnp.where(sub == s, -vr, xr), jnp.where(sub == s, -vi, xi)
    return ar, ai


def times(ar, ai, xr, xi, spread):
    nr = ni = None
    for m in range(8):
        cr, ci = spread(xr[m : m + 1]), spread(xi[m : m + 1])
        r, i = ar[m] * cr - ai[m] * ci, ar[m] * ci + ai[m] * cr
        nr, ni = (r, i) if nr is None else (nr + r, ni + i)
    return nr, ni


def inverse_kernel(kb, at_ref, first_ref, second_ref, re_ref, im_ref, rhs_ref):
    if kb == 0:
        core = at_ref[2]
        rows = first_ref.shape[1]
        for src, part in ((first_ref, core), (second_ref, 1 - core)):
            r = pl.ds(pl.multiple_of(part * rows, rows), rows)
            for h in range(2):
                re_ref[h, r, :] = src[0][:, h * WIDE : (h + 1) * WIDE]
                im_ref[h, r, :] = src[1][:, h * WIDE : (h + 1) * WIDE]
    else:
        re_ref[...] = first_ref[...]
        im_ref[...] = second_ref[...]
    rhs_ref[...] = jnp.zeros_like(rhs_ref)
    lane = lax.broadcasted_iota(i32, (8, WIDE), 1)
    sub = lax.broadcasted_iota(i32, (8, WIDE), 0)
    spread = lambda x: jnp.broadcast_to(x, (8, WIDE))
    groups = PANEL // 8

    order = (kb, 1 - kb)
    for t in range(WIDE // PANEL):
        r = slice(kb * WIDE + t * PANEL, kb * WIDE + (t + 1) * PANEL)
        block = [(re_ref[h, r, :], im_ref[h, r, :]) for h in order]
        tr = [[b[0][8 * g : 8 * g + 8] for g in range(groups)] for b in block]
        ti = [[b[1][8 * g : 8 * g + 8] for g in range(groups)] for b in block]
        for gs in range(groups):
            first = t * PANEL + 8 * gs
            ar = [[spread(x[:, first + m : first + m + 1]) for m in range(8)] for x in tr[0]]
            ai = [[spread(x[:, first + m : first + m + 1]) for m in range(8)] for x in ti[0]]
            dr, di = small_exchange(ar[gs], ai[gs], sub)
            within = (lane >= first) & (lane < first + 8)
            unit = jnp.where(lane == sub + first, -1.0, 0.0)
            xr = [jnp.where(within, unit, tr[0][gs]), tr[1][gs]]
            xi = [jnp.where(within, 0.0, ti[0][gs]), ti[1][gs]]
            for h in range(2):
                nr, ni = times(dr, di, xr[h], xi[h], spread)
                tr[h][gs], ti[h][gs] = -nr, -ni
            for g in range(groups):
                if g == gs:
                    continue
                for h in range(2):
                    nr, ni = times(ar[g], ai[g], tr[h][gs], ti[h][gs], spread)
                    yr, yi = tr[h][g], ti[h][g]
                    if h == 0:
                        yr, yi = jnp.where(within, 0.0, yr), jnp.where(within, 0.0, yi)
                    tr[h][g], ti[h][g] = yr + nr, yi + ni
        pr = jnp.concatenate([jnp.concatenate(tr[h], 0) for h in range(2)], 1)
        pi = jnp.concatenate([jnp.concatenate(ti[h], 0) for h in range(2)], 1)
        top, low = slice(t * PANEL, (t + 1) * PANEL), slice(WIDE + t * PANEL, WIDE + (t + 1) * PANEL)
        rhs_ref[top, :] = jnp.concatenate([pr, pi], 1)
        rhs_ref[low, :] = jnp.concatenate([-pi, pr], 1)
        old = jnp.concatenate([re_ref[kb], im_ref[kb]], 1)
        upd = jnp.dot(old, rhs_ref[...], precision=lax.Precision.HIGHEST, preferred_element_type=f32)
        rhs_ref[top, :] = jnp.zeros((PANEL, 4 * WIDE), f32)
        rhs_ref[low, :] = jnp.zeros((PANEL, 4 * WIDE), f32)
        wide_lane = lax.broadcasted_iota(i32, upd[:, :WIDE].shape, 1)
        gone = (wide_lane >= t * PANEL) & (wide_lane < (t + 1) * PANEL)
        re_ref[kb] = jnp.where(gone, 0.0, re_ref[kb]) + upd[:, :WIDE]
        im_ref[kb] = jnp.where(gone, 0.0, im_ref[kb]) + upd[:, 2 * WIDE : 3 * WIDE]
        re_ref[1 - kb] += upd[:, WIDE : 2 * WIDE]
        im_ref[1 - kb] += upd[:, 3 * WIDE :]
        for n, h in enumerate(order):
            re_ref[h, r, :] = pr[:, n * WIDE : (n + 1) * WIDE]
            im_ref[h, r, :] = pi[:, n * WIDE : (n + 1) * WIDE]


def pivot_exchange(kb, at, first, second):
    order = PANELS * WIDE
    part = jax.ShapeDtypeStruct((2, order, WIDE), f32)
    return pl.pallas_call(
        functools.partial(inverse_kernel, kb),
        out_shape=(part, part),
        in_specs=[SMEM, VMEM, VMEM],
        out_specs=(VMEM, VMEM),
        scratch_shapes=[pltpu.VMEM((2 * WIDE, 4 * WIDE), f32)],
        compiler_params=pltpu.CompilerParams(vmem_limit_bytes=12 * MB),
        cost_estimate=pl.CostEstimate(flops=int(6e9), transcendentals=0, bytes_accessed=1 << 20),
    )(at, first, second)


def split3(x):
    hi = x.astype(bf16)
    rest = x - hi.astype(f32)
    mid = rest.astype(bf16)
    low = (rest - mid.astype(f32)).astype(bf16)
    return hi, mid, low


def real_form(re, im):
    return jnp.concatenate([jnp.concatenate([re, im], 1), jnp.concatenate([-im, re], 1)], 0)


def column_kernel(re_ref, im_ref, c_ref, x_ref):
    left = jnp.concatenate([c_ref[0, 0], c_ref[1, 0], c_ref[0, 1], c_ref[1, 1]], 1)
    re = split3(jnp.concatenate([re_ref[0], re_ref[1]], 1))
    im = split3(jnp.concatenate([im_ref[0], im_ref[1]], 1))
    x = jnp.zeros(x_ref.shape, f32)
    for r, i in zip(re, im):
        x += jnp.dot(left, real_form(r, i), preferred_element_type=f32)
    x_ref[...] = x


def pivot_columns(re, im, column):
    rows = column.shape[2]
    return pl.pallas_call(
        column_kernel,
        out_shape=jax.ShapeDtypeStruct((rows, 2 * PANELS * WIDE), f32),
        in_specs=[VMEM] * 3,
        out_specs=VMEM,
        compiler_params=pltpu.CompilerParams(vmem_limit_bytes=12 * MB),
        cost_estimate=pl.CostEstimate(flops=int(2e9), transcendentals=0, bytes_accessed=1 << 20),
        name="pivot_columns",
    )(re, im, column)


def schur_kernel(blocks, at, x_ref, mine_ref, other_ref, r_ref, out_ref):
    core = at[2]
    b = []
    for p in range(PANELS):
        local = slot_with(at, at[3 + blocks + p], blocks) % 2 == core
        b.append([jnp.where(local, mine_ref[p, k].astype(f32), other_ref[p, k].astype(f32)).astype(bf16) for k in range(2)])
    br = jnp.concatenate([b[p][0] for p in range(PANELS)], 0)
    bi = jnp.concatenate([b[p][1] for p in range(PANELS)], 0)
    right = real_form(br, bi)
    x = x_ref[...]
    x_hi = x.astype(bf16)
    x_lo = (x - x_hi.astype(f32)).astype(bf16)
    prod = jnp.dot(x_hi, right, preferred_element_type=f32) + jnp.dot(x_lo, right, preferred_element_type=f32)
    cols = prod.shape[1] // 2
    out_ref[0] = r_ref[0] - prod[:, :cols]
    out_ref[1] = r_ref[1] - prod[:, cols:]


def schur_tile(at, blocks, x, mine, other, reduced):
    return pl.pallas_call(
        functools.partial(schur_kernel, blocks),
        out_shape=jax.ShapeDtypeStruct(reduced.shape, f32),
        in_specs=[SMEM] + [VMEM] * 4,
        out_specs=VMEM,
        compiler_params=pltpu.CompilerParams(vmem_limit_bytes=12 * MB),
        name="schur",
    )(at, x, mine, other, reduced)


def on_device(inverse, excite, coordinates, block_of_slot, panel_order):
    blk_size, grp_size = lax.axis_size("blk"), lax.axis_size("grp")
    blocks = block_of_slot.shape[0]
    slot, grp = lax.axis_index("blk").astype(i32), lax.axis_index("grp").astype(i32)
    core = slot % 2
    slabs = blocks // grp_size
    swap = [(i, i ^ 1) for i in range(blk_size)]
    same_core = [list(range(c, blk_size, 2)) for c in range(2)]
    at = jnp.concatenate([jnp.stack([slot, grp, core]), block_of_slot, panel_order])

    def spread(x, axis, groups=None):
        return lax.all_to_all(x, axis, split_axis=0, concat_axis=0, tiled=True, axis_index_groups=groups)

    pivots = panel_order[:PANELS]

    own, halves = basis_rows(inverse, excite, blk_size)
    sliced = spread(halves, "blk")

    pieces, held, bit = [own], own, 1
    while bit < grp_size:
        pieces.append(lax.ppermute(held, "grp", [(g, g ^ bit) for g in range(grp_size)]))
        bit *= 2
        if bit < grp_size:
            held = jnp.concatenate([held, pieces[-1]], 0)

    (green_first,) = green_tiles(at, coordinates, 0, 1, False)
    (green_pivot,) = green_tiles(at, coordinates, 2, PANELS, False)
    green_second, green_first, green_pivot = green_tiles(at, coordinates, 1, 1, True, [green_first, green_pivot])

    picked = gathered(at, sliced, grp_size, slabs)
    mine = spread(picked, "grp")
    other = lax.ppermute(mine, "blk", swap)

    (pivot_rows,) = couplings(at, blocks, [green_pivot], mine, other, [], [], True)
    pivot_other = lax.ppermute(pivot_rows, "blk", swap)
    reduced, copies, column = couplings(at, blocks, [green_first, green_second], mine, other, pieces, [pivot_rows], False)

    rows = spread(copies, "blk", same_core)
    column_at = pivots // slabs
    bit = 1
    while bit < grp_size:
        came = lax.ppermute(column, "grp", [(g, g ^ bit) for g in range(grp_size)])
        take = ((grp ^ column_at) & bit) != 0
        column = jnp.where(take[:, None, None, None], came, column)
        bit *= 2
    row_mine = pivot_tiles(at, rows, blocks)
    row_other = lax.ppermute(row_mine, "blk", swap)
    re, im = pivot_exchange(0, at, pivot_rows, pivot_other)
    re, im = pivot_exchange(1, at, re, im)
    x = pivot_columns(re, im, column)
    schur = schur_tile(at, blocks, x, row_mine, row_other, reduced)
    return (reduced, schur)


def solution(mesh):
    placed = (P(None, "blk", "grp", None), P(None, "blk", None, None), P(), P(), P())
    return jax.shard_map(
        on_device,
        mesh=mesh,
        in_specs=placed,
        out_specs=(P(None, "blk", "grp"), P(None, "blk", "grp")),
        check_vma=False,
    )
```

```python
import functools

import jax
import jax.numpy as jnp
import numpy as np
from jax import lax
from jax.experimental import pallas as pl
from jax.experimental.pallas import tpu as pltpu
from jax.sharding import PartitionSpec as P


PANELS = 2
bf16 = jnp.bfloat16
f32 = jnp.float32
i32 = jnp.int32

SELF_REAL = 6.0
SELF_IMAG = -1.5
TURNS = 1.3 / (2 * np.pi)
SHIFT = float(1.5 * 2**23)
SIN = (4.44288283, -7.30824115, 3.60628896, -0.8457636, 0.10920575)
COS = (-1.4142135, 6.97885099, -5.73946117, 1.88356298, -0.31069819)
VMEM = pl.BlockSpec(memory_space=pltpu.VMEM)
SMEM = pl.BlockSpec(memory_space=pltpu.SMEM)
MB = 1 << 20
COUPLE_ROWS = 1024
STRIPS = 8


def horner(coefs, g):
    r = coefs[-1]
    for k in coefs[-2::-1]:
        r = r * g + k
    return r


def half_green(sq):
    inv_r = lax.rsqrt(sq)
    turns = (sq * inv_r) * TURNS
    f = turns - ((turns + SHIFT) - SHIFT)
    g = f * f
    s = horner(SIN, g) * f
    c = horner(COS, g)
    scaled = s * inv_r
    return inv_r - s * scaled, c * scaled


def basis_kernel(inv_ref, exc_ref, own_ref, halves_ref):
    er, ei = exc_ref[0, 0], exc_ref[1, 0]
    j = jnp.dot(inv_ref[0, 0], jnp.concatenate([er, ei], 1), preferred_element_type=f32)
    j += jnp.dot(inv_ref[1, 0], jnp.concatenate([-ei, er], 1), preferred_element_type=f32)
    cols, half = j.shape[1] // 2, j.shape[0] // 2
    jb = j.astype(bf16)
    for part in range(2):
        own_ref[0, part] = jb[:, part * cols : (part + 1) * cols]
        for k in range(halves_ref.shape[0]):
            halves_ref[k, part] = jb[(k % 2) * half : (k % 2 + 1) * half, part * cols : (part + 1) * cols]


def basis_rows(inverse, excite, devices):
    rows, cols = inverse.shape[2], excite.shape[3]
    return pl.pallas_call(
        basis_kernel,
        out_shape=(
            jax.ShapeDtypeStruct((1, 2, rows, cols), bf16),
            jax.ShapeDtypeStruct((devices, 2, rows // 2, cols), bf16),
        ),
        grid=(1,),
        in_specs=[pl.BlockSpec(x.shape, lambda i: (0, 0, 0, 0)) for x in (inverse, excite)],
        out_specs=(VMEM, VMEM),
        compiler_params=pltpu.CompilerParams(vmem_limit_bytes=8 * MB),
        name="basis",
    )(*[pltpu.with_memory_space_constraint(x, pltpu.HBM) for x in (inverse, excite)])


def slot_with(at, block, blocks):
    slot = 0
    for s in range(blocks):
        slot = slot + jnp.where(at[3 + s] == block, s, 0)
    return slot


def gather_kernel(at_ref, rows_ref, out_ref, slot_ref, sems):
    blocks = rows_ref.shape[0]
    for s in range(blocks):
        slot_ref[at_ref[3 + s]] = s
    groups, entries = out_ref.shape[:2]
    slabs = entries - PANELS
    copies = []
    for g in range(groups):
        for e in range(entries):
            block = g * slabs + e if e < slabs else at_ref[3 + blocks + e - slabs]
            copy = pltpu.make_async_copy(rows_ref.at[slot_ref[block]], out_ref.at[g, e], sems.at[g, e])
            copy.start()
            copies.append(copy)
    for copy in copies:
        copy.wait()


def gathered(at, rows, groups, slabs):
    entries = slabs + PANELS
    return pl.pallas_call(
        gather_kernel,
        out_shape=pltpu.HBM((groups, entries, *rows.shape[1:]), rows.dtype),
        in_specs=[SMEM, VMEM],
        out_specs=pl.BlockSpec(memory_space=pltpu.HBM),
        scratch_shapes=[pltpu.SMEM((rows.shape[0],), i32), pltpu.SemaphoreType.DMA((groups, entries))],
        compiler_params=pltpu.CompilerParams(vmem_limit_bytes=8 * MB),
        name="gathered",
    )(at, rows)


def pick_kernel(at_ref, row_ref, out_ref):
    out_ref[...] = row_ref[...]


def pivot_tiles(at, rows, blocks):
    shape = (1, *rows.shape[1:])
    return pl.pallas_call(
        pick_kernel,
        out_shape=jax.ShapeDtypeStruct((PANELS, *rows.shape[1:]), rows.dtype),
        grid_spec=pltpu.PrefetchScalarGridSpec(
            num_scalar_prefetch=1,
            grid=(PANELS,),
            in_specs=[pl.BlockSpec(shape, lambda p, at: (slot_with(at, at[3 + blocks + p], blocks) // 2, 0, 0, 0))],
            out_specs=pl.BlockSpec(shape, lambda p, at: (p, 0, 0, 0)),
        ),
        compiler_params=pltpu.CompilerParams(vmem_limit_bytes=8 * MB),
        name="pivot_tiles",
    )(at, rows)


def features(coords_ref, block, left):
    x, y, z = [coords_ref[d, pl.ds(block, 1), :] for d in range(3)]
    norm = x * x + y * y + z * z
    low = norm & 63
    high = norm - low
    one, zero = jnp.ones_like(norm), jnp.zeros_like(norm)
    rows = [-2 * x, -2 * y, -2 * z, high, low, one, one] if left else [x, y, z, one, one, high, low]
    return jnp.concatenate([v.astype(f32) for v in rows + [zero]], 0).astype(bf16)


def green_kernel(first, whole, carried, at_ref, coords_ref, *refs):
    sources, g_ref, targets = refs[:carried], refs[carried], refs[carried + 1 : 2 * carried + 1]
    fl_ref, fr_ref, sq_ref, *sems = refs[2 * carried + 1 :]
    copies = [pltpu.make_async_copy(a, b, sem) for a, b, sem in zip(sources, targets, sems)]
    for copy in copies:
        copy.start()
    rows, _ = sq_ref.shape
    local, chunk = pl.program_id(0), pl.program_id(1)
    tile = local + first
    blocks = coords_ref.shape[1]
    own, grp, core = at_ref[3 + at_ref[0]], at_ref[1], at_ref[2]
    main = tile < 2
    left = jnp.where(main, own, at_ref[3 + blocks + core])
    right = jnp.where(main, grp * 2 + tile, at_ref[3 + blocks + jnp.maximum(tile - 2, 0)])
    held, base = (local, chunk * rows) if whole else (0, 0)

    @pl.when(chunk == 0)
    def _():
        fl_ref[...] = features(coords_ref, left, True)
        fr_ref[...] = features(coords_ref, right, False)

    at = pl.ds(pl.multiple_of(chunk * rows, rows), rows)
    sq_ref[...] = lax.dot_general(
        fl_ref[:, at], fr_ref[...], (((0,), (0,)), ((), ())), preferred_element_type=f32
    )

    def strip(i, _):
        re, im = half_green(sq_ref[pl.ds(pl.multiple_of(i * 8, 8), 8), :])
        r = pl.ds(pl.multiple_of(base + i * 8, 8), 8)
        g_ref[held, 0, r, :] = re.astype(bf16)
        g_ref[held, 1, r, :] = im.astype(bf16)
        return 0

    lax.fori_loop(0, rows // 8, strip, 0, unroll=STRIPS)

    @pl.when(left == right)
    def _():
        size = 256
        same = lax.broadcasted_iota(i32, (size, size), 0) == lax.broadcasted_iota(i32, (size, size), 1)
        for k in range(rows // size):
            r = pl.ds(pl.multiple_of(base + k * size, size), size)
            c = pl.ds(pl.multiple_of(chunk * rows + k * size, size), size)
            for part, value in ((0, SELF_REAL), (1, SELF_IMAG)):
                block = g_ref[held, part, r, c].astype(f32)
                g_ref[held, part, r, c] = jnp.where(same, value, block).astype(bf16)

    for copy in copies:
        copy.wait()


def green_tiles(at, coordinates, first, count, whole, carry=()):
    unk = coordinates.shape[2]
    rows = unk if whole else unk // 2
    shape = (count, 2, unk, unk)
    return pl.pallas_call(
        functools.partial(green_kernel, first, whole, len(carry)),
        out_shape=[(pltpu.VMEM if whole else pltpu.HBM)(shape, bf16)] + [pltpu.VMEM(x.shape, x.dtype) for x in carry],
        grid=(count, unk // rows),
        in_specs=[SMEM, pl.BlockSpec(coordinates.shape, lambda t, m: (0, 0, 0))]
        + [pl.BlockSpec(memory_space=pltpu.HBM)] * len(carry),
        out_specs=[VMEM if whole else pl.BlockSpec((1, 2, rows, unk), lambda t, m: (t, 0, m, 0))] + [VMEM] * len(carry),
        scratch_shapes=[pltpu.VMEM((8, unk), bf16), pltpu.VMEM((8, unk), bf16), pltpu.VMEM((rows, unk), f32)]
        + [pltpu.SemaphoreType.DMA] * len(carry),
        compiler_params=pltpu.CompilerParams(vmem_limit_bytes=10 * MB),
        cost_estimate=pl.CostEstimate(
            flops=count * unk * unk * 30, transcendentals=count * unk * unk, bytes_accessed=count * unk * unk * 4
        ),
    )(at, *[pltpu.with_memory_space_constraint(x, pltpu.HBM) for x in (coordinates, *carry)])


def add_tile(y, left, acc):
    y_hi = y.astype(bf16)
    y_lo = (y - y_hi.astype(f32)).astype(bf16)
    acc[...] += jnp.dot(left, y_hi, preferred_element_type=f32) + jnp.dot(left, y_lo, preferred_element_type=f32)


def coupling_kernel(pivot, panel_at, greens, bits, at_ref, *refs):
    g_refs, refs = refs[:greens], refs[greens:]
    mine_ref, other_ref, refs = refs[0], refs[1], refs[2:]
    if pivot:
        out_ref, lhs, stage, top, bottom, acc = refs
    else:
        count = 1 + len(bits)
        pieces = refs[:count]
        out_ref, copies_ref, column_ref, lhs, stage, top, bottom, acc = refs[count + 1 :]
    tile, chunk = pl.program_id(0), pl.program_id(1)
    chunks = pl.num_programs(1)
    grp, core = at_ref[1], at_ref[2]
    groups, _, _, half, cols = mine_ref.shape
    rows = COUPLE_ROWS
    first = 2 if pivot else 0
    halves = ((mine_ref, core), (other_ref, 1 - core))

    def rows_of(g, part):
        return pl.ds(pl.multiple_of(g * 2 * half + part * half, half), half)

    @pl.when((tile == 0) & (chunk == 0))
    def _():
        if pivot:
            for g in range(groups):
                for src, part in halves:
                    r = rows_of(g, part)
                    stage[r, :cols] = src[g, first + core, 0]
                    stage[r, cols:] = src[g, first + core, 1]
        else:
            away = [0]
            for bit in bits:
                away = away + [d ^ bit for d in away]
            for piece in pieces:
                for k in range(piece.shape[0]):
                    r = pl.ds(pl.multiple_of((grp ^ away.pop(0)) * 2 * half, 2 * half), 2 * half)
                    stage[r, :cols] = piece[k, 0]
                    stage[r, cols:] = piece[k, 1]
        lhs[...] = stage[...].T

    @pl.when(chunk == 0)
    def _():
        acc[...] = jnp.zeros_like(acc)
        for g in range(groups):
            for src, part in halves:
                r = rows_of(g, part)
                jr, ji = src[g, first + tile, 0], src[g, first + tile, 1]
                top[r, :cols] = jr
                top[r, cols:] = ji
                bottom[r, :cols] = -ji
                bottom[r, cols:] = jr

    at_rows = pl.ds(pl.multiple_of(chunk * rows, rows), rows)

    def product(g_ref, held):
        y = jnp.dot(g_ref[held, 0, at_rows, :], top[...], preferred_element_type=f32)
        return y + jnp.dot(g_ref[held, 1, at_rows, :], bottom[...], preferred_element_type=f32)

    if greens == 1:
        add_tile(product(g_refs[0], tile), lhs[:, at_rows], acc)
    else:
        for n, g_ref in enumerate(g_refs):

            @pl.when(tile == n)
            def _():
                add_tile(product(g_ref, 0), lhs[:, at_rows], acc)

    @pl.when(chunk == chunks - 1)
    def _():
        both = (2.0 * (acc[:cols, :cols] + acc[cols:, cols:]), 2.0 * (acc[:cols, cols:] - acc[cols:, :cols]))
        for part, value in enumerate(both):
            out_ref[part] = value
            if not pivot:
                for k in range(copies_ref.shape[0]):
                    copies_ref[k, part] = value.astype(bf16)
                for p in range(PANELS):
                    here = at_ref[panel_at + p] == grp * 2 + tile

                    @pl.when(here | (tile == 0))
                    def _():
                        column_ref[p, part] = value.astype(bf16)


def couplings(at, blocks, greens, mine, other, pieces, bits, after, pivot):
    unk = greens[0].shape[2]
    cols = mine.shape[4]
    tiles = 2
    rows = COUPLE_ROWS
    copies = 8
    whole = lambda x: pl.BlockSpec(x.shape, lambda t, m: (0,) * x.ndim)
    out_shape = [jax.ShapeDtypeStruct((2, cols, tiles * cols), f32)]
    out_specs = [pl.BlockSpec((2, cols, cols), lambda t, m: (0, 0, t))]
    if not pivot:
        out_shape.append(jax.ShapeDtypeStruct((copies, 2, cols, tiles * cols), bf16))
        out_specs.append(pl.BlockSpec((copies, 2, cols, cols), lambda t, m: (0, 0, 0, t)))
        out_shape.append(jax.ShapeDtypeStruct((PANELS, 2, cols, cols), bf16))
        out_specs.append(pl.BlockSpec((PANELS, 2, cols, cols), lambda t, m: (0, 0, 0, 0)))
    return pl.pallas_call(
        functools.partial(coupling_kernel, pivot, 3 + blocks, len(greens), bits),
        out_shape=out_shape,
        grid=(tiles, unk // rows),
        in_specs=[SMEM] + [VMEM] * len(greens)
        + [whole(x) for x in (mine, other, *pieces)]
        + [pl.BlockSpec(memory_space=pl.ANY)] * len(after),
        out_specs=out_specs,
        scratch_shapes=[
            pltpu.VMEM((2 * cols, unk), bf16),
            pltpu.VMEM((unk, 2 * cols), bf16),
            pltpu.VMEM((unk, 2 * cols), bf16),
            pltpu.VMEM((unk, 2 * cols), bf16),
            pltpu.VMEM((2 * cols, 2 * cols), f32),
        ],
        compiler_params=pltpu.CompilerParams(vmem_limit_bytes=16 * MB),
        cost_estimate=pl.CostEstimate(
            flops=tiles * unk * unk * 2048, transcendentals=0, bytes_accessed=tiles * unk * unk * 4
        ),
    )(at, *greens, mine, other, *pieces, *after)


WIDE = 128
PANEL = 64


def small_exchange(ar, ai, sub):
    ar, ai = list(ar), list(ai)
    for s in range(8):
        row = lambda x: jnp.broadcast_to(x[s : s + 1], x.shape)
        pr, pi = row(ar[s]), row(ai[s])
        scale = 1.0 / (pr * pr + pi * pi)
        qr, qi = pr * scale, pi * scale
        br, bi = ar[s], ai[s]
        for m in range(8):
            if m == s:
                vr, vi = -qr, qi
                xr, xi = br * qr + bi * qi, bi * qr - br * qi
            else:
                cr, ci = row(ar[m]), row(ai[m])
                vr, vi = cr * qr + ci * qi, ci * qr - cr * qi
                xr, xi = ar[m] - (br * vr - bi * vi), ai[m] - (br * vi + bi * vr)
            ar[m], ai[m] = jnp.where(sub == s, -vr, xr), jnp.where(sub == s, -vi, xi)
    return ar, ai


def times(ar, ai, xr, xi, spread):
    nr = ni = None
    for m in range(8):
        cr, ci = spread(xr[m : m + 1]), spread(xi[m : m + 1])
        r, i = ar[m] * cr - ai[m] * ci, ar[m] * ci + ai[m] * cr
        nr, ni = (r, i) if nr is None else (nr + r, ni + i)
    return nr, ni


def inverse_kernel(kb, at_ref, first_ref, second_ref, re_ref, im_ref, rhs_ref):
    if kb == 0:
        core = at_ref[2]
        rows = first_ref.shape[1]
        for src, part in ((first_ref, core), (second_ref, 1 - core)):
            r = pl.ds(pl.multiple_of(part * rows, rows), rows)
            for h in range(2):
                re_ref[h, r, :] = src[0][:, h * WIDE : (h + 1) * WIDE]
                im_ref[h, r, :] = src[1][:, h * WIDE : (h + 1) * WIDE]
    else:
        re_ref[...] = first_ref[...]
        im_ref[...] = second_ref[...]
    rhs_ref[...] = jnp.zeros_like(rhs_ref)
    lane = lax.broadcasted_iota(i32, (8, WIDE), 1)
    sub = lax.broadcasted_iota(i32, (8, WIDE), 0)
    spread = lambda x: jnp.broadcast_to(x, (8, WIDE))
    groups = PANEL // 8

    order = (kb, 1 - kb)
    for t in range(WIDE // PANEL):
        r = slice(kb * WIDE + t * PANEL, kb * WIDE + (t + 1) * PANEL)
        block = [(re_ref[h, r, :], im_ref[h, r, :]) for h in order]
        tr = [[b[0][8 * g : 8 * g + 8] for g in range(groups)] for b in block]
        ti = [[b[1][8 * g : 8 * g + 8] for g in range(groups)] for b in block]
        for gs in range(groups):
            first = t * PANEL + 8 * gs
            ar = [[spread(x[:, first + m : first + m + 1]) for m in range(8)] for x in tr[0]]
            ai = [[spread(x[:, first + m : first + m + 1]) for m in range(8)] for x in ti[0]]
            dr, di = small_exchange(ar[gs], ai[gs], sub)
            within = (lane >= first) & (lane < first + 8)
            unit = jnp.where(lane == sub + first, -1.0, 0.0)
            xr = [jnp.where(within, unit, tr[0][gs]), tr[1][gs]]
            xi = [jnp.where(within, 0.0, ti[0][gs]), ti[1][gs]]
            for h in range(2):
                nr, ni = times(dr, di, xr[h], xi[h], spread)
                tr[h][gs], ti[h][gs] = -nr, -ni
            for g in range(groups):
                if g == gs:
                    continue
                for h in range(2):
                    nr, ni = times(ar[g], ai[g], tr[h][gs], ti[h][gs], spread)
                    yr, yi = tr[h][g], ti[h][g]
                    if h == 0:
                        yr, yi = jnp.where(within, 0.0, yr), jnp.where(within, 0.0, yi)
                    tr[h][g], ti[h][g] = yr + nr, yi + ni
        pr = jnp.concatenate([jnp.concatenate(tr[h], 0) for h in range(2)], 1)
        pi = jnp.concatenate([jnp.concatenate(ti[h], 0) for h in range(2)], 1)
        top, low = slice(t * PANEL, (t + 1) * PANEL), slice(WIDE + t * PANEL, WIDE + (t + 1) * PANEL)
        rhs_ref[top, :] = jnp.concatenate([pr, pi], 1)
        rhs_ref[low, :] = jnp.concatenate([-pi, pr], 1)
        old = jnp.concatenate([re_ref[kb], im_ref[kb]], 1)
        upd = jnp.dot(old, rhs_ref[...], precision=lax.Precision.HIGHEST, preferred_element_type=f32)
        rhs_ref[top, :] = jnp.zeros((PANEL, 4 * WIDE), f32)
        rhs_ref[low, :] = jnp.zeros((PANEL, 4 * WIDE), f32)
        wide_lane = lax.broadcasted_iota(i32, upd[:, :WIDE].shape, 1)
        gone = (wide_lane >= t * PANEL) & (wide_lane < (t + 1) * PANEL)
        re_ref[kb] = jnp.where(gone, 0.0, re_ref[kb]) + upd[:, :WIDE]
        im_ref[kb] = jnp.where(gone, 0.0, im_ref[kb]) + upd[:, 2 * WIDE : 3 * WIDE]
        re_ref[1 - kb] += upd[:, WIDE : 2 * WIDE]
        im_ref[1 - kb] += upd[:, 3 * WIDE :]
        for n, h in enumerate(order):
            re_ref[h, r, :] = pr[:, n * WIDE : (n + 1) * WIDE]
            im_ref[h, r, :] = pi[:, n * WIDE : (n + 1) * WIDE]


def pivot_exchange(kb, at, first, second):
    order = PANELS * WIDE
    part = jax.ShapeDtypeStruct((2, order, WIDE), f32)
    return pl.pallas_call(
        functools.partial(inverse_kernel, kb),
        out_shape=(part, part),
        in_specs=[SMEM, VMEM, VMEM],
        out_specs=(VMEM, VMEM),
        scratch_shapes=[pltpu.VMEM((2 * WIDE, 4 * WIDE), f32)],
        compiler_params=pltpu.CompilerParams(vmem_limit_bytes=12 * MB),
        cost_estimate=pl.CostEstimate(flops=int(6e9), transcendentals=0, bytes_accessed=1 << 20),
    )(at, first, second)


def split3(x):
    hi = x.astype(bf16)
    rest = x - hi.astype(f32)
    mid = rest.astype(bf16)
    low = (rest - mid.astype(f32)).astype(bf16)
    return hi, mid, low


def real_form(re, im):
    return jnp.concatenate([jnp.concatenate([re, im], 1), jnp.concatenate([-im, re], 1)], 0)


def column_kernel(re_ref, im_ref, c_ref, x_ref):
    left = jnp.concatenate([c_ref[0, 0], c_ref[1, 0], c_ref[0, 1], c_ref[1, 1]], 1)
    re = split3(jnp.concatenate([re_ref[0], re_ref[1]], 1))
    im = split3(jnp.concatenate([im_ref[0], im_ref[1]], 1))
    x = jnp.zeros(x_ref.shape, f32)
    for r, i in zip(re, im):
        x += jnp.dot(left, real_form(r, i), preferred_element_type=f32)
    x_ref[...] = x


def pivot_columns(re, im, column):
    rows = column.shape[2]
    return pl.pallas_call(
        column_kernel,
        out_shape=jax.ShapeDtypeStruct((rows, 2 * PANELS * WIDE), f32),
        in_specs=[VMEM] * 3,
        out_specs=VMEM,
        compiler_params=pltpu.CompilerParams(vmem_limit_bytes=12 * MB),
        cost_estimate=pl.CostEstimate(flops=int(2e9), transcendentals=0, bytes_accessed=1 << 20),
        name="pivot_columns",
    )(re, im, column)


def schur_kernel(blocks, at, x_ref, mine_ref, other_ref, r_ref, out_ref):
    core = at[2]
    b = []
    for p in range(PANELS):
        local = slot_with(at, at[3 + blocks + p], blocks) % 2 == core
        b.append([jnp.where(local, mine_ref[p, k].astype(f32), other_ref[p, k].astype(f32)).astype(bf16) for k in range(2)])
    br = jnp.concatenate([b[p][0] for p in range(PANELS)], 0)
    bi = jnp.concatenate([b[p][1] for p in range(PANELS)], 0)
    right = real_form(br, bi)
    x = x_ref[...]
    x_hi = x.astype(bf16)
    x_lo = (x - x_hi.astype(f32)).astype(bf16)
    prod = jnp.dot(x_hi, right, preferred_element_type=f32) + jnp.dot(x_lo, right, preferred_element_type=f32)
    cols = prod.shape[1] // 2
    out_ref[0] = r_ref[0] - prod[:, :cols]
    out_ref[1] = r_ref[1] - prod[:, cols:]


def schur_tile(at, blocks, x, mine, other, reduced):
    return pl.pallas_call(
        functools.partial(schur_kernel, blocks),
        out_shape=jax.ShapeDtypeStruct(reduced.shape, f32),
        in_specs=[SMEM] + [VMEM] * 4,
        out_specs=VMEM,
        compiler_params=pltpu.CompilerParams(vmem_limit_bytes=12 * MB),
        name="schur",
    )(at, x, mine, other, reduced)


def on_device(inverse, excite, coordinates, block_of_slot, panel_order):
    blk_size, grp_size = lax.axis_size("blk"), lax.axis_size("grp")
    blocks = block_of_slot.shape[0]
    slot, grp = lax.axis_index("blk").astype(i32), lax.axis_index("grp").astype(i32)
    core = slot % 2
    slabs = blocks // grp_size
    swap = [(i, i ^ 1) for i in range(blk_size)]
    same_core = [list(range(c, blk_size, 2)) for c in range(2)]
    at = jnp.concatenate([jnp.stack([slot, grp, core]), block_of_slot, panel_order])

    def spread(x, axis, groups=None):
        return lax.all_to_all(x, axis, split_axis=0, concat_axis=0, tiled=True, axis_index_groups=groups)

    pivots = panel_order[:PANELS]

    own, halves = basis_rows(inverse, excite, blk_size)
    sliced = spread(halves, "blk")

    bits = [1] + [1 << k for k in range(grp_size.bit_length() - 2, 0, -1)]
    pieces, held = [own], own
    for n, bit in enumerate(bits):
        pieces.append(lax.ppermute(held, "grp", [(g, g ^ bit) for g in range(grp_size)]))
        if n + 1 < len(bits):
            held = jnp.concatenate([held, pieces[-1]], 0)

    (green_first,) = green_tiles(at, coordinates, 0, 1, False)
    (green_pivot,) = green_tiles(at, coordinates, 2, PANELS, False)
    green_second, green_first, green_pivot = green_tiles(at, coordinates, 1, 1, True, [green_first, green_pivot])

    picked = gathered(at, sliced, grp_size, slabs)
    mine = spread(picked, "grp")
    other = lax.ppermute(mine, "blk", swap)

    (pivot_rows,) = couplings(at, blocks, [green_pivot], mine, other, [], [], [], True)
    pivot_other = lax.ppermute(pivot_rows, "blk", swap)
    reduced, copies, column = couplings(at, blocks, [green_first, green_second], mine, other, pieces, bits, [pivot_rows], False)

    rows = spread(copies, "blk", same_core)
    column_at = pivots // slabs
    for bit in bits:
        came = lax.ppermute(column, "grp", [(g, g ^ bit) for g in range(grp_size)])
        take = ((grp ^ column_at) & bit) != 0
        column = jnp.where(take[:, None, None, None], came, column)
    row_mine = pivot_tiles(at, rows, blocks)
    row_other = lax.ppermute(row_mine, "blk", swap)
    re, im = pivot_exchange(0, at, pivot_rows, pivot_other)
    re, im = pivot_exchange(1, at, re, im)
    x = pivot_columns(re, im, column)
    schur = schur_tile(at, blocks, x, row_mine, row_other, reduced)
    return (reduced, schur)


def solution(mesh):
    placed = (P(None, "blk", "grp", None), P(None, "blk", None, None), P(), P(), P())
    return jax.shard_map(
        on_device,
        mesh=mesh,
        in_specs=placed,
        out_specs=(P(None, "blk", "grp"), P(None, "blk", "grp")),
        check_vma=False,
    )
```

```python
import functools

import jax
import jax.numpy as jnp
import numpy as np
from jax import lax
from jax.experimental import pallas as pl
from jax.experimental.pallas import tpu as pltpu
from jax.sharding import PartitionSpec as P


PANELS = 2
bf16 = jnp.bfloat16
f32 = jnp.float32
i32 = jnp.int32

SELF_REAL = 6.0
SELF_IMAG = -1.5
TURNS = 1.3 / (2 * np.pi)
SHIFT = float(1.5 * 2**23)
SIN = (4.44288283, -7.30824115, 3.60628896, -0.8457636, 0.10920575)
COS = (-1.4142135, 6.97885099, -5.73946117, 1.88356298, -0.31069819)
VMEM = pl.BlockSpec(memory_space=pltpu.VMEM)
SMEM = pl.BlockSpec(memory_space=pltpu.SMEM)
MB = 1 << 20
COUPLE_ROWS = 1024
STRIPS = 8


def horner(coefs, g):
    r = coefs[-1]
    for k in coefs[-2::-1]:
        r = r * g + k
    return r


def half_green(sq):
    inv_r = lax.rsqrt(sq)
    turns = (sq * inv_r) * TURNS
    f = turns - ((turns + SHIFT) - SHIFT)
    g = f * f
    s = horner(SIN, g) * f
    c = horner(COS, g)
    scaled = s * inv_r
    return inv_r - s * scaled, c * scaled


def basis_kernel(inv_ref, exc_ref, own_ref, halves_ref):
    er, ei = exc_ref[0, 0], exc_ref[1, 0]
    j = jnp.dot(inv_ref[0, 0], jnp.concatenate([er, ei], 1), preferred_element_type=f32)
    j += jnp.dot(inv_ref[1, 0], jnp.concatenate([-ei, er], 1), preferred_element_type=f32)
    cols, half = j.shape[1] // 2, j.shape[0] // 2
    jb = j.astype(bf16)
    for part in range(2):
        own_ref[0, part] = jb[:, part * cols : (part + 1) * cols]
        for k in range(halves_ref.shape[0]):
            halves_ref[k, part] = jb[(k % 2) * half : (k % 2 + 1) * half, part * cols : (part + 1) * cols]


def basis_rows(inverse, excite, devices):
    rows, cols = inverse.shape[2], excite.shape[3]
    return pl.pallas_call(
        basis_kernel,
        out_shape=(
            jax.ShapeDtypeStruct((1, 2, rows, cols), bf16),
            jax.ShapeDtypeStruct((devices, 2, rows // 2, cols), bf16),
        ),
        grid=(1,),
        in_specs=[pl.BlockSpec(x.shape, lambda i: (0, 0, 0, 0)) for x in (inverse, excite)],
        out_specs=(VMEM, VMEM),
        compiler_params=pltpu.CompilerParams(vmem_limit_bytes=8 * MB),
        name="basis",
    )(*[pltpu.with_memory_space_constraint(x, pltpu.HBM) for x in (inverse, excite)])


def slot_with(at, block, blocks):
    slot = 0
    for s in range(blocks):
        slot = slot + jnp.where(at[3 + s] == block, s, 0)
    return slot


def gather_kernel(at_ref, rows_ref, out_ref, slot_ref):
    blocks = rows_ref.shape[0]
    for s in range(blocks):
        slot_ref[at_ref[3 + s]] = s
    groups, entries = out_ref.shape[:2]
    slabs = entries - PANELS
    for p in range(PANELS):
        value = rows_ref[slot_ref[at_ref[3 + blocks + p]]]
        for g in range(groups):
            out_ref[g, slabs + p] = value
    for g in range(groups):
        for e in range(slabs):
            out_ref[g, e] = rows_ref[slot_ref[g * slabs + e]]


def gathered(at, rows, groups, slabs):
    return pl.pallas_call(
        gather_kernel,
        out_shape=jax.ShapeDtypeStruct((groups, slabs + PANELS, *rows.shape[1:]), rows.dtype),
        in_specs=[SMEM, VMEM],
        out_specs=VMEM,
        scratch_shapes=[pltpu.SMEM((rows.shape[0],), i32)],
        compiler_params=pltpu.CompilerParams(vmem_limit_bytes=8 * MB),
        name="gathered",
    )(at, rows)


def pick_kernel(at_ref, row_ref, out_ref):
    out_ref[...] = row_ref[...]


def pivot_tiles(at, rows, blocks):
    shape = (1, *rows.shape[1:])
    return pl.pallas_call(
        pick_kernel,
        out_shape=jax.ShapeDtypeStruct((PANELS, *rows.shape[1:]), rows.dtype),
        grid_spec=pltpu.PrefetchScalarGridSpec(
            num_scalar_prefetch=1,
            grid=(PANELS,),
            in_specs=[pl.BlockSpec(shape, lambda p, at: (slot_with(at, at[3 + blocks + p], blocks) // 2, 0, 0, 0))],
            out_specs=pl.BlockSpec(shape, lambda p, at: (p, 0, 0, 0)),
        ),
        compiler_params=pltpu.CompilerParams(vmem_limit_bytes=8 * MB),
        name="pivot_tiles",
    )(at, rows)


def features(coords_ref, block, left):
    x, y, z = [coords_ref[d, pl.ds(block, 1), :] for d in range(3)]
    norm = x * x + y * y + z * z
    low = norm & 63
    high = norm - low
    one, zero = jnp.ones_like(norm), jnp.zeros_like(norm)
    rows = [-2 * x, -2 * y, -2 * z, high, low, one, one] if left else [x, y, z, one, one, high, low]
    return jnp.concatenate([v.astype(f32) for v in rows + [zero]], 0).astype(bf16)


def green_kernel(first, whole, carried, at_ref, coords_ref, *refs):
    sources, g_ref, targets = refs[:carried], refs[carried], refs[carried + 1 : 2 * carried + 1]
    fl_ref, fr_ref, sq_ref, *sems = refs[2 * carried + 1 :]
    copies = [pltpu.make_async_copy(a, b, sem) for a, b, sem in zip(sources, targets, sems)]
    for copy in copies:
        copy.start()
    rows, _ = sq_ref.shape
    local, chunk = pl.program_id(0), pl.program_id(1)
    tile = local + first
    blocks = coords_ref.shape[1]
    own, grp, core = at_ref[3 + at_ref[0]], at_ref[1], at_ref[2]
    main = tile < 2
    left = jnp.where(main, own, at_ref[3 + blocks + core])
    right = jnp.where(main, grp * 2 + tile, at_ref[3 + blocks + jnp.maximum(tile - 2, 0)])
    held, base = (local, chunk * rows) if whole else (0, 0)

    @pl.when(chunk == 0)
    def _():
        fl_ref[...] = features(coords_ref, left, True)
        fr_ref[...] = features(coords_ref, right, False)

    at = pl.ds(pl.multiple_of(chunk * rows, rows), rows)
    sq_ref[...] = lax.dot_general(
        fl_ref[:, at], fr_ref[...], (((0,), (0,)), ((), ())), preferred_element_type=f32
    )

    def strip(i, _):
        re, im = half_green(sq_ref[pl.ds(pl.multiple_of(i * 8, 8), 8), :])
        r = pl.ds(pl.multiple_of(base + i * 8, 8), 8)
        g_ref[held, 0, r, :] = re.astype(bf16)
        g_ref[held, 1, r, :] = im.astype(bf16)
        return 0

    lax.fori_loop(0, rows // 8, strip, 0, unroll=STRIPS)

    @pl.when(left == right)
    def _():
        size = 256
        same = lax.broadcasted_iota(i32, (size, size), 0) == lax.broadcasted_iota(i32, (size, size), 1)
        for k in range(rows // size):
            r = pl.ds(pl.multiple_of(base + k * size, size), size)
            c = pl.ds(pl.multiple_of(chunk * rows + k * size, size), size)
            for part, value in ((0, SELF_REAL), (1, SELF_IMAG)):
                block = g_ref[held, part, r, c].astype(f32)
                g_ref[held, part, r, c] = jnp.where(same, value, block).astype(bf16)

    for copy in copies:
        copy.wait()


def green_tiles(at, coordinates, first, count, whole, carry=()):
    unk = coordinates.shape[2]
    rows = unk if whole else unk // 2
    shape = (count, 2, unk, unk)
    return pl.pallas_call(
        functools.partial(green_kernel, first, whole, len(carry)),
        out_shape=[(pltpu.VMEM if whole else pltpu.HBM)(shape, bf16)] + [pltpu.VMEM(x.shape, x.dtype) for x in carry],
        grid=(count, unk // rows),
        in_specs=[SMEM, pl.BlockSpec(coordinates.shape, lambda t, m: (0, 0, 0))]
        + [pl.BlockSpec(memory_space=pltpu.HBM)] * len(carry),
        out_specs=[VMEM if whole else pl.BlockSpec((1, 2, rows, unk), lambda t, m: (t, 0, m, 0))] + [VMEM] * len(carry),
        scratch_shapes=[pltpu.VMEM((8, unk), bf16), pltpu.VMEM((8, unk), bf16), pltpu.VMEM((rows, unk), f32)]
        + [pltpu.SemaphoreType.DMA] * len(carry),
        compiler_params=pltpu.CompilerParams(vmem_limit_bytes=10 * MB),
        cost_estimate=pl.CostEstimate(
            flops=count * unk * unk * 30, transcendentals=count * unk * unk, bytes_accessed=count * unk * unk * 4
        ),
    )(at, *[pltpu.with_memory_space_constraint(x, pltpu.HBM) for x in (coordinates, *carry)])


def add_tile(y, left, acc):
    y_hi = y.astype(bf16)
    y_lo = (y - y_hi.astype(f32)).astype(bf16)
    acc[...] += jnp.dot(left, y_hi, preferred_element_type=f32) + jnp.dot(left, y_lo, preferred_element_type=f32)


def coupling_kernel(pivot, panel_at, greens, bits, at_ref, *refs):
    g_refs, refs = refs[:greens], refs[greens:]
    mine_ref, other_ref, refs = refs[0], refs[1], refs[2:]
    if pivot:
        out_ref, lhs, stage, top, bottom, acc = refs
    else:
        count = 1 + len(bits)
        pieces = refs[:count]
        out_ref, copies_ref, column_ref, lhs, stage, top, bottom, acc = refs[count + 1 :]
    tile, chunk = pl.program_id(0), pl.program_id(1)
    chunks = pl.num_programs(1)
    grp, core = at_ref[1], at_ref[2]
    groups, _, _, half, cols = mine_ref.shape
    rows = COUPLE_ROWS
    first = 2 if pivot else 0
    halves = ((mine_ref, core), (other_ref, 1 - core))

    def rows_of(g, part):
        return pl.ds(pl.multiple_of(g * 2 * half + part * half, half), half)

    @pl.when((tile == 0) & (chunk == 0))
    def _():
        if pivot:
            for g in range(groups):
                for src, part in halves:
                    r = rows_of(g, part)
                    stage[r, :cols] = src[g, first + core, 0]
                    stage[r, cols:] = src[g, first + core, 1]
        else:
            away = [0]
            for bit in bits:
                away = away + [d ^ bit for d in away]
            for piece in pieces:
                for k in range(piece.shape[0]):
                    r = pl.ds(pl.multiple_of((grp ^ away.pop(0)) * 2 * half, 2 * half), 2 * half)
                    stage[r, :cols] = piece[k, 0]
                    stage[r, cols:] = piece[k, 1]
        lhs[...] = stage[...].T

    @pl.when(chunk == 0)
    def _():
        acc[...] = jnp.zeros_like(acc)
        for g in range(groups):
            for src, part in halves:
                r = rows_of(g, part)
                jr, ji = src[g, first + tile, 0], src[g, first + tile, 1]
                top[r, :cols] = jr
                top[r, cols:] = ji
                bottom[r, :cols] = -ji
                bottom[r, cols:] = jr

    at_rows = pl.ds(pl.multiple_of(chunk * rows, rows), rows)

    def product(g_ref, held):
        y = jnp.dot(g_ref[held, 0, at_rows, :], top[...], preferred_element_type=f32)
        return y + jnp.dot(g_ref[held, 1, at_rows, :], bottom[...], preferred_element_type=f32)

    if greens == 1:
        add_tile(product(g_refs[0], tile), lhs[:, at_rows], acc)
    else:
        for n, g_ref in enumerate(g_refs):

            @pl.when(tile == n)
            def _():
                add_tile(product(g_ref, 0), lhs[:, at_rows], acc)

    @pl.when(chunk == chunks - 1)
    def _():
        both = (2.0 * (acc[:cols, :cols] + acc[cols:, cols:]), 2.0 * (acc[:cols, cols:] - acc[cols:, :cols]))
        for part, value in enumerate(both):
            out_ref[part] = value
            if not pivot:
                for k in range(copies_ref.shape[0]):
                    copies_ref[k, part] = value.astype(bf16)
                for p in range(PANELS):
                    here = at_ref[panel_at + p] == grp * 2 + tile

                    @pl.when(here | (tile == 0))
                    def _():
                        column_ref[p, part] = value.astype(bf16)


def couplings(at, blocks, greens, mine, other, pieces, bits, after, pivot):
    unk = greens[0].shape[2]
    cols = mine.shape[4]
    tiles = 2
    rows = COUPLE_ROWS
    copies = 8
    whole = lambda x: pl.BlockSpec(x.shape, lambda t, m: (0,) * x.ndim)
    out_shape = [jax.ShapeDtypeStruct((2, cols, tiles * cols), f32)]
    out_specs = [pl.BlockSpec((2, cols, cols), lambda t, m: (0, 0, t))]
    if not pivot:
        out_shape.append(jax.ShapeDtypeStruct((copies, 2, cols, tiles * cols), bf16))
        out_specs.append(pl.BlockSpec((copies, 2, cols, cols), lambda t, m: (0, 0, 0, t)))
        out_shape.append(jax.ShapeDtypeStruct((PANELS, 2, cols, cols), bf16))
        out_specs.append(pl.BlockSpec((PANELS, 2, cols, cols), lambda t, m: (0, 0, 0, 0)))
    return pl.pallas_call(
        functools.partial(coupling_kernel, pivot, 3 + blocks, len(greens), bits),
        out_shape=out_shape,
        grid=(tiles, unk // rows),
        in_specs=[SMEM] + [VMEM] * len(greens)
        + [whole(x) for x in (mine, other, *pieces)]
        + [pl.BlockSpec(memory_space=pl.ANY)] * len(after),
        out_specs=out_specs,
        scratch_shapes=[
            pltpu.VMEM((2 * cols, unk), bf16),
            pltpu.VMEM((unk, 2 * cols), bf16),
            pltpu.VMEM((unk, 2 * cols), bf16),
            pltpu.VMEM((unk, 2 * cols), bf16),
            pltpu.VMEM((2 * cols, 2 * cols), f32),
        ],
        compiler_params=pltpu.CompilerParams(vmem_limit_bytes=16 * MB),
        cost_estimate=pl.CostEstimate(
            flops=tiles * unk * unk * 2048, transcendentals=0, bytes_accessed=tiles * unk * unk * 4
        ),
    )(at, *greens, mine, other, *pieces, *after)


WIDE = 128
PANEL = 64


def small_exchange(ar, ai, sub):
    ar, ai = list(ar), list(ai)
    for s in range(8):
        row = lambda x: jnp.broadcast_to(x[s : s + 1], x.shape)
        pr, pi = row(ar[s]), row(ai[s])
        scale = 1.0 / (pr * pr + pi * pi)
        qr, qi = pr * scale, pi * scale
        br, bi = ar[s], ai[s]
        for m in range(8):
            if m == s:
                vr, vi = -qr, qi
                xr, xi = br * qr + bi * qi, bi * qr - br * qi
            else:
                cr, ci = row(ar[m]), row(ai[m])
                vr, vi = cr * qr + ci * qi, ci * qr - cr * qi
                xr, xi = ar[m] - (br * vr - bi * vi), ai[m] - (br * vi + bi * vr)
            ar[m], ai[m] = jnp.where(sub == s, -vr, xr), jnp.where(sub == s, -vi, xi)
    return ar, ai


def times(ar, ai, xr, xi, spread):
    nr = ni = None
    for m in range(8):
        cr, ci = spread(xr[m : m + 1]), spread(xi[m : m + 1])
        r, i = ar[m] * cr - ai[m] * ci, ar[m] * ci + ai[m] * cr
        nr, ni = (r, i) if nr is None else (nr + r, ni + i)
    return nr, ni


def inverse_kernel(kb, at_ref, first_ref, second_ref, re_ref, im_ref, rhs_ref):
    if kb == 0:
        core = at_ref[2]
        rows = first_ref.shape[1]
        for src, part in ((first_ref, core), (second_ref, 1 - core)):
            r = pl.ds(pl.multiple_of(part * rows, rows), rows)
            for h in range(2):
                re_ref[h, r, :] = src[0][:, h * WIDE : (h + 1) * WIDE]
                im_ref[h, r, :] = src[1][:, h * WIDE : (h + 1) * WIDE]
    else:
        re_ref[...] = first_ref[...]
        im_ref[...] = second_ref[...]
    rhs_ref[...] = jnp.zeros_like(rhs_ref)
    lane = lax.broadcasted_iota(i32, (8, WIDE), 1)
    sub = lax.broadcasted_iota(i32, (8, WIDE), 0)
    spread = lambda x: jnp.broadcast_to(x, (8, WIDE))
    groups = PANEL // 8

    order = (kb, 1 - kb)
    for t in range(WIDE // PANEL):
        r = slice(kb * WIDE + t * PANEL, kb * WIDE + (t + 1) * PANEL)
        block = [(re_ref[h, r, :], im_ref[h, r, :]) for h in order]
        tr = [[b[0][8 * g : 8 * g + 8] for g in range(groups)] for b in block]
        ti = [[b[1][8 * g : 8 * g + 8] for g in range(groups)] for b in block]
        for gs in range(groups):
            first = t * PANEL + 8 * gs
            ar = [[spread(x[:, first + m : first + m + 1]) for m in range(8)] for x in tr[0]]
            ai = [[spread(x[:, first + m : first + m + 1]) for m in range(8)] for x in ti[0]]
            dr, di = small_exchange(ar[gs], ai[gs], sub)
            within = (lane >= first) & (lane < first + 8)
            unit = jnp.where(lane == sub + first, -1.0, 0.0)
            xr = [jnp.where(within, unit, tr[0][gs]), tr[1][gs]]
            xi = [jnp.where(within, 0.0, ti[0][gs]), ti[1][gs]]
            for h in range(2):
                nr, ni = times(dr, di, xr[h], xi[h], spread)
                tr[h][gs], ti[h][gs] = -nr, -ni
            for g in range(groups):
                if g == gs:
                    continue
                for h in range(2):
                    nr, ni = times(ar[g], ai[g], tr[h][gs], ti[h][gs], spread)
                    yr, yi = tr[h][g], ti[h][g]
                    if h == 0:
                        yr, yi = jnp.where(within, 0.0, yr), jnp.where(within, 0.0, yi)
                    tr[h][g], ti[h][g] = yr + nr, yi + ni
        pr = jnp.concatenate([jnp.concatenate(tr[h], 0) for h in range(2)], 1)
        pi = jnp.concatenate([jnp.concatenate(ti[h], 0) for h in range(2)], 1)
        top, low = slice(t * PANEL, (t + 1) * PANEL), slice(WIDE + t * PANEL, WIDE + (t + 1) * PANEL)
        rhs_ref[top, :] = jnp.concatenate([pr, pi], 1)
        rhs_ref[low, :] = jnp.concatenate([-pi, pr], 1)
        old = jnp.concatenate([re_ref[kb], im_ref[kb]], 1)
        upd = jnp.dot(old, rhs_ref[...], precision=lax.Precision.HIGHEST, preferred_element_type=f32)
        rhs_ref[top, :] = jnp.zeros((PANEL, 4 * WIDE), f32)
        rhs_ref[low, :] = jnp.zeros((PANEL, 4 * WIDE), f32)
        wide_lane = lax.broadcasted_iota(i32, upd[:, :WIDE].shape, 1)
        gone = (wide_lane >= t * PANEL) & (wide_lane < (t + 1) * PANEL)
        re_ref[kb] = jnp.where(gone, 0.0, re_ref[kb]) + upd[:, :WIDE]
        im_ref[kb] = jnp.where(gone, 0.0, im_ref[kb]) + upd[:, 2 * WIDE : 3 * WIDE]
        re_ref[1 - kb] += upd[:, WIDE : 2 * WIDE]
        im_ref[1 - kb] += upd[:, 3 * WIDE :]
        for n, h in enumerate(order):
            re_ref[h, r, :] = pr[:, n * WIDE : (n + 1) * WIDE]
            im_ref[h, r, :] = pi[:, n * WIDE : (n + 1) * WIDE]


def pivot_exchange(kb, at, first, second):
    order = PANELS * WIDE
    part = jax.ShapeDtypeStruct((2, order, WIDE), f32)
    return pl.pallas_call(
        functools.partial(inverse_kernel, kb),
        out_shape=(part, part),
        in_specs=[SMEM, VMEM, VMEM],
        out_specs=(VMEM, VMEM),
        scratch_shapes=[pltpu.VMEM((2 * WIDE, 4 * WIDE), f32)],
        compiler_params=pltpu.CompilerParams(vmem_limit_bytes=12 * MB),
        cost_estimate=pl.CostEstimate(flops=int(6e9), transcendentals=0, bytes_accessed=1 << 20),
    )(at, first, second)


def split3(x):
    hi = x.astype(bf16)
    rest = x - hi.astype(f32)
    mid = rest.astype(bf16)
    low = (rest - mid.astype(f32)).astype(bf16)
    return hi, mid, low


def real_form(re, im):
    return jnp.concatenate([jnp.concatenate([re, im], 1), jnp.concatenate([-im, re], 1)], 0)


def column_kernel(re_ref, im_ref, c_ref, x_ref):
    left = jnp.concatenate([c_ref[0, 0], c_ref[1, 0], c_ref[0, 1], c_ref[1, 1]], 1)
    re = split3(jnp.concatenate([re_ref[0], re_ref[1]], 1))
    im = split3(jnp.concatenate([im_ref[0], im_ref[1]], 1))
    x = jnp.zeros(x_ref.shape, f32)
    for r, i in zip(re, im):
        x += jnp.dot(left, real_form(r, i), preferred_element_type=f32)
    x_ref[...] = x


def pivot_columns(re, im, column):
    rows = column.shape[2]
    return pl.pallas_call(
        column_kernel,
        out_shape=jax.ShapeDtypeStruct((rows, 2 * PANELS * WIDE), f32),
        in_specs=[VMEM] * 3,
        out_specs=VMEM,
        compiler_params=pltpu.CompilerParams(vmem_limit_bytes=12 * MB),
        cost_estimate=pl.CostEstimate(flops=int(2e9), transcendentals=0, bytes_accessed=1 << 20),
        name="pivot_columns",
    )(re, im, column)


def schur_kernel(blocks, at, x_ref, mine_ref, other_ref, r_ref, out_ref):
    core = at[2]
    b = []
    for p in range(PANELS):
        local = slot_with(at, at[3 + blocks + p], blocks) % 2 == core
        b.append([jnp.where(local, mine_ref[p, k].astype(f32), other_ref[p, k].astype(f32)).astype(bf16) for k in range(2)])
    br = jnp.concatenate([b[p][0] for p in range(PANELS)], 0)
    bi = jnp.concatenate([b[p][1] for p in range(PANELS)], 0)
    right = real_form(br, bi)
    x = x_ref[...]
    x_hi = x.astype(bf16)
    x_lo = (x - x_hi.astype(f32)).astype(bf16)
    prod = jnp.dot(x_hi, right, preferred_element_type=f32) + jnp.dot(x_lo, right, preferred_element_type=f32)
    cols = prod.shape[1] // 2
    out_ref[0] = r_ref[0] - prod[:, :cols]
    out_ref[1] = r_ref[1] - prod[:, cols:]


def schur_tile(at, blocks, x, mine, other, reduced):
    return pl.pallas_call(
        functools.partial(schur_kernel, blocks),
        out_shape=jax.ShapeDtypeStruct(reduced.shape, f32),
        in_specs=[SMEM] + [VMEM] * 4,
        out_specs=VMEM,
        compiler_params=pltpu.CompilerParams(vmem_limit_bytes=12 * MB),
        name="schur",
    )(at, x, mine, other, reduced)


def on_device(inverse, excite, coordinates, block_of_slot, panel_order):
    blk_size, grp_size = lax.axis_size("blk"), lax.axis_size("grp")
    blocks = block_of_slot.shape[0]
    slot, grp = lax.axis_index("blk").astype(i32), lax.axis_index("grp").astype(i32)
    core = slot % 2
    slabs = blocks // grp_size
    swap = [(i, i ^ 1) for i in range(blk_size)]
    same_core = [list(range(c, blk_size, 2)) for c in range(2)]
    at = jnp.concatenate([jnp.stack([slot, grp, core]), block_of_slot, panel_order])

    def spread(x, axis, groups=None):
        return lax.all_to_all(x, axis, split_axis=0, concat_axis=0, tiled=True, axis_index_groups=groups)

    pivots = panel_order[:PANELS]

    own, halves = basis_rows(inverse, excite, blk_size)
    sliced = spread(halves, "blk")

    bits = [1] + [1 << k for k in range(grp_size.bit_length() - 2, 0, -1)]
    pieces, held = [own], own
    for n, bit in enumerate(bits):
        pieces.append(lax.ppermute(held, "grp", [(g, g ^ bit) for g in range(grp_size)]))
        if n + 1 < len(bits):
            held = jnp.concatenate([held, pieces[-1]], 0)

    (green_first,) = green_tiles(at, coordinates, 0, 1, False)
    (green_pivot,) = green_tiles(at, coordinates, 2, PANELS, False)
    green_second, green_first, green_pivot = green_tiles(at, coordinates, 1, 1, True, [green_first, green_pivot])

    picked = gathered(at, sliced, grp_size, slabs)
    mine = spread(picked, "grp")
    other = lax.ppermute(mine, "blk", swap)

    (pivot_rows,) = couplings(at, blocks, [green_pivot], mine, other, [], [], [], True)
    pivot_other = lax.ppermute(pivot_rows, "blk", swap)
    reduced, copies, column = couplings(at, blocks, [green_first, green_second], mine, other, pieces, bits, [pivot_rows], False)

    rows = spread(copies, "blk", same_core)
    column_at = pivots // slabs
    for bit in bits:
        came = lax.ppermute(column, "grp", [(g, g ^ bit) for g in range(grp_size)])
        take = ((grp ^ column_at) & bit) != 0
        column = jnp.where(take[:, None, None, None], came, column)
    row_mine = pivot_tiles(at, rows, blocks)
    row_other = lax.ppermute(row_mine, "blk", swap)
    re, im = pivot_exchange(0, at, pivot_rows, pivot_other)
    re, im = pivot_exchange(1, at, re, im)
    x = pivot_columns(re, im, column)
    schur = schur_tile(at, blocks, x, row_mine, row_other, reduced)
    return (reduced, schur)


def solution(mesh):
    placed = (P(None, "blk", "grp", None), P(None, "blk", None, None), P(), P(), P())
    return jax.shard_map(
        on_device,
        mesh=mesh,
        in_specs=placed,
        out_specs=(P(None, "blk", "grp"), P(None, "blk", "grp")),
        check_vma=False,
    )
```
